32 devices in a mesh: tm: 2 (over x), sx: 4 (over z), sy: 4 (over y, core).
Axes of the slice: x: 2, y: 2, z: 4, core: 2. Of those that a mesh axis runs over, the one named last changes fastest.
Arguments:
- heat_source: float32 [8, 64, 64, 128], P('tm', 'sx', 'sy'), may hold values from -8 to 8
- conductivity: float32 [64, 64, 128], P('sx', 'sy'), may hold values from 0.001 to 0.5
- initial_iterate: float32 [8, 64, 64, 128], P('tm', 'sx', 'sy'), may hold values from -6 to 6
Outputs:
- solution: float32 [8, 64, 64, 128], P('tm', 'sx', 'sy')
- residual: float32 [8, 64, 64, 128], P('tm', 'sx', 'sy')
The draws below stay inside these ranges and needn't reach their ends.
All inputs are finite; a program needn't handle non-finite values.
Results may differ from the reference program's by a relative error of at most 0.000074.
Values sent between devices are 32-bit elements; how exact they have to be, the bound alone decides.
A program may use at most 64 MiB of HBM per device.

```python
import jax
import jax.numpy as jnp
from jax import lax

STEPS = 4
NT = 8
NX = 64
NY = 64
NZ = 128


def draw_heat_source(key, part):
    rough = jax.random.normal(key, (NT, NX, NY, NZ), jnp.float32)
    return jnp.clip(rough, -8.0, 8.0)


def draw_conductivity(key, part):
    region_key = jax.random.fold_in(key, 13)
    high_key = jax.random.fold_in(key, 11)
    low_key = jax.random.fold_in(key, 12)
    regions_x = (NX + 2) // 4 + 1
    regions_y = (NY + 2) // 4 + 1
    flags = jax.random.randint(region_key, (regions_x, regions_y), 0, 2)
    index_x = ((jnp.arange(NX) + 2) // 4).astype(jnp.int32)
    index_y = ((jnp.arange(NY) + 2) // 4).astype(jnp.int32)
    low_cells = jnp.take(jnp.take(flags, index_x, axis=0), index_y, axis=1)
    high = jnp.exp(jax.random.uniform(high_key, (NX, NY, NZ), jnp.float32, jnp.log(0.02), jnp.log(0.5)))
    low = jnp.exp(jax.random.uniform(low_key, (NX, NY, NZ), jnp.float32, jnp.log(0.001), jnp.log(0.004)))
    return jnp.clip(jnp.where(low_cells[:, :, None] == 1, low, high), 0.001, 0.5)


def block_levels(key, dims, cuts, low, top_value):
    loudness, own = 1.0, jax.random.fold_in(key, 6)
    for axis_at, blocks in cuts:
        draws = jnp.exp(jax.random.uniform(jax.random.fold_in(own, axis_at), (blocks,), jnp.float32, low / len(cuts), top_value / len(cuts)))
        loudness = loudness * jnp.repeat(draws, dims[axis_at] // blocks).reshape([-1 if axis == axis_at else 1 for axis in range(len(dims))])
    return loudness


def gaussian(rng, extent, width, reach, cuts=(), dtype=jnp.bfloat16):
    values = jax.random.normal(rng, extent, jnp.float32) * width
    if len(cuts) > 0:
        values = block_levels(rng, extent, cuts, -0.22, 0.18) * values
    return jnp.clip(values, min=-reach, max=reach).astype(dtype)


def setup_inputs(seed: int = 0) -> dict:
    key_list = jax.random.split(jax.random.key(seed), 4)
    return {
        "heat_source": draw_heat_source(jax.random.fold_in(key_list[3], 71), 0),
        "conductivity": draw_conductivity(jax.random.fold_in(key_list[3], 71), 0),
        "initial_iterate": gaussian(key_list[2], (NT, NX, NY, NZ), 1.0, 6.0, ((0, 2), (1, 4), (2, 4)), jnp.float32),
    }


relax_weight = 0.8
fine_step = 1.0


def face_terms(conductivity):
    padded = jnp.pad(conductivity, 1)
    center = conductivity
    couple = (0.5 * (center + padded[2:, 1:-1, 1:-1]), 0.5 * (center + padded[:-2, 1:-1, 1:-1]),
              0.5 * (center + padded[1:-1, 2:, 1:-1]), 0.5 * (center + padded[1:-1, :-2, 1:-1]),
              0.5 * (center + padded[1:-1, 1:-1, 2:]), 0.5 * (center + padded[1:-1, 1:-1, :-2]))
    coupling = couple[0] + couple[1] + couple[2] + couple[3] + couple[4] + couple[5]
    return couple, coupling


def combine_neighbours(values, padded, couple, coupling, tau_step):
    beside = couple[0] * padded[:, 2:, 1:-1, 1:-1] + couple[1] * padded[:, :-2, 1:-1, 1:-1]
    beside = beside + couple[2] * padded[:, 1:-1, 2:, 1:-1] + couple[3] * padded[:, 1:-1, :-2, 1:-1]
    beside = beside + couple[4] * padded[:, 1:-1, 1:-1, 2:] + couple[5] * padded[:, 1:-1, 1:-1, :-2]
    return (1.0 + tau_step * coupling) * values - tau_step * beside


def apply_operator(values, couple, coupling, tau_step):
    padded = jnp.pad(values, ((0, 0), (1, 1), (1, 1), (1, 1)))
    return combine_neighbours(values, padded, couple, coupling, tau_step)


def smooth(values, source, couple, coupling, tau_step, block_len):
    diagonal = 1.0 + tau_step * coupling
    factor = relax_weight / diagonal
    applied = apply_operator(values, couple, coupling, tau_step)
    update = values + relax_weight * (source - applied) / diagonal
    earlier = jnp.concatenate([jnp.zeros_like(values[:1]), values[:-1]], axis=0)
    groups = values.shape[0] // block_len
    shaped = update.reshape((groups, block_len) + values.shape[1:])
    running = earlier.reshape((groups, block_len) + values.shape[1:])[:, 0]
    results = []
    for position in range(block_len):
        running = shaped[:, position] + factor * running
        results.append(running)
    return jnp.stack(results, axis=1).reshape(values.shape)


def defect(values, source, couple, coupling, tau_step):
    earlier = jnp.concatenate([jnp.zeros_like(values[:1]), values[:-1]], axis=0)
    return source + earlier - apply_operator(values, couple, coupling, tau_step)


def coarse_sweep(values, source, couple, coupling, tau_step):
    diagonal = 1.0 + tau_step * coupling
    factor = relax_weight / diagonal
    applied = apply_operator(values, couple, coupling, tau_step)
    update = values + relax_weight * (source - applied) / diagonal

    def advance(running, term):
        fresh_value = term + factor * running
        return fresh_value, fresh_value

    _, result = lax.scan(advance, jnp.zeros_like(values[0]), update)
    return result


def reference(heat_source, conductivity, initial_iterate):
    couple, coupling = face_terms(conductivity)
    first = smooth(initial_iterate, heat_source, couple, coupling, fine_step, STEPS)
    defect_fine = defect(first, heat_source, couple, coupling, fine_step)
    source_one = defect_fine[0::2] + defect_fine[1::2]
    error_one = smooth(jnp.zeros_like(source_one), source_one, couple, coupling, 2.0 * fine_step, STEPS // 2)
    defect_one = defect(error_one, source_one, couple, coupling, 2.0 * fine_step)
    source_two = defect_one[0::2] + defect_one[1::2]
    error_two = smooth(jnp.zeros_like(source_two), source_two, couple, coupling, 4.0 * fine_step, 1)
    defect_two = defect(error_two, source_two, couple, coupling, 4.0 * fine_step)
    source_three = defect_two[0::2] + defect_two[1::2]
    error_three = coarse_sweep(jnp.zeros_like(source_three), source_three, couple, coupling, 8.0 * fine_step)
    error_three = coarse_sweep(error_three, source_three, couple, coupling, 8.0 * fine_step)
    error_two = smooth(error_two + jnp.repeat(error_three, 2, axis=0), source_two, couple, coupling, 4.0 * fine_step, 1)
    error_one = smooth(error_one + jnp.repeat(error_two, 2, axis=0), source_one, couple, coupling, 2.0 * fine_step, STEPS // 2)
    solution = smooth(first + jnp.repeat(error_one, 2, axis=0), heat_source, couple, coupling, fine_step, STEPS)
    return solution, defect(solution, heat_source, couple, coupling, fine_step)
```

```python
import functools

import jax
import jax.numpy as jnp
from jax import lax
from jax.experimental import pallas as pl
from jax.experimental.pallas import tpu as pltpu
from jax.sharding import PartitionSpec as P

relax_weight = 0.8
keep_weight = 1.0 - relax_weight
MESH = pl.DeviceIdType.MESH

KAPPA, INIT, FIRST, ERR1, ERR2, ERR3, FIX2, FIX1, SUM0, SOL, PART, PAIR, PART2, PAIR2 = range(14)
FIELDS = 14
P_INIT, P_FIRST, P_ERR1, P_ERR2, P_FIX1, P_SUM0, P_SOL = range(7)
XLO, XHI, YLO, YHI = range(4)


def kernel(n_tm, n_sx, n_sy, hs_hbm, k_hbm, in_hbm, sol_hbm, res_hbm, *scratch):
    fields = scratch[:FIELDS]
    yrecv = scratch[FIELDS:2 * FIELDS]
    ysend = scratch[2 * FIELDS:3 * FIELDS]
    (hs, res, before, second, rhs1, rhs2, rhs3, mine, theirs, chain,
     face, coupling, factor, send_sem, recv_sem, tsend, trecv,
     qsend, qrecv, csend, crecv, local) = scratch[3 * FIELDS:]
    steps, nx, ny, nz = hs.shape
    tm, sx, sy = lax.axis_index("tm"), lax.axis_index("sx"), lax.axis_index("sy")
    has = (sx > 0, sx < n_sx - 1, sy > 0, sy < n_sy - 1)
    partner = tm + 1 - 2 * lax.rem(tm, 2)
    even = lax.rem(tm, 2) == 0

    loads = [
        pltpu.make_async_copy(k_hbm, fields[KAPPA].at[0, pl.ds(1, nx)], local.at[0]),
        pltpu.make_async_copy(in_hbm, fields[INIT].at[:, pl.ds(1, nx)], local.at[1]),
        pltpu.make_async_copy(hs_hbm, hs, local.at[2]),
    ]
    for load in loads:
        load.start()

    barrier = pltpu.get_barrier_semaphore()
    greet = [
        (has[XLO], {"sx": sx - 1}), (has[XHI], {"sx": sx + 1}),
        (has[YLO], {"sy": sy - 1}), (has[YHI], {"sy": sy + 1}),
        (tm > 0, {"tm": tm - 1}), (tm < n_tm - 1, {"tm": tm + 1}),
    ]
    if n_tm == 2:
        greet += [
            (has[XLO], {"tm": partner, "sx": sx - 1}), (has[XHI], {"tm": partner, "sx": sx + 1}),
            (has[YLO], {"tm": partner, "sy": sy - 1}), (has[YHI], {"tm": partner, "sy": sy + 1}),
        ]
    if n_tm > 2:
        greet += [(tm > 1, {"tm": tm - 2}), (tm < n_tm - 2, {"tm": tm + 2})]
    count = jnp.int32(0)
    for there, device in greet:
        count = count + jnp.where(there, 1, 0)

        @pl.when(there)
        def _(device=device):
            pl.semaphore_signal(barrier, inc=1, device_id=device, device_id_type=MESH)

    pl.semaphore_wait(barrier, count)

    def face_copy(i, side, pair=False):
        field = fields[i]
        to = i + 1 if pair else i
        land = fields[to]
        if side == XLO:
            if i == INIT:
                src = in_hbm.at[:, pl.ds(0, 1)]
            elif i == KAPPA:
                src = k_hbm.at[pl.ds(0, 1)]
            else:
                src = field.at[:, pl.ds(1, 1)]
            dst, device = land.at[:, pl.ds(nx + 1, 1)], {"sx": sx - 1}
        elif side == XHI:
            if i == INIT:
                src = in_hbm.at[:, pl.ds(nx - 1, 1)]
            elif i == KAPPA:
                src = k_hbm.at[pl.ds(nx - 1, 1)]
            else:
                src = field.at[:, pl.ds(nx, 1)]
            dst, device = land.at[:, pl.ds(0, 1)], {"sx": sx + 1}
        elif side == YLO:
            src, dst, device = ysend[i].at[0], yrecv[to].at[1], {"sy": sy - 1}
        else:
            src, dst, device = ysend[i].at[1], yrecv[to].at[0], {"sy": sy + 1}
        if i == KAPPA and side in (XLO, XHI):
            dst = field.at[0, pl.ds(nx + 1 if side == XLO else 0, 1)]
        if pair:
            device["tm"] = partner
        return pltpu.make_async_remote_copy(
            src_ref=src, dst_ref=dst, send_sem=send_sem.at[to, side],
            recv_sem=recv_sem.at[to, side], device_id=device, device_id_type=MESH)

    def send_faces(i, sides, pair=False):
        for side in sides:
            @pl.when(has[side])
            def _(side=side):
                face_copy(i, side).start()
                if pair:
                    face_copy(i, side, True).start()

    def wait_faces(i, pair=False):
        for side in (YLO, YHI, XLO, XHI):
            @pl.when(has[side ^ 1])
            def _(side=side):
                face_copy(i, side, pair).wait_recv()

    half = nx // 2
    halves = (pl.ds(0, half), pl.ds(half, nx - half))

    def last_copy(i, part):
        field = fields[lasts[i]]
        if i == P_INIT:
            src = in_hbm.at[steps - 1, halves[part]]
        else:
            src = field.at[field.shape[0] - 1, (pl.ds(1, half), pl.ds(1 + half, nx - half))[part]]
        return pltpu.make_async_remote_copy(
            src_ref=src, dst_ref=before.at[i, halves[part]],
            send_sem=tsend.at[i, part], recv_sem=trecv.at[i, part],
            device_id={"tm": tm + 1}, device_id_type=MESH)

    lasts = (INIT, FIRST, ERR1, ERR2, FIX1, SUM0, SOL)

    def send_last(i, part):
        @pl.when(tm < n_tm - 1)
        def _():
            last_copy(i, part).start()

    def wait_last(i, parts=(0, 1)):
        @pl.when(tm > 0)
        def _():
            for part in parts:
                last_copy(i, part).wait_recv()

    send_faces(KAPPA, (XLO, XHI))
    send_faces(INIT, (XLO, XHI))
    send_last(P_INIT, 0)
    send_last(P_INIT, 1)

    def over_rows(body, by=8, start=0, stop=nx):
        def step(x, carry):
            body(x)
            return carry

        lax.fori_loop(start, stop, step, 0, unroll=by)

    def phase(body, i, send_part=None, pair=False, awaited=None):
        if awaited is not None:
            wait_last(awaited, (0,))
        body(0)
        if awaited is None:
            body(nx - 1)
            send_faces(i, (XLO, XHI), pair)
        else:
            send_faces(i, (XLO,), pair)
        over_rows(body, half - 1, 1, half)
        if send_part is not None:
            send_part(0)
        if awaited is not None:
            wait_last(awaited, (1,))
            body(nx - 1)
            send_faces(i, (XHI,), pair)
        over_rows(body, half - 1, half, nx - 1)
        send_faces(i, (YLO, YHI), pair)
        if send_part is not None:
            send_part(1)

    def put_faces(i, t, x, value):
        ysend[i][0, t, pl.ds(x, 1), :] = value[0:1, :]
        ysend[i][1, t, pl.ds(x, 1), :] = value[ny - 1:ny, :]

    def put(i, t, x, value):
        fields[i][t, x + 1] = value
        put_faces(i, t, x, value)

    loads[0].wait()
    loads[1].wait()

    def pack(x):
        put_faces(KAPPA, 0, x, fields[KAPPA][0, x + 1])
        for t in range(steps):
            put_faces(INIT, t, x, fields[INIT][t, x + 1])

    over_rows(pack)
    send_faces(KAPPA, (YLO, YHI))
    send_faces(INIT, (YLO, YHI))

    @pl.when(sx == 0)
    def _():
        for i in range(FIELDS):
            for t in range(fields[i].shape[0]):
                fields[i][t, 0] = jnp.zeros((ny, nz), jnp.float32)

    @pl.when(sx == n_sx - 1)
    def _():
        for i in range(FIELDS):
            for t in range(fields[i].shape[0]):
                fields[i][t, nx + 1] = jnp.zeros((ny, nz), jnp.float32)

    @pl.when(sy == 0)
    def _():
        for i in range(FIELDS):
            yrecv[i][0] = jnp.zeros(yrecv[i].shape[1:], jnp.float32)

    @pl.when(sy == n_sy - 1)
    def _():
        for i in range(FIELDS):
            yrecv[i][1] = jnp.zeros(yrecv[i].shape[1:], jnp.float32)

    @pl.when(tm == 0)
    def _():
        def clear(x):
            for i in range(7):
                before[i, x] = jnp.zeros((ny, nz), jnp.float32)

        over_rows(clear, 1)

    row = lax.broadcasted_iota(jnp.int32, (ny, nz), 0)
    column = lax.broadcasted_iota(jnp.int32, (ny, nz), 1)

    def around(i, t, x):
        field = fields[i]
        here = field[t, x + 1]
        return here, (
            field[t, x + 2],
            field[t, x],
            jnp.where(row == ny - 1, yrecv[i][1, t, pl.ds(x, 1), :], pltpu.roll(here, ny - 1, 0)),
            jnp.where(row == 0, yrecv[i][0, t, pl.ds(x, 1), :], pltpu.roll(here, 1, 0)),
            pltpu.roll(here, nz - 1, 1),
            pltpu.roll(here, 1, 1),
        )

    def beside(i, t, x, g):
        here, sides = around(i, t, x)
        terms = [g[j] * sides[j] for j in range(6)]
        return here, (terms[0] + terms[1]) + (terms[2] + terms[3]) + (terms[4] + terms[5])

    def faces_at(x):
        return [face[j, x] for j in range(6)]

    wait_faces(KAPPA)

    def coefficients(x):
        here, sides = around(KAPPA, 0, x)
        sides = list(sides)
        sides[4] = jnp.where(column == nz - 1, 0.0, sides[4])
        sides[5] = jnp.where(column == 0, 0.0, sides[5])
        g = [0.5 * (here + side) for side in sides]
        total = (g[0] + g[1]) + (g[2] + g[3]) + (g[4] + g[5])
        coupling[x] = total
        g[4] = jnp.where(column == nz - 1, 0.0, g[4])
        g[5] = jnp.where(column == 0, 0.0, g[5])
        for j in range(6):
            face[j, x] = g[j]
        for level in range(4):
            factor[level, x] = relax_weight / (1.0 + (2.0 ** level) * total)

    over_rows(coefficients)
    loads[2].wait()
    wait_faces(INIT)

    def sweep_first(x):
        g, f = faces_at(x), factor[0, x]
        running = before[P_INIT, x]
        for t in range(steps):
            here, near = beside(INIT, t, x, g)
            running = keep_weight * here + f * (hs[t, x] + near + running)
            put(FIRST, t, x, running)

    phase(sweep_first, FIRST, functools.partial(send_last, P_FIRST), awaited=P_INIT)
    wait_faces(FIRST)

    def down_one(x):
        g, diagonal, f = faces_at(x), 1.0 + coupling[x], factor[1, x]
        earlier = before[P_FIRST, x]
        running = None
        for m in range(steps // 2):
            total = None
            for t in (2 * m, 2 * m + 1):
                here, near = beside(FIRST, t, x, g)
                value = hs[t, x] + earlier - (diagonal * here - near)
                total = value if total is None else total + value
                earlier = here
            rhs1[m, x] = total
            running = f * total if running is None else f * (total + running)
            put(ERR1, m, x, running)

    phase(down_one, ERR1, functools.partial(send_last, P_ERR1), awaited=P_FIRST)
    wait_faces(ERR1)
    wait_last(P_ERR1)

    def down_two(x):
        g, diagonal, f = faces_at(x), 1.0 + 2.0 * coupling[x], factor[2, x]
        earlier = before[P_ERR1, x]
        total = None
        for t in range(2):
            here, near = beside(ERR1, t, x, g)
            value = rhs1[t, x] + earlier - (diagonal * here - 2.0 * near)
            total = value if total is None else total + value
            earlier = here
        rhs2[x] = total
        put(ERR2, 0, x, f * total)

    phase(down_two, ERR2, functools.partial(send_last, P_ERR2))
    wait_faces(ERR2)
    if n_tm > 2:
        wait_last(P_ERR2)

    def down_three(x):
        g, diagonal = faces_at(x), 1.0 + 4.0 * coupling[x]
        here, near = beside(ERR2, 0, x, g)
        earlier = here + before[P_ERR2, x] if n_tm > 2 else here
        value = rhs2[x] + jnp.where(even, earlier, 0.0) - (diagonal * here - 4.0 * near)
        mine[x] = value
        if n_tm == 2:
            put(PART, 0, x, factor[3, x] * value)

    def swap(part):
        return pltpu.make_async_remote_copy(
            src_ref=mine.at[halves[part]], dst_ref=theirs.at[halves[part]],
            send_sem=qsend.at[part], recv_sem=qrecv.at[part],
            device_id={"tm": partner}, device_id_type=MESH)

    if n_tm == 2:
        phase(down_three, PART, lambda part: swap(part).start(), True)
        wait_faces(PART)

        def part_two(x):
            here, near = beside(PART, 0, x, faces_at(x))
            put(PART2, 0, x, keep_weight * here + factor[3, x] * (mine[x] + 8.0 * near))

        phase(part_two, PART2, None, True)
    else:
        over_rows(down_three)
        swap(0).start()
        swap(1).start()
    swap(0).wait_recv()
    swap(1).wait_recv()

    def chain_copy(i, field):
        src = field.at[0, pl.ds(1, nx)] if i == 0 else second
        return pltpu.make_async_remote_copy(
            src_ref=src, dst_ref=chain.at[i], send_sem=csend.at[i],
            recv_sem=crecv.at[i], device_id={"tm": tm + 2}, device_id_type=MESH)

    def chain_wait(i):
        if n_tm > 2:
            @pl.when(tm > 1)
            def _():
                chain_copy(i, fields[ERR3]).wait_recv()

            @pl.when(tm < 2)
            def _():
                def clear(x):
                    chain[i, x] = jnp.zeros((ny, nz), jnp.float32)

                over_rows(clear, 1)

    def chain_send(i):
        if n_tm > 2:
            @pl.when(tm < n_tm - 2)
            def _():
                chain_copy(i, fields[ERR3]).start()

    chain_wait(0)

    def coarse_one(x):
        total = mine[x] + theirs[x]
        rhs3[x] = total
        if n_tm > 2:
            total = total + chain[0, x]
        value = factor[3, x] * total
        if n_tm > 2:
            put(ERR3, 0, x, value)
        else:
            fields[ERR3][0, x + 1] = value

    if n_tm > 2:
        phase(coarse_one, ERR3)
        chain_send(0)
        wait_faces(ERR3)
    else:
        over_rows(coarse_one)
        wait_faces(PART, True)
        for edge in (0, nx + 1):
            fields[ERR3][0, edge] = fields[PART][0, edge] + fields[PAIR][0, edge]
        for edge in range(2):
            yrecv[ERR3][edge, 0] = yrecv[PART][edge, 0] + yrecv[PAIR][edge, 0]
    if n_tm == 2:
        wait_last(P_ERR2)
    chain_wait(1)

    def coarse_two(x):
        here, near = beside(ERR3, 0, x, faces_at(x))
        total = rhs3[x] + 8.0 * near
        if n_tm > 2:
            total = total + chain[1, x]
        value = keep_weight * here + factor[3, x] * total
        if n_tm > 2:
            second[x] = value
            earlier = jnp.where(even, chain[1, x], value)
        else:
            earlier = jnp.where(even, 0.0, value)
        mine_next[x] = before[P_ERR2, x] + earlier
        value = fields[ERR2][0, x + 1] + value
        if n_tm > 2:
            put(FIX2, 0, x, value)
        else:
            fields[FIX2][0, x + 1] = value

    mine_next = res.at[0]
    if n_tm > 2:
        phase(coarse_two, FIX2)
        chain_send(1)
        wait_faces(FIX2)
    else:
        over_rows(coarse_two)
        wait_faces(PART2)
        wait_faces(PART2, True)
        for edge in (0, nx + 1):
            fields[FIX2][0, edge] = fields[ERR2][0, edge] + (
                fields[PART2][0, edge] + fields[PAIR2][0, edge])
        for edge in range(2):
            yrecv[FIX2][edge, 0] = yrecv[ERR2][edge, 0] + (
                yrecv[PART2][edge, 0] + yrecv[PAIR2][edge, 0])

    def up_two(x):
        here, near = beside(FIX2, 0, x, faces_at(x))
        value = keep_weight * here + factor[2, x] * (rhs2[x] + 4.0 * near + mine_next[x])
        for m in range(2):
            put(FIX1, m, x, fields[ERR1][m, x + 1] + value)

    phase(up_two, FIX1, functools.partial(send_last, P_FIX1))
    wait_faces(FIX1)

    def up_one(x):
        g, f = faces_at(x), factor[1, x]
        running = before[P_FIX1, x]
        for m in range(2):
            here, near = beside(FIX1, m, x, g)
            running = keep_weight * here + f * (rhs1[m, x] + 2.0 * near + running)
            for t in (2 * m, 2 * m + 1):
                put(SUM0, t, x, fields[FIRST][t, x + 1] + running)

    phase(up_one, SUM0, functools.partial(send_last, P_SUM0), awaited=P_FIX1)
    wait_faces(SUM0)
    wait_last(P_SUM0)

    def up_zero(x):
        g, f = faces_at(x), factor[0, x]
        running = before[P_SUM0, x]
        for t in range(steps):
            here, near = beside(SUM0, t, x, g)
            running = keep_weight * here + f * (hs[t, x] + near + running)
            put(SOL, t, x, running)
            sol_hbm[t, x] = running

    phase(up_zero, SOL, functools.partial(send_last, P_SOL))
    wait_faces(SOL)
    wait_last(P_SOL)

    def last_defect(x):
        g, diagonal = faces_at(x), 1.0 + coupling[x]
        earlier = before[P_SOL, x]
        for t in range(steps):
            here, near = beside(SOL, t, x, g)
            res_hbm[t, x] = hs[t, x] + earlier - (diagonal * here - near)
            earlier = here

    over_rows(last_defect)

    for i in range(FIELDS):
        if i in ((PAIR, PAIR2, ERR3, FIX2) if n_tm == 2 else (PART, PAIR, PART2, PAIR2)):
            continue
        for side in (XLO, XHI, YLO, YHI):
            @pl.when(has[side])
            def _(i=i, side=side):
                face_copy(i, side).wait_send()
                if i in (PART, PART2):
                    face_copy(i, side, True).wait_send()

    @pl.when(tm < n_tm - 1)
    def _():
        for i in range(7):
            for part in range(2):
                last_copy(i, part).wait_send()

    swap(0).wait_send()
    swap(1).wait_send()
    if n_tm > 2:
        @pl.when(tm < n_tm - 2)
        def _():
            for i in range(2):
                chain_copy(i, fields[ERR3]).wait_send()


def store(one, two, one_hbm, two_hbm, sem):
    copies = [pltpu.make_async_copy(one, one_hbm, sem.at[0]), pltpu.make_async_copy(two, two_hbm, sem.at[1])]
    for copy in copies:
        copy.start()
    for copy in copies:
        copy.wait()


def solution(mesh):
    n_tm, n_sx, n_sy = (mesh.shape[axis] for axis in ("tm", "sx", "sy"))
    f32 = jnp.float32

    def per_device(heat_source, conductivity, initial_iterate):
        steps, nx, ny, nz = heat_source.shape
        depth = (1, steps, steps, steps // 2, 1, 1, 1, steps // 2, steps, steps, 1, 1, 1, 1)
        scratch = [pltpu.VMEM((d, nx + 2, ny, nz), f32) for d in depth]
        scratch += [pltpu.VMEM((2, d, nx, nz), f32) for d in depth] * 2
        cells = (nx, ny, nz)
        dma = pltpu.SemaphoreType.DMA
        scratch += [
            pltpu.VMEM((steps,) + cells, f32),
            pltpu.VMEM((steps,) + cells, f32),
            pltpu.VMEM((7,) + cells, f32),
            pltpu.VMEM(cells, f32),
            pltpu.VMEM((steps // 2,) + cells, f32),
            pltpu.VMEM(cells, f32),
            pltpu.VMEM(cells, f32),
            pltpu.VMEM(cells, f32),
            pltpu.VMEM(cells, f32),
            pltpu.VMEM((2,) + cells, f32),
            pltpu.VMEM((6,) + cells, f32),
            pltpu.VMEM(cells, f32),
            pltpu.VMEM((4,) + cells, f32),
            dma((FIELDS, 4)), dma((FIELDS, 4)), dma((7, 2)), dma((7, 2)),
            dma((2,)), dma((2,)), dma((2,)), dma((2,)), dma((5,)),
        ]
        field = jax.ShapeDtypeStruct(heat_source.shape, f32)
        one, two = pl.pallas_call(
            functools.partial(kernel, n_tm, n_sx, n_sy),
            out_shape=(pltpu.VMEM(heat_source.shape, f32),) * 2,
            in_specs=[pl.BlockSpec(memory_space=pltpu.HBM)] * 3,
            out_specs=(pl.BlockSpec(memory_space=pltpu.VMEM),) * 2,
            scratch_shapes=scratch,
            compiler_params=pltpu.CompilerParams(
                collective_id=0, has_side_effects=True, vmem_limit_bytes=40000000
            ),
            name="vcycle",
        )(*(pltpu.with_memory_space_constraint(x, pltpu.HBM) for x in (heat_source, conductivity, initial_iterate)))
        return pl.pallas_call(
            store,
            out_shape=(field, field),
            in_specs=[pl.BlockSpec(memory_space=pltpu.VMEM)] * 2,
            out_specs=(pl.BlockSpec(memory_space=pltpu.HBM),) * 2,
            scratch_shapes=[dma((2,))],
            name="store",
        )(*(pltpu.with_memory_space_constraint(x, pltpu.VMEM) for x in (one, two)))

    placed = (P("tm", "sx", "sy", None), P("sx", "sy", None), P("tm", "sx", "sy", None))
    return jax.shard_map(
        per_device,
        mesh=mesh,
        in_specs=placed,
        out_specs=(P("tm", "sx", "sy", None), P("tm", "sx", "sy", None)),
        check_vma=False,
    )
```

```python
import functools

import jax
import jax.numpy as jnp
from jax import lax
from jax.experimental import pallas as pl
from jax.experimental.pallas import tpu as pltpu
from jax.sharding import PartitionSpec as P

relax_weight = 0.8
keep_weight = 1.0 - relax_weight
MESH = pl.DeviceIdType.MESH

KAPPA, INIT, FIRST, ERR1, ERR2, ERR3, FIX2, FIX1, SUM0, SOL, PART, PAIR, PART2, PAIR2 = range(14)
FIELDS = 14
P_INIT, P_FIRST, P_ERR1, P_ERR2, P_FIX1, P_SUM0, P_SOL = range(7)
XLO, XHI, YLO, YHI = range(4)


def kernel(n_tm, n_sx, n_sy, hs_hbm, k_hbm, in_hbm, sol_hbm, res_hbm, *scratch):
    fields = scratch[:FIELDS]
    yrecv = scratch[FIELDS:2 * FIELDS]
    ysend = scratch[2 * FIELDS:3 * FIELDS]
    (hs, res, before, second, rhs1, rhs2, rhs3, mine, theirs, chain,
     face, coupling, factor, send_sem, recv_sem, tsend, trecv,
     qsend, qrecv, csend, crecv, local) = scratch[3 * FIELDS:]
    steps, nx, ny, nz = hs.shape
    tm, sx, sy = lax.axis_index("tm"), lax.axis_index("sx"), lax.axis_index("sy")
    has = (sx > 0, sx < n_sx - 1, sy > 0, sy < n_sy - 1)
    partner = tm + 1 - 2 * lax.rem(tm, 2)
    even = lax.rem(tm, 2) == 0

    loads = [
        pltpu.make_async_copy(k_hbm, fields[KAPPA].at[0, pl.ds(1, nx)], local.at[0]),
        pltpu.make_async_copy(in_hbm, fields[INIT].at[:, pl.ds(1, nx)], local.at[1]),
        pltpu.make_async_copy(hs_hbm, hs, local.at[2]),
    ]
    for load in loads:
        load.start()

    barrier = pltpu.get_barrier_semaphore()
    greet = [
        (has[XLO], {"sx": sx - 1}), (has[XHI], {"sx": sx + 1}),
        (has[YLO], {"sy": sy - 1}), (has[YHI], {"sy": sy + 1}),
        (tm > 0, {"tm": tm - 1}), (tm < n_tm - 1, {"tm": tm + 1}),
    ]
    if n_tm == 2:
        greet += [
            (has[XLO], {"tm": partner, "sx": sx - 1}), (has[XHI], {"tm": partner, "sx": sx + 1}),
            (has[YLO], {"tm": partner, "sy": sy - 1}), (has[YHI], {"tm": partner, "sy": sy + 1}),
        ]
    if n_tm > 2:
        greet += [(tm > 1, {"tm": tm - 2}), (tm < n_tm - 2, {"tm": tm + 2})]
    count = jnp.int32(0)
    for there, device in greet:
        count = count + jnp.where(there, 1, 0)

        @pl.when(there)
        def _(device=device):
            pl.semaphore_signal(barrier, inc=1, device_id=device, device_id_type=MESH)

    pl.semaphore_wait(barrier, count)

    def face_copy(i, side, pair=False):
        field = fields[i]
        to = i + 1 if pair else i
        land = fields[to]
        if side == XLO:
            if i == INIT:
                src = in_hbm.at[:, pl.ds(0, 1)]
            elif i == KAPPA:
                src = k_hbm.at[pl.ds(0, 1)]
            else:
                src = field.at[:, pl.ds(1, 1)]
            dst, device = land.at[:, pl.ds(nx + 1, 1)], {"sx": sx - 1}
        elif side == XHI:
            if i == INIT:
                src = in_hbm.at[:, pl.ds(nx - 1, 1)]
            elif i == KAPPA:
                src = k_hbm.at[pl.ds(nx - 1, 1)]
            else:
                src = field.at[:, pl.ds(nx, 1)]
            dst, device = land.at[:, pl.ds(0, 1)], {"sx": sx + 1}
        elif side == YLO:
            src, dst, device = ysend[i].at[0], yrecv[to].at[1], {"sy": sy - 1}
        else:
            src, dst, device = ysend[i].at[1], yrecv[to].at[0], {"sy": sy + 1}
        if i == KAPPA and side in (XLO, XHI):
            dst = field.at[0, pl.ds(nx + 1 if side == XLO else 0, 1)]
        if pair:
            device["tm"] = partner
        return pltpu.make_async_remote_copy(
            src_ref=src, dst_ref=dst, send_sem=send_sem.at[to, side],
            recv_sem=recv_sem.at[to, side], device_id=device, device_id_type=MESH)

    def send_faces(i, sides, pair=False):
        for side in sides:
            @pl.when(has[side])
            def _(side=side):
                face_copy(i, side).start()
                if pair:
                    face_copy(i, side, True).start()

    def wait_faces(i, pair=False):
        for side in (YLO, YHI, XLO, XHI):
            @pl.when(has[side ^ 1])
            def _(side=side):
                face_copy(i, side, pair).wait_recv()

    half = nx // 2
    halves = (pl.ds(0, half), pl.ds(half, nx - half))

    def last_copy(i, part):
        field = fields[lasts[i]]
        if i == P_INIT:
            src = in_hbm.at[steps - 1, halves[part]]
        else:
            src = field.at[field.shape[0] - 1, (pl.ds(1, half), pl.ds(1 + half, nx - half))[part]]
        return pltpu.make_async_remote_copy(
            src_ref=src, dst_ref=before.at[i, halves[part]],
            send_sem=tsend.at[i, part], recv_sem=trecv.at[i, part],
            device_id={"tm": tm + 1}, device_id_type=MESH)

    lasts = (INIT, FIRST, ERR1, ERR2, FIX1, SUM0, SOL)

    def send_last(i, part):
        @pl.when(tm < n_tm - 1)
        def _():
            last_copy(i, part).start()

    def wait_last(i, parts=(0, 1)):
        @pl.when(tm > 0)
        def _():
            for part in parts:
                last_copy(i, part).wait_recv()

    send_faces(KAPPA, (XLO, XHI))
    send_faces(INIT, (XLO, XHI))
    send_last(P_INIT, 0)
    send_last(P_INIT, 1)

    def over_rows(body, by=8, start=0, stop=nx):
        def step(x, carry):
            body(x)
            return carry

        lax.fori_loop(start, stop, step, 0, unroll=by)

    def phase(body, i, send_part=None, pair=False, awaited=None):
        if awaited is not None:
            wait_last(awaited, (0,))
        body(0)
        if awaited is None:
            body(nx - 1)
            send_faces(i, (XLO, XHI), pair)
        else:
            send_faces(i, (XLO,), pair)
        over_rows(body, half - 1, 1, half)
        if send_part is not None:
            send_part(0)
        if awaited is not None:
            wait_last(awaited, (1,))
            body(nx - 1)
            send_faces(i, (XHI,), pair)
        over_rows(body, half - 1, half, nx - 1)
        send_faces(i, (YLO, YHI), pair)
        if send_part is not None:
            send_part(1)

    def put_faces(i, t, x, value):
        ysend[i][0, t, pl.ds(x, 1), :] = value[0:1, :]
        ysend[i][1, t, pl.ds(x, 1), :] = value[ny - 1:ny, :]

    def put(i, t, x, value):
        fields[i][t, x + 1] = value
        put_faces(i, t, x, value)

    loads[0].wait()
    loads[1].wait()

    def pack(x):
        put_faces(KAPPA, 0, x, fields[KAPPA][0, x + 1])
        for t in range(steps):
            put_faces(INIT, t, x, fields[INIT][t, x + 1])

    over_rows(pack)
    send_faces(KAPPA, (YLO, YHI))
    send_faces(INIT, (YLO, YHI))

    @pl.when(sx == 0)
    def _():
        for i in range(FIELDS):
            for t in range(fields[i].shape[0]):
                fields[i][t, 0] = jnp.zeros((ny, nz), jnp.float32)

    @pl.when(sx == n_sx - 1)
    def _():
        for i in range(FIELDS):
            for t in range(fields[i].shape[0]):
                fields[i][t, nx + 1] = jnp.zeros((ny, nz), jnp.float32)

    @pl.when(sy == 0)
    def _():
        for i in range(FIELDS):
            yrecv[i][0] = jnp.zeros(yrecv[i].shape[1:], jnp.float32)

    @pl.when(sy == n_sy - 1)
    def _():
        for i in range(FIELDS):
            yrecv[i][1] = jnp.zeros(yrecv[i].shape[1:], jnp.float32)

    @pl.when(tm == 0)
    def _():
        def clear(x):
            for i in range(7):
                before[i, x] = jnp.zeros((ny, nz), jnp.float32)

        over_rows(clear, 1)

    row = lax.broadcasted_iota(jnp.int32, (ny, nz), 0)
    column = lax.broadcasted_iota(jnp.int32, (ny, nz), 1)

    def around(i, t, x):
        field = fields[i]
        here = field[t, x + 1]
        return here, (
            field[t, x + 2],
            field[t, x],
            jnp.where(row == ny - 1, yrecv[i][1, t, pl.ds(x, 1), :], pltpu.roll(here, ny - 1, 0)),
            jnp.where(row == 0, yrecv[i][0, t, pl.ds(x, 1), :], pltpu.roll(here, 1, 0)),
            pltpu.roll(here, nz - 1, 1),
            pltpu.roll(here, 1, 1),
        )

    def beside(i, t, x, g):
        here, sides = around(i, t, x)
        terms = [g[j] * sides[j] for j in range(6)]
        return here, (terms[0] + terms[1]) + (terms[2] + terms[3]) + (terms[4] + terms[5])

    def faces_at(x):
        return [face[j, x] for j in range(6)]

    wait_faces(KAPPA)

    def coefficients(x):
        here, sides = around(KAPPA, 0, x)
        sides = list(sides)
        sides[4] = jnp.where(column == nz - 1, 0.0, sides[4])
        sides[5] = jnp.where(column == 0, 0.0, sides[5])
        g = [0.5 * (here + side) for side in sides]
        total = (g[0] + g[1]) + (g[2] + g[3]) + (g[4] + g[5])
        coupling[x] = total
        g[4] = jnp.where(column == nz - 1, 0.0, g[4])
        g[5] = jnp.where(column == 0, 0.0, g[5])
        for j in range(6):
            face[j, x] = g[j]
        for level in range(4):
            factor[level, x] = relax_weight / (1.0 + (2.0 ** level) * total)

    over_rows(coefficients)
    loads[2].wait()
    wait_faces(INIT)

    def sweep_first(x):
        g, f = faces_at(x), factor[0, x]
        running = before[P_INIT, x]
        for t in range(steps):
            here, near = beside(INIT, t, x, g)
            running = keep_weight * here + f * (hs[t, x] + near + running)
            put(FIRST, t, x, running)

    phase(sweep_first, FIRST, functools.partial(send_last, P_FIRST), awaited=P_INIT)
    wait_faces(FIRST)

    def down_one(x):
        g, diagonal, f = faces_at(x), 1.0 + coupling[x], factor[1, x]
        earlier = before[P_FIRST, x]
        running = None
        for m in range(steps // 2):
            total = None
            for t in (2 * m, 2 * m + 1):
                here, near = beside(FIRST, t, x, g)
                value = hs[t, x] + earlier - (diagonal * here - near)
                total = value if total is None else total + value
                earlier = here
            rhs1[m, x] = total
            running = f * total if running is None else f * (total + running)
            put(ERR1, m, x, running)

    phase(down_one, ERR1, functools.partial(send_last, P_ERR1), awaited=P_FIRST)
    wait_faces(ERR1)
    wait_last(P_ERR1)

    def down_two(x):
        g, diagonal, f = faces_at(x), 1.0 + 2.0 * coupling[x], factor[2, x]
        earlier = before[P_ERR1, x]
        total = None
        for t in range(2):
            here, near = beside(ERR1, t, x, g)
            value = rhs1[t, x] + earlier - (diagonal * here - 2.0 * near)
            total = value if total is None else total + value
            earlier = here
        rhs2[x] = total
        put(ERR2, 0, x, f * total)

    phase(down_two, ERR2, functools.partial(send_last, P_ERR2))
    wait_faces(ERR2)
    if n_tm > 2:
        wait_last(P_ERR2)

    def down_three(x):
        g, diagonal = faces_at(x), 1.0 + 4.0 * coupling[x]
        here, near = beside(ERR2, 0, x, g)
        earlier = here + before[P_ERR2, x] if n_tm > 2 else here
        value = rhs2[x] + jnp.where(even, earlier, 0.0) - (diagonal * here - 4.0 * near)
        mine[x] = value
        if n_tm == 2:
            put(PART, 0, x, factor[3, x] * value)

    def swap(part):
        return pltpu.make_async_remote_copy(
            src_ref=mine.at[halves[part]], dst_ref=theirs.at[halves[part]],
            send_sem=qsend.at[part], recv_sem=qrecv.at[part],
            device_id={"tm": partner}, device_id_type=MESH)

    if n_tm == 2:
        phase(down_three, PART, lambda part: swap(part).start(), True)
        wait_faces(PART)

        def part_two(x):
            here, near = beside(PART, 0, x, faces_at(x))
            put(PART2, 0, x, keep_weight * here + factor[3, x] * (mine[x] + 8.0 * near))

        phase(part_two, PART2, None, True)
    else:
        over_rows(down_three)
        swap(0).start()
        swap(1).start()
    swap(0).wait_recv()
    swap(1).wait_recv()

    def chain_copy(i, field):
        src = field.at[0, pl.ds(1, nx)] if i == 0 else second
        return pltpu.make_async_remote_copy(
            src_ref=src, dst_ref=chain.at[i], send_sem=csend.at[i],
            recv_sem=crecv.at[i], device_id={"tm": tm + 2}, device_id_type=MESH)

    def chain_wait(i):
        if n_tm > 2:
            @pl.when(tm > 1)
            def _():
                chain_copy(i, fields[ERR3]).wait_recv()

            @pl.when(tm < 2)
            def _():
                def clear(x):
                    chain[i, x] = jnp.zeros((ny, nz), jnp.float32)

                over_rows(clear, 1)

    def chain_send(i):
        if n_tm > 2:
            @pl.when(tm < n_tm - 2)
            def _():
                chain_copy(i, fields[ERR3]).start()

    chain_wait(0)

    def coarse_one(x):
        total = mine[x] + theirs[x]
        rhs3[x] = total
        if n_tm > 2:
            total = total + chain[0, x]
        value = factor[3, x] * total
        if n_tm > 2:
            put(ERR3, 0, x, value)
        else:
            fields[ERR3][0, x + 1] = value

    if n_tm > 2:
        phase(coarse_one, ERR3)
        chain_send(0)
        wait_faces(ERR3)
    else:
        over_rows(coarse_one)
        wait_faces(PART, True)
        for edge in (0, nx + 1):
            fields[ERR3][0, edge] = fields[PART][0, edge] + fields[PAIR][0, edge]
        for edge in range(2):
            yrecv[ERR3][edge, 0] = yrecv[PART][edge, 0] + yrecv[PAIR][edge, 0]
    if n_tm == 2:
        wait_last(P_ERR2)
    chain_wait(1)

    def coarse_two(x):
        here, near = beside(ERR3, 0, x, faces_at(x))
        total = rhs3[x] + 8.0 * near
        if n_tm > 2:
            total = total + chain[1, x]
        value = keep_weight * here + factor[3, x] * total
        if n_tm > 2:
            second[x] = value
            earlier = jnp.where(even, chain[1, x], value)
        else:
            earlier = jnp.where(even, 0.0, value)
        mine_next[x] = before[P_ERR2, x] + earlier
        value = fields[ERR2][0, x + 1] + value
        if n_tm > 2:
            put(FIX2, 0, x, value)
        else:
            fields[FIX2][0, x + 1] = value

    mine_next = res.at[0]
    if n_tm > 2:
        phase(coarse_two, FIX2)
        chain_send(1)
        wait_faces(FIX2)
    else:
        over_rows(coarse_two)
        wait_faces(PART2)
        wait_faces(PART2, True)
        for edge in (0, nx + 1):
            fields[FIX2][0, edge] = fields[ERR2][0, edge] + (
                fields[PART2][0, edge] + fields[PAIR2][0, edge])
        for edge in range(2):
            yrecv[FIX2][edge, 0] = yrecv[ERR2][edge, 0] + (
                yrecv[PART2][edge, 0] + yrecv[PAIR2][edge, 0])

    def up_two(x):
        here, near = beside(FIX2, 0, x, faces_at(x))
        value = keep_weight * here + factor[2, x] * (rhs2[x] + 4.0 * near + mine_next[x])
        for m in range(2):
            put(FIX1, m, x, fields[ERR1][m, x + 1] + value)

    phase(up_two, FIX1, functools.partial(send_last, P_FIX1))
    wait_faces(FIX1)

    def up_one(x):
        g, f = faces_at(x), factor[1, x]
        running = before[P_FIX1, x]
        for m in range(2):
            here, near = beside(FIX1, m, x, g)
            running = keep_weight * here + f * (rhs1[m, x] + 2.0 * near + running)
            for t in (2 * m, 2 * m + 1):
                put(SUM0, t, x, fields[FIRST][t, x + 1] + running)

    phase(up_one, SUM0, functools.partial(send_last, P_SUM0), awaited=P_FIX1)
    wait_faces(SUM0)
    wait_last(P_SUM0)

    def up_zero(x):
        g, f = faces_at(x), factor[0, x]
        running = before[P_SUM0, x]
        for t in range(steps):
            here, near = beside(SUM0, t, x, g)
            running = keep_weight * here + f * (hs[t, x] + near + running)
            put(SOL, t, x, running)
            sol_hbm[t, x] = running

    phase(up_zero, SOL, functools.partial(send_last, P_SOL))
    wait_faces(SOL)
    wait_last(P_SOL)

    def last_defect(x):
        g, diagonal = faces_at(x), 1.0 + coupling[x]
        earlier = before[P_SOL, x]
        for t in range(steps):
            here, near = beside(SOL, t, x, g)
            res_hbm[t, x] = hs[t, x] + earlier - (diagonal * here - near)
            earlier = here

    over_rows(last_defect)

    for i in range(FIELDS):
        if i in ((PAIR, PAIR2, ERR3, FIX2) if n_tm == 2 else (PART, PAIR, PART2, PAIR2)):
            continue
        for side in (XLO, XHI, YLO, YHI):
            @pl.when(has[side])
            def _(i=i, side=side):
                face_copy(i, side).wait_send()
                if i in (PART, PART2):
                    face_copy(i, side, True).wait_send()

    @pl.when(tm < n_tm - 1)
    def _():
        for i in range(7):
            for part in range(2):
                last_copy(i, part).wait_send()

    swap(0).wait_send()
    swap(1).wait_send()
    if n_tm > 2:
        @pl.when(tm < n_tm - 2)
        def _():
            for i in range(2):
                chain_copy(i, fields[ERR3]).wait_send()


DEPTH = 6
EDGE = 8
EXCHANGES = {
    "kappa": ("k", (0, 1), ()),
    "kappa_far": ("k", (1, 6), ((0, 5, 0, 5),)),
    "init": ("in", (0, 1), ()),
    "source": ("hs", (0, 1), ()),
    "first": ("first", (0, 1), ()),
    "first_far": ("first", (1, 2), ((0, 1, 0, 1),)),
    "pair": ("pair", (0, 2), ((0, 1, 0, 1),)),
    "err": ("err", (0, 5), ((0, 4, 0, 4),)),
    "last": ("last", (0, 5), ((0, 4, 0, 4),)),
    "prev_one": ("prev", (0, 5), ((0, 4, 0, 4),)),
    "prev_zero": ("prev", (0, 5), ((0, 4, 0, 4),)),
    "rhs3": ("rhs3", (0, 5), ((0, 4, 0, 4),)),
}
NAMES = tuple(EXCHANGES)
X_FACES = ((-1, 0), (1, 0))
REST = ((0, -1), (0, 1), (-1, -1), (-1, 1), (1, -1), (1, 1))
ALL = X_FACES + REST
T_INIT, T_LAST, T_ONE, T_ZERO, T_MINE, T_GUESS = range(6)


def wide_kernel(n_sx, n_sy, hs_hbm, k_hbm, in_hbm, sol_out, res_out,
                kap, ini, src, first, pair, err, last, prev, sums, fr, rhs3, one, err3, wave,
                err2, fix, vee, total, sol, face, coupling, factor,
                before, mine, theirs, guess, ahead,
                send_sem, recv_sem, tsend, trecv, local):
    nx, ny, nz = k_hbm.shape
    steps = in_hbm.shape[0]
    wide = ny + 2 * EDGE
    tm, sx, sy = lax.axis_index("tm"), lax.axis_index("sx"), lax.axis_index("sy")
    at_one = jnp.where(tm > 0, 1.0, 0.0)
    at_zero = 1.0 - at_one
    mid = pl.ds(EDGE, ny)
    inner = pl.ds(DEPTH, nx)
    homes = {"k": kap, "in": ini, "hs": src, "first": first, "pair": pair, "err": err,
             "last": last, "prev": prev, "rhs3": rhs3}
    outside = {"k": k_hbm, "in": in_hbm, "hs": hs_hbm}

    loads = [
        pltpu.make_async_copy(k_hbm, kap.at[0, inner, mid], local.at[0]),
        pltpu.make_async_copy(in_hbm, ini.at[:, inner, mid], local.at[1]),
        pltpu.make_async_copy(hs_hbm, src.at[:, inner, mid], local.at[2]),
    ]
    for load in loads:
        load.start()

    def there(way, sign=1):
        ok = None
        for step, at, size in ((sign * way[0], sx, n_sx), (sign * way[1], sy, n_sy)):
            if step:
                here = at > 0 if step < 0 else at < size - 1
                ok = here if ok is None else jnp.logical_and(ok, here)
        return ok

    def target(way):
        device = {}
        if way[0]:
            device["sx"] = sx + way[0]
        if way[1]:
            device["sy"] = sy + way[1]
        return device

    barrier = pltpu.get_barrier_semaphore()
    count = jnp.int32(1)
    for way in ALL:
        count = count + jnp.where(there(way), 1, 0)

        @pl.when(there(way))
        def _(way=way):
            pl.semaphore_signal(barrier, inc=1, device_id=target(way), device_id_type=MESH)

    pl.semaphore_signal(barrier, inc=1, device_id={"tm": 1 - tm}, device_id_type=MESH)

    def rows(body, depth, by=4):
        def step(x, carry):
            body(x)
            return carry

        lax.fori_loop(DEPTH - depth, DEPTH + nx + depth, step, 0, unroll=by)

    filled = ((kap, 6), (ini, 1), (src, 1), (first, 2), (pair, 2), (err, 5), (last, 5), (prev, 5), (rhs3, 5))
    plane = jnp.zeros((wide, nz), jnp.float32)
    strip = jnp.zeros((EDGE, nz), jnp.float32)

    def fill(edge_rows):
        for array, depth in filled:
            for t in range(array.shape[0]):
                for i in range(depth):
                    array[t, DEPTH - 1 - i if edge_rows < 0 else DEPTH + nx + i] = plane

    def fill_side(start):
        for array, depth in filled:
            def body(x):
                for t in range(array.shape[0]):
                    array[t, x, pl.ds(start, EDGE), :] = strip

            rows(body, depth)

    @pl.when(sx == 0)
    def _():
        fill(-1)

    @pl.when(sx == n_sx - 1)
    def _():
        fill(1)

    @pl.when(sy == 0)
    def _():
        fill_side(0)

    @pl.when(sy == n_sy - 1)
    def _():
        fill_side(EDGE + ny)

    @pl.when(tm == 0)
    def _():
        def body(x):
            last[0, x] = plane
            prev[0, x] = plane
            prev[1, x] = plane

        rows(body, 5)

        def empty(x):
            before[x - DEPTH] = jnp.zeros((ny, nz), jnp.float32)
            ahead[x - DEPTH] = jnp.zeros((ny, nz), jnp.float32)

        rows(empty, 0)

    pl.semaphore_wait(barrier, count)

    def span(step, size, low, high):
        if step == 0:
            return 0, size, 0
        if step < 0:
            return low, high - low, size + low
        return size - high, high - low, -high

    def pieces(name, ways):
        kind, (low, high), corners = EXCHANGES[name]
        slot = 0
        for way in ALL:
            boxes = corners if way[0] and way[1] else ((low, high, low, high),)
            for box in boxes:
                if way in ways:
                    yield way, box, slot
                slot += 1

    def copy_of(name, way, box, slot):
        kind = EXCHANGES[name][0]
        land = homes[kind]
        fx, wx, tx = span(way[0], nx, box[0], box[1])
        fy, wy, ty = span(way[1], ny, box[2], box[3])
        steps_at = {"prev_zero": pl.ds(0, 1), "prev_one": pl.ds(1, 1)}.get(name, slice(None))
        if kind == "k":
            source = k_hbm.at[pl.ds(fx, wx), pl.ds(fy, wy)]
            dest = land.at[0, pl.ds(DEPTH + tx, wx), pl.ds(EDGE + ty, wy)]
        else:
            if kind in outside:
                source = outside[kind].at[:, pl.ds(fx, wx), pl.ds(fy, wy)]
            else:
                source = land.at[steps_at, pl.ds(DEPTH + fx, wx), pl.ds(EDGE + fy, wy)]
            dest = land.at[steps_at, pl.ds(DEPTH + tx, wx), pl.ds(EDGE + ty, wy)]
        number = NAMES.index(name)
        return pltpu.make_async_remote_copy(
            src_ref=source, dst_ref=dest, send_sem=send_sem.at[number, slot],
            recv_sem=recv_sem.at[number, slot], device_id=target(way), device_id_type=MESH)

    def send(name, ways=ALL):
        for way, box, slot in pieces(name, ways):
            @pl.when(there(way))
            def _(way=way, box=box, slot=slot):
                copy_of(name, way, box, slot).start()

    def wait(name):
        for way, box, slot in pieces(name, REST + X_FACES):
            @pl.when(there(way, -1))
            def _(way=way, box=box, slot=slot):
                copy_of(name, way, box, slot).wait_recv()

    def wait_sent(name):
        for way, box, slot in pieces(name, ALL):
            @pl.when(there(way))
            def _(way=way, box=box, slot=slot):
                copy_of(name, way, box, slot).wait_send()

    half = nx // 2
    ends = ((0, half), (half, nx - half))

    def across(which, part):
        low, size = ends[part]
        near, far = pl.ds(low, size), pl.ds(DEPTH + low, size)
        source, dest = {
            T_INIT: lambda: (in_hbm.at[steps - 1, near], before.at[near]),
            T_LAST: lambda: (first.at[steps - 1, far, mid], last.at[0, far, mid]),
            T_ONE: lambda: (err.at[1, far, mid], prev.at[1, far, mid]),
            T_ZERO: lambda: (err.at[0, far, mid], prev.at[0, far, mid]),
            T_MINE: lambda: (mine.at[near], theirs.at[near]),
            T_GUESS: lambda: (guess.at[near], ahead.at[near]),
        }[which]()
        return pltpu.make_async_remote_copy(
            src_ref=source, dst_ref=dest, send_sem=tsend.at[which, part],
            recv_sem=trecv.at[which, part], device_id={"tm": 1 - tm}, device_id_type=MESH)

    def pass_on(which, parts=(0, 1)):
        @pl.when(tm == 0)
        def _():
            for part in parts:
                across(which, part).start()

    def arrive(which, parts=(0, 1)):
        @pl.when(tm > 0)
        def _():
            for part in parts:
                across(which, part).wait_recv()

    send("kappa")
    send("init")
    pass_on(T_INIT)
    send("source")
    send("kappa_far")

    column = lax.broadcasted_iota(jnp.int32, (wide, nz), 1)
    height = lax.broadcasted_iota(jnp.int32, (wide, nz), 0)
    low_side = jnp.where(sy == 0, EDGE, 0)
    high_side = jnp.where(sy == n_sy - 1, EDGE + ny, wide)
    within = jnp.logical_and(height >= low_side, height < high_side)
    low_row = jnp.where(sx == 0, DEPTH, 0)
    high_row = jnp.where(sx == n_sx - 1, DEPTH + nx, nx + 2 * DEPTH)

    def around(ref, t, x):
        here = ref[t, x]
        return here, (
            ref[t, x + 1], ref[t, x - 1],
            pltpu.roll(here, wide - 1, 0), pltpu.roll(here, 1, 0),
            pltpu.roll(here, nz - 1, 1), pltpu.roll(here, 1, 1),
        )

    def around_mid(ref, t, x):
        here = ref[t, x, mid, :]
        return here, (
            ref[t, x + 1, mid, :], ref[t, x - 1, mid, :],
            ref[t, x, pl.ds(EDGE + 1, ny), :], ref[t, x, pl.ds(EDGE - 1, ny), :],
            pltpu.roll(here, nz - 1, 1), pltpu.roll(here, 1, 1),
        )

    def beside(ref, t, x, g):
        here, sides = (around if g[0].shape[0] == wide else around_mid)(ref, t, x)
        terms = [g[j] * sides[j] for j in range(6)]
        return here, (terms[0] + terms[1]) + (terms[2] + terms[3]) + (terms[4] + terms[5])

    def faces(x):
        return [face[j, x] for j in range(6)]

    def faces_mid(x):
        return [face[j, x, mid, :] for j in range(6)]

    def couple(here, sides, col):
        sides = list(sides)
        top, bottom = col == nz - 1, col == 0
        sides[4] = jnp.where(top, 0.0, sides[4])
        sides[5] = jnp.where(bottom, 0.0, sides[5])
        g = [0.5 * (here + side) for side in sides]
        whole = (g[0] + g[1]) + (g[2] + g[3]) + (g[4] + g[5])
        g[4] = jnp.where(top, 0.0, g[4])
        g[5] = jnp.where(bottom, 0.0, g[5])
        return g, whole

    def coefficients_mid(x):
        g, whole = couple(*around_mid(kap, 0, x), column[:ny])
        coupling[x, mid, :] = whole
        for j in range(6):
            face[j, x, mid, :] = g[j]
        for level in range(2):
            factor[level, x, mid, :] = relax_weight / (1.0 + (2.0 ** level) * whole)

    def coefficients(x):
        g, whole = couple(*around(kap, 0, x), column)
        coupling[x] = whole
        inside = jnp.logical_and(within, jnp.logical_and(x >= low_row, x < high_row))
        for j in range(6):
            face[j, x] = g[j]
        for level in range(4):
            factor[level, x] = jnp.where(inside, relax_weight / (1.0 + (2.0 ** level) * whole), 0.0)

    def phase(body, edge, name):
        for i in range(edge):
            body(DEPTH + i)
            body(DEPTH + nx - 1 - i)
        send(name, X_FACES)

        def step(x, carry):
            body(x)
            return carry

        lax.fori_loop(DEPTH + edge, DEPTH + nx - edge, step, 0, unroll=4)
        send(name, REST)

    loads[0].wait()
    wait("kappa")
    rows(coefficients_mid, 0)
    loads[1].wait()
    loads[2].wait()
    wait("init")
    arrive(T_INIT)

    def sweep_first(x):
        g, f = faces_mid(x), factor[0, x, mid, :]
        running = before[x - DEPTH]
        for t in range(steps):
            here, near = beside(ini, t, x, g)
            running = keep_weight * here + f * (src[t, x, mid, :] + near + running)
            first[t, x, mid, :] = running

    phase(sweep_first, 1, "first")
    pass_on(T_LAST)
    wait("kappa_far")
    rows(coefficients, 5)
    send("first_far")
    wait("first")

    def down_one(x):
        g, f, c = faces_mid(x), factor[0, x, mid, :], coupling[x, mid, :]
        f_one = factor[1, x, mid, :]
        diagonal = 1.0 + c
        earlier = None
        ahead_value = None
        running = None
        pair_zero = None
        for m in range(2):
            both = None
            for t in (2 * m, 2 * m + 1):
                here, near = beside(first, t, x, g)
                supply = src[t, x, mid, :] + near
                value = supply - diagonal * here
                if earlier is not None:
                    value = value + earlier
                both = value if both is None else both + value
                ahead_value = keep_weight * here + f * (supply if ahead_value is None else supply + ahead_value)
                earlier = here
            running = f_one * both if running is None else f_one * (both + running)
            err[m, x, mid, :] = running
            pair_zero = running if m == 0 else pair_zero
        both = pair_zero + running
        pair[1, x, mid, :] = both
        pair[0, x, mid, :] = both + at_zero * ((f_one + f_one * f_one) * earlier)
        pair[2, x, mid, :] = at_zero * running
        guess[x - DEPTH] = ahead_value

    phase(down_one, 2, "pair")
    pass_on(T_ONE)
    pass_on(T_ZERO)
    send("err")
    arrive(T_LAST)

    @pl.when(tm > 0)
    def _():
        send("last")

    wait("pair")

    def down_two(x):
        here, near = beside(pair, 0, x, faces(x))
        value = 0.25 * (1.0 + 2.0 * coupling[x]) * here + 2.0 * near + pair[2, x]
        fr[0, x] = factor[2, x] * value

    rows(down_two, 1)

    def down_three(x):
        g, c = faces_mid(x), coupling[x, mid, :]
        here, near = beside(fr, 0, x, g)
        value = 0.25 * (1.0 + 4.0 * c) * here + 4.0 * near
        here, near = beside(pair, 1, x, g)
        base = factor[2, x, mid, :] * (0.25 * (1.0 + 2.0 * c) * here + 2.0 * near)
        mine[x - DEPTH] = value + at_zero * base

    rows(down_three, 0)
    across(T_MINE, 0).start()
    across(T_MINE, 1).start()
    pass_on(T_GUESS)
    arrive(T_ONE)

    @pl.when(tm > 0)
    def _():
        send("prev_one")

    arrive(T_ZERO)

    @pl.when(tm > 0)
    def _():
        send("prev_zero")

    across(T_MINE, 0).wait_recv()
    across(T_MINE, 1).wait_recv()

    def add_up(x):
        rhs3[0, x, mid, :] = mine[x - DEPTH] + theirs[x - DEPTH]

    rows(add_up, 0)
    send("rhs3")

    wait("err")
    wait("first_far")

    @pl.when(tm > 0)
    def _():
        wait("last")
        wait("prev_one")
        wait("prev_zero")

    def gather_far(x):
        f = factor[1, x]
        sums[0, x] = err[0, x] + err[1, x] + (f + f * f) * last[0, x]
        sums[1, x] = prev[0, x] + prev[1, x]

    rows(gather_far, 5)

    def level_two(x):
        g, f, weight = faces(x), factor[2, x], 0.25 * (1.0 + 2.0 * coupling[x])
        here, near = beside(sums, 0, x, g)
        err2[0, x] = f * (weight * here + 2.0 * near + prev[1, x])
        here, near = beside(sums, 1, x, g)
        err2[1, x] = f * (weight * here + 2.0 * near)

    rows(level_two, 4)

    def own_errors(x):
        f = factor[1, x]
        carried = f * last[0, x]
        return err[0, x] + carried, err[1, x] + f * carried

    def fix_two(x):
        g, f = faces(x), factor[2, x]
        own, near = beside(err2, 0, x, g)
        past, near_past = beside(err2, 1, x, g)
        value = (2.0 - relax_weight) * own + f * (4.0 * near + past)
        value_past = (2.0 - relax_weight) * past + 4.0 * (f * near_past)
        zero, first_one = own_errors(x)
        fix[0, x] = zero + value
        fix[1, x] = first_one + value
        fix[2, x] = prev[0, x] + value_past
        fix[3, x] = prev[1, x] + value_past

    rows(fix_two, 3)

    def fix_one(x):
        g, f = faces(x), factor[1, x]
        here, near = [], []
        for i in range(4):
            a, b = beside(fix, i, x, g)
            here.append(a)
            near.append(keep_weight * a + 2.0 * (f * b))
        zero, first_one = own_errors(x)
        value = near[0] + zero + f * here[3]
        vee[0, x] = value
        vee[1, x] = near[1] + first_one + f * (value - zero)
        value = near[2] + prev[0, x]
        vee[2, x] = value
        vee[3, x] = near[3] + prev[1, x] + f * (value - prev[0, x])

    rows(fix_one, 2)
    wait("rhs3")

    def coarse_one(x):
        one[0, x] = factor[3, x] * rhs3[0, x]

    rows(coarse_one, 5)

    def coarse_two(x):
        here, near = beside(one, 0, x, faces(x))
        err3[0, x] = keep_weight * here + factor[3, x] * (rhs3[0, x] + 8.0 * near)

    rows(coarse_two, 4)

    def up_two(x):
        f = factor[2, x]
        here, near = beside(err3, 0, x, faces(x))
        value = keep_weight * here + 4.0 * (f * near)
        wave[0, x] = value + at_one * (f * here)
        wave[1, x] = value

    rows(up_two, 3)

    def up_one(x):
        g, f = faces(x), factor[1, x]
        here, near = beside(wave, 0, x, g)
        past, near_past = beside(wave, 1, x, g)
        own = keep_weight * here + 2.0 * (f * near)
        shadow = at_one * (keep_weight * past + 2.0 * (f * near_past))
        zero = own + at_one * (f * past)
        gain = (vee[0, x] + zero, vee[1, x] + own + f * zero)
        for t in range(steps):
            total[t, x] = first[t, x] + gain[t // 2]
        vee[2, x] = vee[2, x] + shadow
        vee[3, x] = vee[3, x] + shadow + f * shadow

    rows(up_one, 2)
    wait("source")

    def up_zero(x):
        g, f = faces(x), factor[0, x]
        running = last[0, x] + vee[3, x]
        for t in range(steps):
            here, near = beside(total, t, x, g)
            running = keep_weight * here + f * (src[t, x] + near + running)
            sol[t, x] = running

    rows(up_zero, 1)
    arrive(T_GUESS)

    def finish(x):
        g, f = faces_mid(x), factor[0, x, mid, :]
        diagonal = 1.0 + coupling[x, mid, :]
        lifted = []
        for i in (2, 3):
            here, near = beside(vee, i, x, g)
            lifted.append(keep_weight * here + f * near)
        earlier = ahead[x - DEPTH] + (1.0 + f) * (f * f * lifted[0] + lifted[1])
        for t in range(steps):
            here, near = beside(sol, t, x, g)
            sol_out[t, x - DEPTH] = here
            res_out[t, x - DEPTH] = src[t, x, mid, :] + earlier - (diagonal * here - near)
            earlier = here

    rows(finish, 0)

    for name in NAMES:
        if name in ("last", "prev_one", "prev_zero"):
            @pl.when(tm > 0)
            def _(name=name):
                wait_sent(name)
        else:
            wait_sent(name)

    @pl.when(tm == 0)
    def _():
        for which in (T_INIT, T_LAST, T_ONE, T_ZERO, T_GUESS):
            for part in range(2):
                across(which, part).wait_send()

    across(T_MINE, 0).wait_send()
    across(T_MINE, 1).wait_send()


def wide_scratch(steps, nx, ny, nz):
    f32, dma = jnp.float32, pltpu.SemaphoreType.DMA
    depths = (1, steps, steps, steps, 3, 2, 1, 2, 2, 1, 1, 1, 1, 2, 2, 4, 4, steps, steps, 6)
    large = (nx + 2 * DEPTH, ny + 2 * EDGE, nz)
    scratch = [pltpu.VMEM((d,) + large, f32) for d in depths]
    scratch += [pltpu.VMEM(large, f32), pltpu.VMEM((4,) + large, f32)]
    scratch += [pltpu.VMEM((nx, ny, nz), f32)] * 5
    scratch += [dma((len(NAMES), 12)), dma((len(NAMES), 12)), dma((6, 2)), dma((6, 2)), dma((3,))]
    return scratch


def store(one, two, one_hbm, two_hbm, sem):
    copies = [pltpu.make_async_copy(one, one_hbm, sem.at[0]), pltpu.make_async_copy(two, two_hbm, sem.at[1])]
    for copy in copies:
        copy.start()
    for copy in copies:
        copy.wait()


def solution(mesh):
    n_tm, n_sx, n_sy = (mesh.shape[axis] for axis in ("tm", "sx", "sy"))
    f32 = jnp.float32

    def per_device(heat_source, conductivity, initial_iterate):
        steps, nx, ny, nz = heat_source.shape
        depth = (1, steps, steps, steps // 2, 1, 1, 1, steps // 2, steps, steps, 1, 1, 1, 1)
        scratch = [pltpu.VMEM((d, nx + 2, ny, nz), f32) for d in depth]
        scratch += [pltpu.VMEM((2, d, nx, nz), f32) for d in depth] * 2
        cells = (nx, ny, nz)
        dma = pltpu.SemaphoreType.DMA
        scratch += [
            pltpu.VMEM((steps,) + cells, f32),
            pltpu.VMEM((steps,) + cells, f32),
            pltpu.VMEM((7,) + cells, f32),
            pltpu.VMEM(cells, f32),
            pltpu.VMEM((steps // 2,) + cells, f32),
            pltpu.VMEM(cells, f32),
            pltpu.VMEM(cells, f32),
            pltpu.VMEM(cells, f32),
            pltpu.VMEM(cells, f32),
            pltpu.VMEM((2,) + cells, f32),
            pltpu.VMEM((6,) + cells, f32),
            pltpu.VMEM(cells, f32),
            pltpu.VMEM((4,) + cells, f32),
            dma((FIELDS, 4)), dma((FIELDS, 4)), dma((7, 2)), dma((7, 2)),
            dma((2,)), dma((2,)), dma((2,)), dma((2,)), dma((5,)),
        ]
        field = jax.ShapeDtypeStruct(heat_source.shape, f32)
        small = n_tm == 2 and steps == 4 and nx >= DEPTH and ny >= EDGE and ny % EDGE == 0
        if small:
            scratch = wide_scratch(steps, nx, ny, nz)
        one, two = pl.pallas_call(
            functools.partial(wide_kernel, n_sx, n_sy) if small else functools.partial(kernel, n_tm, n_sx, n_sy),
            out_shape=(pltpu.VMEM(heat_source.shape, f32),) * 2,
            in_specs=[pl.BlockSpec(memory_space=pltpu.HBM)] * 3,
            out_specs=(pl.BlockSpec(memory_space=pltpu.VMEM),) * 2,
            scratch_shapes=scratch,
            compiler_params=pltpu.CompilerParams(
                collective_id=0, has_side_effects=True, vmem_limit_bytes=40000000
            ),
            name="vcycle",
        )(*(pltpu.with_memory_space_constraint(x, pltpu.HBM) for x in (heat_source, conductivity, initial_iterate)))
        return pl.pallas_call(
            store,
            out_shape=(field, field),
            in_specs=[pl.BlockSpec(memory_space=pltpu.VMEM)] * 2,
            out_specs=(pl.BlockSpec(memory_space=pltpu.HBM),) * 2,
            scratch_shapes=[dma((2,))],
            name="store",
        )(*(pltpu.with_memory_space_constraint(x, pltpu.VMEM) for x in (one, two)))

    placed = (P("tm", "sx", "sy", None), P("sx", "sy", None), P("tm", "sx", "sy", None))
    return jax.shard_map(
        per_device,
        mesh=mesh,
        in_specs=placed,
        out_specs=(P("tm", "sx", "sy", None), P("tm", "sx", "sy", None)),
        check_vma=False,
    )
```

```python
import functools

import jax
import jax.numpy as jnp
from jax import lax
from jax.experimental import pallas as pl
from jax.experimental.pallas import tpu as pltpu
from jax.sharding import PartitionSpec as P

relax_weight = 0.8
keep_weight = 1.0 - relax_weight
MESH = pl.DeviceIdType.MESH

KAPPA, INIT, FIRST, ERR1, ERR2, ERR3, FIX2, FIX1, SUM0, SOL, PART, PAIR, PART2, PAIR2 = range(14)
FIELDS = 14
P_INIT, P_FIRST, P_ERR1, P_ERR2, P_FIX1, P_SUM0, P_SOL = range(7)
XLO, XHI, YLO, YHI = range(4)


def kernel(n_tm, n_sx, n_sy, hs_hbm, k_hbm, in_hbm, sol_hbm, res_hbm, *scratch):
    fields = scratch[:FIELDS]
    yrecv = scratch[FIELDS:2 * FIELDS]
    ysend = scratch[2 * FIELDS:3 * FIELDS]
    (hs, res, before, second, rhs1, rhs2, rhs3, mine, theirs, chain,
     face, coupling, factor, send_sem, recv_sem, tsend, trecv,
     qsend, qrecv, csend, crecv, local) = scratch[3 * FIELDS:]
    steps, nx, ny, nz = hs.shape
    tm, sx, sy = lax.axis_index("tm"), lax.axis_index("sx"), lax.axis_index("sy")
    has = (sx > 0, sx < n_sx - 1, sy > 0, sy < n_sy - 1)
    partner = tm + 1 - 2 * lax.rem(tm, 2)
    even = lax.rem(tm, 2) == 0

    loads = [
        pltpu.make_async_copy(k_hbm, fields[KAPPA].at[0, pl.ds(1, nx)], local.at[0]),
        pltpu.make_async_copy(in_hbm, fields[INIT].at[:, pl.ds(1, nx)], local.at[1]),
        pltpu.make_async_copy(hs_hbm, hs, local.at[2]),
    ]
    for load in loads:
        load.start()

    barrier = pltpu.get_barrier_semaphore()
    greet = [
        (has[XLO], {"sx": sx - 1}), (has[XHI], {"sx": sx + 1}),
        (has[YLO], {"sy": sy - 1}), (has[YHI], {"sy": sy + 1}),
        (tm > 0, {"tm": tm - 1}), (tm < n_tm - 1, {"tm": tm + 1}),
    ]
    if n_tm == 2:
        greet += [
            (has[XLO], {"tm": partner, "sx": sx - 1}), (has[XHI], {"tm": partner, "sx": sx + 1}),
            (has[YLO], {"tm": partner, "sy": sy - 1}), (has[YHI], {"tm": partner, "sy": sy + 1}),
        ]
    if n_tm > 2:
        greet += [(tm > 1, {"tm": tm - 2}), (tm < n_tm - 2, {"tm": tm + 2})]
    count = jnp.int32(0)
    for there, device in greet:
        count = count + jnp.where(there, 1, 0)

        @pl.when(there)
        def _(device=device):
            pl.semaphore_signal(barrier, inc=1, device_id=device, device_id_type=MESH)

    pl.semaphore_wait(barrier, count)

    def face_copy(i, side, pair=False):
        field = fields[i]
        to = i + 1 if pair else i
        land = fields[to]
        if side == XLO:
            if i == INIT:
                src = in_hbm.at[:, pl.ds(0, 1)]
            elif i == KAPPA:
                src = k_hbm.at[pl.ds(0, 1)]
            else:
                src = field.at[:, pl.ds(1, 1)]
            dst, device = land.at[:, pl.ds(nx + 1, 1)], {"sx": sx - 1}
        elif side == XHI:
            if i == INIT:
                src = in_hbm.at[:, pl.ds(nx - 1, 1)]
            elif i == KAPPA:
                src = k_hbm.at[pl.ds(nx - 1, 1)]
            else:
                src = field.at[:, pl.ds(nx, 1)]
            dst, device = land.at[:, pl.ds(0, 1)], {"sx": sx + 1}
        elif side == YLO:
            src, dst, device = ysend[i].at[0], yrecv[to].at[1], {"sy": sy - 1}
        else:
            src, dst, device = ysend[i].at[1], yrecv[to].at[0], {"sy": sy + 1}
        if i == KAPPA and side in (XLO, XHI):
            dst = field.at[0, pl.ds(nx + 1 if side == XLO else 0, 1)]
        if pair:
            device["tm"] = partner
        return pltpu.make_async_remote_copy(
            src_ref=src, dst_ref=dst, send_sem=send_sem.at[to, side],
            recv_sem=recv_sem.at[to, side], device_id=device, device_id_type=MESH)

    def send_faces(i, sides, pair=False):
        for side in sides:
            @pl.when(has[side])
            def _(side=side):
                face_copy(i, side).start()
                if pair:
                    face_copy(i, side, True).start()

    def wait_faces(i, pair=False):
        for side in (YLO, YHI, XLO, XHI):
            @pl.when(has[side ^ 1])
            def _(side=side):
                face_copy(i, side, pair).wait_recv()

    half = nx // 2
    halves = (pl.ds(0, half), pl.ds(half, nx - half))

    def last_copy(i, part):
        field = fields[lasts[i]]
        if i == P_INIT:
            src = in_hbm.at[steps - 1, halves[part]]
        else:
            src = field.at[field.shape[0] - 1, (pl.ds(1, half), pl.ds(1 + half, nx - half))[part]]
        return pltpu.make_async_remote_copy(
            src_ref=src, dst_ref=before.at[i, halves[part]],
            send_sem=tsend.at[i, part], recv_sem=trecv.at[i, part],
            device_id={"tm": tm + 1}, device_id_type=MESH)

    lasts = (INIT, FIRST, ERR1, ERR2, FIX1, SUM0, SOL)

    def send_last(i, part):
        @pl.when(tm < n_tm - 1)
        def _():
            last_copy(i, part).start()

    def wait_last(i, parts=(0, 1)):
        @pl.when(tm > 0)
        def _():
            for part in parts:
                last_copy(i, part).wait_recv()

    send_faces(KAPPA, (XLO, XHI))
    send_faces(INIT, (XLO, XHI))
    send_last(P_INIT, 0)
    send_last(P_INIT, 1)

    def over_rows(body, by=8, start=0, stop=nx):
        def step(x, carry):
            body(x)
            return carry

        lax.fori_loop(start, stop, step, 0, unroll=by)

    def phase(body, i, send_part=None, pair=False, awaited=None):
        if awaited is not None:
            wait_last(awaited, (0,))
        body(0)
        if awaited is None:
            body(nx - 1)
            send_faces(i, (XLO, XHI), pair)
        else:
            send_faces(i, (XLO,), pair)
        over_rows(body, half - 1, 1, half)
        if send_part is not None:
            send_part(0)
        if awaited is not None:
            wait_last(awaited, (1,))
            body(nx - 1)
            send_faces(i, (XHI,), pair)
        over_rows(body, half - 1, half, nx - 1)
        send_faces(i, (YLO, YHI), pair)
        if send_part is not None:
            send_part(1)

    def put_faces(i, t, x, value):
        ysend[i][0, t, pl.ds(x, 1), :] = value[0:1, :]
        ysend[i][1, t, pl.ds(x, 1), :] = value[ny - 1:ny, :]

    def put(i, t, x, value):
        fields[i][t, x + 1] = value
        put_faces(i, t, x, value)

    loads[0].wait()
    loads[1].wait()

    def pack(x):
        put_faces(KAPPA, 0, x, fields[KAPPA][0, x + 1])
        for t in range(steps):
            put_faces(INIT, t, x, fields[INIT][t, x + 1])

    over_rows(pack)
    send_faces(KAPPA, (YLO, YHI))
    send_faces(INIT, (YLO, YHI))

    @pl.when(sx == 0)
    def _():
        for i in range(FIELDS):
            for t in range(fields[i].shape[0]):
                fields[i][t, 0] = jnp.zeros((ny, nz), jnp.float32)

    @pl.when(sx == n_sx - 1)
    def _():
        for i in range(FIELDS):
            for t in range(fields[i].shape[0]):
                fields[i][t, nx + 1] = jnp.zeros((ny, nz), jnp.float32)

    @pl.when(sy == 0)
    def _():
        for i in range(FIELDS):
            yrecv[i][0] = jnp.zeros(yrecv[i].shape[1:], jnp.float32)

    @pl.when(sy == n_sy - 1)
    def _():
        for i in range(FIELDS):
            yrecv[i][1] = jnp.zeros(yrecv[i].shape[1:], jnp.float32)

    @pl.when(tm == 0)
    def _():
        def clear(x):
            for i in range(7):
                before[i, x] = jnp.zeros((ny, nz), jnp.float32)

        over_rows(clear, 1)

    row = lax.broadcasted_iota(jnp.int32, (ny, nz), 0)
    column = lax.broadcasted_iota(jnp.int32, (ny, nz), 1)

    def around(i, t, x):
        field = fields[i]
        here = field[t, x + 1]
        return here, (
            field[t, x + 2],
            field[t, x],
            jnp.where(row == ny - 1, yrecv[i][1, t, pl.ds(x, 1), :], pltpu.roll(here, ny - 1, 0)),
            jnp.where(row == 0, yrecv[i][0, t, pl.ds(x, 1), :], pltpu.roll(here, 1, 0)),
            pltpu.roll(here, nz - 1, 1),
            pltpu.roll(here, 1, 1),
        )

    def beside(i, t, x, g):
        here, sides = around(i, t, x)
        terms = [g[j] * sides[j] for j in range(6)]
        return here, (terms[0] + terms[1]) + (terms[2] + terms[3]) + (terms[4] + terms[5])

    def faces_at(x):
        return [face[j, x] for j in range(6)]

    wait_faces(KAPPA)

    def coefficients(x):
        here, sides = around(KAPPA, 0, x)
        sides = list(sides)
        sides[4] = jnp.where(column == nz - 1, 0.0, sides[4])
        sides[5] = jnp.where(column == 0, 0.0, sides[5])
        g = [0.5 * (here + side) for side in sides]
        total = (g[0] + g[1]) + (g[2] + g[3]) + (g[4] + g[5])
        coupling[x] = total
        g[4] = jnp.where(column == nz - 1, 0.0, g[4])
        g[5] = jnp.where(column == 0, 0.0, g[5])
        for j in range(6):
            face[j, x] = g[j]
        for level in range(4):
            factor[level, x] = relax_weight / (1.0 + (2.0 ** level) * total)

    over_rows(coefficients)
    loads[2].wait()
    wait_faces(INIT)

    def sweep_first(x):
        g, f = faces_at(x), factor[0, x]
        running = before[P_INIT, x]
        for t in range(steps):
            here, near = beside(INIT, t, x, g)
            running = keep_weight * here + f * (hs[t, x] + near + running)
            put(FIRST, t, x, running)

    phase(sweep_first, FIRST, functools.partial(send_last, P_FIRST), awaited=P_INIT)
    wait_faces(FIRST)

    def down_one(x):
        g, diagonal, f = faces_at(x), 1.0 + coupling[x], factor[1, x]
        earlier = before[P_FIRST, x]
        running = None
        for m in range(steps // 2):
            total = None
            for t in (2 * m, 2 * m + 1):
                here, near = beside(FIRST, t, x, g)
                value = hs[t, x] + earlier - (diagonal * here - near)
                total = value if total is None else total + value
                earlier = here
            rhs1[m, x] = total
            running = f * total if running is None else f * (total + running)
            put(ERR1, m, x, running)

    phase(down_one, ERR1, functools.partial(send_last, P_ERR1), awaited=P_FIRST)
    wait_faces(ERR1)
    wait_last(P_ERR1)

    def down_two(x):
        g, diagonal, f = faces_at(x), 1.0 + 2.0 * coupling[x], factor[2, x]
        earlier = before[P_ERR1, x]
        total = None
        for t in range(2):
            here, near = beside(ERR1, t, x, g)
            value = rhs1[t, x] + earlier - (diagonal * here - 2.0 * near)
            total = value if total is None else total + value
            earlier = here
        rhs2[x] = total
        put(ERR2, 0, x, f * total)

    phase(down_two, ERR2, functools.partial(send_last, P_ERR2))
    wait_faces(ERR2)
    if n_tm > 2:
        wait_last(P_ERR2)

    def down_three(x):
        g, diagonal = faces_at(x), 1.0 + 4.0 * coupling[x]
        here, near = beside(ERR2, 0, x, g)
        earlier = here + before[P_ERR2, x] if n_tm > 2 else here
        value = rhs2[x] + jnp.where(even, earlier, 0.0) - (diagonal * here - 4.0 * near)
        mine[x] = value
        if n_tm == 2:
            put(PART, 0, x, factor[3, x] * value)

    def swap(part):
        return pltpu.make_async_remote_copy(
            src_ref=mine.at[halves[part]], dst_ref=theirs.at[halves[part]],
            send_sem=qsend.at[part], recv_sem=qrecv.at[part],
            device_id={"tm": partner}, device_id_type=MESH)

    if n_tm == 2:
        phase(down_three, PART, lambda part: swap(part).start(), True)
        wait_faces(PART)

        def part_two(x):
            here, near = beside(PART, 0, x, faces_at(x))
            put(PART2, 0, x, keep_weight * here + factor[3, x] * (mine[x] + 8.0 * near))

        phase(part_two, PART2, None, True)
    else:
        over_rows(down_three)
        swap(0).start()
        swap(1).start()
    swap(0).wait_recv()
    swap(1).wait_recv()

    def chain_copy(i, field):
        src = field.at[0, pl.ds(1, nx)] if i == 0 else second
        return pltpu.make_async_remote_copy(
            src_ref=src, dst_ref=chain.at[i], send_sem=csend.at[i],
            recv_sem=crecv.at[i], device_id={"tm": tm + 2}, device_id_type=MESH)

    def chain_wait(i):
        if n_tm > 2:
            @pl.when(tm > 1)
            def _():
                chain_copy(i, fields[ERR3]).wait_recv()

            @pl.when(tm < 2)
            def _():
                def clear(x):
                    chain[i, x] = jnp.zeros((ny, nz), jnp.float32)

                over_rows(clear, 1)

    def chain_send(i):
        if n_tm > 2:
            @pl.when(tm < n_tm - 2)
            def _():
                chain_copy(i, fields[ERR3]).start()

    chain_wait(0)

    def coarse_one(x):
        total = mine[x] + theirs[x]
        rhs3[x] = total
        if n_tm > 2:
            total = total + chain[0, x]
        value = factor[3, x] * total
        if n_tm > 2:
            put(ERR3, 0, x, value)
        else:
            fields[ERR3][0, x + 1] = value

    if n_tm > 2:
        phase(coarse_one, ERR3)
        chain_send(0)
        wait_faces(ERR3)
    else:
        over_rows(coarse_one)
        wait_faces(PART, True)
        for edge in (0, nx + 1):
            fields[ERR3][0, edge] = fields[PART][0, edge] + fields[PAIR][0, edge]
        for edge in range(2):
            yrecv[ERR3][edge, 0] = yrecv[PART][edge, 0] + yrecv[PAIR][edge, 0]
    if n_tm == 2:
        wait_last(P_ERR2)
    chain_wait(1)

    def coarse_two(x):
        here, near = beside(ERR3, 0, x, faces_at(x))
        total = rhs3[x] + 8.0 * near
        if n_tm > 2:
            total = total + chain[1, x]
        value = keep_weight * here + factor[3, x] * total
        if n_tm > 2:
            second[x] = value
            earlier = jnp.where(even, chain[1, x], value)
        else:
            earlier = jnp.where(even, 0.0, value)
        mine_next[x] = before[P_ERR2, x] + earlier
        value = fields[ERR2][0, x + 1] + value
        if n_tm > 2:
            put(FIX2, 0, x, value)
        else:
            fields[FIX2][0, x + 1] = value

    mine_next = res.at[0]
    if n_tm > 2:
        phase(coarse_two, FIX2)
        chain_send(1)
        wait_faces(FIX2)
    else:
        over_rows(coarse_two)
        wait_faces(PART2)
        wait_faces(PART2, True)
        for edge in (0, nx + 1):
            fields[FIX2][0, edge] = fields[ERR2][0, edge] + (
                fields[PART2][0, edge] + fields[PAIR2][0, edge])
        for edge in range(2):
            yrecv[FIX2][edge, 0] = yrecv[ERR2][edge, 0] + (
                yrecv[PART2][edge, 0] + yrecv[PAIR2][edge, 0])

    def up_two(x):
        here, near = beside(FIX2, 0, x, faces_at(x))
        value = keep_weight * here + factor[2, x] * (rhs2[x] + 4.0 * near + mine_next[x])
        for m in range(2):
            put(FIX1, m, x, fields[ERR1][m, x + 1] + value)

    phase(up_two, FIX1, functools.partial(send_last, P_FIX1))
    wait_faces(FIX1)

    def up_one(x):
        g, f = faces_at(x), factor[1, x]
        running = before[P_FIX1, x]
        for m in range(2):
            here, near = beside(FIX1, m, x, g)
            running = keep_weight * here + f * (rhs1[m, x] + 2.0 * near + running)
            for t in (2 * m, 2 * m + 1):
                put(SUM0, t, x, fields[FIRST][t, x + 1] + running)

    phase(up_one, SUM0, functools.partial(send_last, P_SUM0), awaited=P_FIX1)
    wait_faces(SUM0)
    wait_last(P_SUM0)

    def up_zero(x):
        g, f = faces_at(x), factor[0, x]
        running = before[P_SUM0, x]
        for t in range(steps):
            here, near = beside(SUM0, t, x, g)
            running = keep_weight * here + f * (hs[t, x] + near + running)
            put(SOL, t, x, running)
            sol_hbm[t, x] = running

    phase(up_zero, SOL, functools.partial(send_last, P_SOL))
    wait_faces(SOL)
    wait_last(P_SOL)

    def last_defect(x):
        g, diagonal = faces_at(x), 1.0 + coupling[x]
        earlier = before[P_SOL, x]
        for t in range(steps):
            here, near = beside(SOL, t, x, g)
            res_hbm[t, x] = hs[t, x] + earlier - (diagonal * here - near)
            earlier = here

    over_rows(last_defect)

    for i in range(FIELDS):
        if i in ((PAIR, PAIR2, ERR3, FIX2) if n_tm == 2 else (PART, PAIR, PART2, PAIR2)):
            continue
        for side in (XLO, XHI, YLO, YHI):
            @pl.when(has[side])
            def _(i=i, side=side):
                face_copy(i, side).wait_send()
                if i in (PART, PART2):
                    face_copy(i, side, True).wait_send()

    @pl.when(tm < n_tm - 1)
    def _():
        for i in range(7):
            for part in range(2):
                last_copy(i, part).wait_send()

    swap(0).wait_send()
    swap(1).wait_send()
    if n_tm > 2:
        @pl.when(tm < n_tm - 2)
        def _():
            for i in range(2):
                chain_copy(i, fields[ERR3]).wait_send()


DEPTH = 6
EDGE = 8
REACH = 4
EXCHANGES = {
    "kappa": ("k", (0, 1), ()),
    "kappa_far": ("k", (1, 6), ((0, 5, 0, 5),)),
    "init": ("in", (0, 1), ()),
    "source": ("hs", (0, 1), ()),
    "first": ("first", (0, 1), ()),
    "first_far": ("first", (1, 2), ((0, 1, 0, 1),)),
    "pair": ("pair", (0, 2), ((0, 1, 0, 1),)),
    "err": ("err", (0, 5), ((0, 4, 0, 4),)),
    "last": ("last", (0, 5), ((0, 4, 0, 4),)),
    "prev_one": ("prev", (0, 5), ((0, 4, 0, 4),)),
    "prev_zero": ("prev", (0, 5), ((0, 4, 0, 4),)),
    "rhs3": ("rhs3", (0, 5), ((0, 4, 0, 4),)),
}
NAMES = tuple(EXCHANGES)
X_FACES = ((-1, 0), (1, 0))
REST = ((0, -1), (0, 1), (-1, -1), (-1, 1), (1, -1), (1, 1))
ALL = X_FACES + REST
T_INIT, T_LAST, T_ONE, T_ZERO, T_MINE, T_GUESS = range(6)


def wide_kernel(n_sx, n_sy, hs_hbm, k_hbm, in_hbm, sol_out, res_out,
                kap, ini, src, first, pair, err, last, prev, sums, fr, rhs3, one, err3, wave,
                err2, fix, vee, total, sol, face, coupling, factor,
                before, mine, theirs, guess, ahead,
                send_sem, recv_sem, tsend, trecv, local):
    nx, ny, nz = k_hbm.shape
    steps = in_hbm.shape[0]
    wide = ny + 2 * EDGE
    tm, sx, sy = lax.axis_index("tm"), lax.axis_index("sx"), lax.axis_index("sy")
    at_one = jnp.where(tm > 0, 1.0, 0.0)
    at_zero = 1.0 - at_one
    mid = pl.ds(EDGE, ny)
    win = pl.ds(EDGE - REACH, ny + 2 * REACH)
    inner = pl.ds(DEPTH, nx)
    homes = {"k": kap, "in": ini, "hs": src, "first": first, "pair": pair, "err": err,
             "last": last, "prev": prev, "rhs3": rhs3}
    outside = {"k": k_hbm, "in": in_hbm, "hs": hs_hbm}

    loads = [
        pltpu.make_async_copy(k_hbm, kap.at[0, inner, mid], local.at[0]),
        pltpu.make_async_copy(in_hbm, ini.at[:, inner, mid], local.at[1]),
        pltpu.make_async_copy(hs_hbm, src.at[:, inner, mid], local.at[2]),
    ]
    for load in loads:
        load.start()

    def there(way, sign=1):
        ok = None
        for step, at, size in ((sign * way[0], sx, n_sx), (sign * way[1], sy, n_sy)):
            if step:
                here = at > 0 if step < 0 else at < size - 1
                ok = here if ok is None else jnp.logical_and(ok, here)
        return ok

    def target(way):
        device = {}
        if way[0]:
            device["sx"] = sx + way[0]
        if way[1]:
            device["sy"] = sy + way[1]
        return device

    barrier = pltpu.get_barrier_semaphore()
    count = jnp.int32(1)
    for way in ALL:
        count = count + jnp.where(there(way), 1, 0)

        @pl.when(there(way))
        def _(way=way):
            pl.semaphore_signal(barrier, inc=1, device_id=target(way), device_id_type=MESH)

    pl.semaphore_signal(barrier, inc=1, device_id={"tm": 1 - tm}, device_id_type=MESH)

    def rows(body, depth, by=None):
        def step(x, carry):
            body(x)
            return carry

        if by is None:
            by = (nx + 2 * depth) // (2 if depth else 1)
        lax.fori_loop(DEPTH - depth, DEPTH + nx + depth, step, 0, unroll=by)

    filled = ((kap, 6), (ini, 1), (src, 1), (first, 2), (pair, 2), (err, 5), (last, 5), (prev, 5), (rhs3, 5))
    plane = jnp.zeros((wide, nz), jnp.float32)
    strip = jnp.zeros((EDGE, nz), jnp.float32)

    def fill(edge_rows):
        for array, depth in filled:
            for t in range(array.shape[0]):
                for i in range(depth):
                    array[t, DEPTH - 1 - i if edge_rows < 0 else DEPTH + nx + i] = plane

    def fill_side(start):
        for array, depth in filled:
            def body(x):
                for t in range(array.shape[0]):
                    array[t, x, pl.ds(start, EDGE), :] = strip

            rows(body, depth, 2)

    @pl.when(sx == 0)
    def _():
        fill(-1)

    @pl.when(sx == n_sx - 1)
    def _():
        fill(1)

    @pl.when(sy == 0)
    def _():
        fill_side(0)

    @pl.when(sy == n_sy - 1)
    def _():
        fill_side(EDGE + ny)

    @pl.when(tm == 0)
    def _():
        def body(x):
            last[0, x] = plane
            prev[0, x] = plane
            prev[1, x] = plane

        rows(body, 5, 2)

        def empty(x):
            before[x - DEPTH] = jnp.zeros((ny, nz), jnp.float32)
            ahead[x - DEPTH] = jnp.zeros((ny, nz), jnp.float32)

        rows(empty, 0, 2)

    pl.semaphore_wait(barrier, count)

    def span(step, size, low, high):
        if step == 0:
            return 0, size, 0
        if step < 0:
            return low, high - low, size + low
        return size - high, high - low, -high

    def pieces(name, ways):
        kind, (low, high), corners = EXCHANGES[name]
        slot = 0
        for way in ALL:
            boxes = corners if way[0] and way[1] else ((low, high, low, high),)
            for box in boxes:
                if way in ways:
                    yield way, box, slot
                slot += 1

    def copy_of(name, way, box, slot):
        kind = EXCHANGES[name][0]
        land = homes[kind]
        fx, wx, tx = span(way[0], nx, box[0], box[1])
        fy, wy, ty = span(way[1], ny, box[2], box[3])
        steps_at = {"prev_zero": pl.ds(0, 1), "prev_one": pl.ds(1, 1)}.get(name, slice(None))
        if kind == "k":
            source = k_hbm.at[pl.ds(fx, wx), pl.ds(fy, wy)]
            dest = land.at[0, pl.ds(DEPTH + tx, wx), pl.ds(EDGE + ty, wy)]
        else:
            if kind in outside:
                source = outside[kind].at[:, pl.ds(fx, wx), pl.ds(fy, wy)]
            else:
                source = land.at[steps_at, pl.ds(DEPTH + fx, wx), pl.ds(EDGE + fy, wy)]
            dest = land.at[steps_at, pl.ds(DEPTH + tx, wx), pl.ds(EDGE + ty, wy)]
        number = NAMES.index(name)
        return pltpu.make_async_remote_copy(
            src_ref=source, dst_ref=dest, send_sem=send_sem.at[number, slot],
            recv_sem=recv_sem.at[number, slot], device_id=target(way), device_id_type=MESH)

    def send(name, ways=ALL):
        for way, box, slot in pieces(name, ways):
            @pl.when(there(way))
            def _(way=way, box=box, slot=slot):
                copy_of(name, way, box, slot).start()

    def wait(name):
        for way, box, slot in pieces(name, REST + X_FACES):
            @pl.when(there(way, -1))
            def _(way=way, box=box, slot=slot):
                copy_of(name, way, box, slot).wait_recv()

    def wait_sent(name):
        for way, box, slot in pieces(name, ALL):
            @pl.when(there(way))
            def _(way=way, box=box, slot=slot):
                copy_of(name, way, box, slot).wait_send()

    half = nx // 2
    ends = ((0, half), (half, nx - half))

    def across(which, part):
        low, size = ends[part]
        near, far = pl.ds(low, size), pl.ds(DEPTH + low, size)
        source, dest = {
            T_INIT: lambda: (in_hbm.at[steps - 1, near], before.at[near]),
            T_LAST: lambda: (first.at[steps - 1, far, mid], last.at[0, far, mid]),
            T_ONE: lambda: (err.at[1, far, mid], prev.at[1, far, mid]),
            T_ZERO: lambda: (err.at[0, far, mid], prev.at[0, far, mid]),
            T_MINE: lambda: (mine.at[near], theirs.at[near]),
            T_GUESS: lambda: (guess.at[near], ahead.at[near]),
        }[which]()
        return pltpu.make_async_remote_copy(
            src_ref=source, dst_ref=dest, send_sem=tsend.at[which, part],
            recv_sem=trecv.at[which, part], device_id={"tm": 1 - tm}, device_id_type=MESH)

    def pass_on(which, parts=(0, 1)):
        @pl.when(tm == 0)
        def _():
            for part in parts:
                across(which, part).start()

    def arrive(which, parts=(0, 1)):
        @pl.when(tm > 0)
        def _():
            for part in parts:
                across(which, part).wait_recv()

    send("kappa")
    send("init")
    pass_on(T_INIT)
    send("source")
    send("kappa_far")

    column = lax.broadcasted_iota(jnp.int32, (wide, nz), 1)
    height = lax.broadcasted_iota(jnp.int32, (wide, nz), 0)
    low_side = jnp.where(sy == 0, EDGE, 0)
    high_side = jnp.where(sy == n_sy - 1, EDGE + ny, wide)
    within = jnp.logical_and(height >= low_side, height < high_side)
    low_row = jnp.where(sx == 0, DEPTH, 0)
    high_row = jnp.where(sx == n_sx - 1, DEPTH + nx, nx + 2 * DEPTH)

    def around(ref, t, x):
        here = ref[t, x]
        return here, (
            ref[t, x + 1], ref[t, x - 1],
            pltpu.roll(here, wide - 1, 0), pltpu.roll(here, 1, 0),
            pltpu.roll(here, nz - 1, 1), pltpu.roll(here, 1, 1),
        )

    def around_part(ref, t, x, size):
        low = EDGE - (size - ny) // 2
        part = pl.ds(low, size)
        here = ref[t, x, part, :]
        return here, (
            ref[t, x + 1, part, :], ref[t, x - 1, part, :],
            ref[t, x, pl.ds(low + 1, size), :], ref[t, x, pl.ds(low - 1, size), :],
            pltpu.roll(here, nz - 1, 1), pltpu.roll(here, 1, 1),
        )

    def beside(ref, t, x, g):
        here, sides = around_part(ref, t, x, g[0].shape[0])
        terms = [g[j] * sides[j] for j in range(6)]
        return here, (terms[0] + terms[1]) + (terms[2] + terms[3]) + (terms[4] + terms[5])

    def faces(x):
        return [face[j, x, win, :] for j in range(6)]

    def faces_mid(x):
        return [face[j, x, mid, :] for j in range(6)]

    def couple(here, sides, col):
        sides = list(sides)
        top, bottom = col == nz - 1, col == 0
        sides[4] = jnp.where(top, 0.0, sides[4])
        sides[5] = jnp.where(bottom, 0.0, sides[5])
        g = [0.5 * (here + side) for side in sides]
        whole = (g[0] + g[1]) + (g[2] + g[3]) + (g[4] + g[5])
        g[4] = jnp.where(top, 0.0, g[4])
        g[5] = jnp.where(bottom, 0.0, g[5])
        return g, whole

    def coefficients_mid(x):
        g, whole = couple(*around_part(kap, 0, x, ny), column[:ny])
        coupling[x, mid, :] = whole
        for j in range(6):
            face[j, x, mid, :] = g[j]
        for level in range(2):
            factor[level, x, mid, :] = relax_weight / (1.0 + (2.0 ** level) * whole)

    def coefficients(x):
        g, whole = couple(*around(kap, 0, x), column)
        coupling[x] = whole
        inside = jnp.logical_and(within, jnp.logical_and(x >= low_row, x < high_row))
        for j in range(6):
            face[j, x] = g[j]
        for level in range(4):
            factor[level, x] = jnp.where(inside, relax_weight / (1.0 + (2.0 ** level) * whole), 0.0)

    def phase(body, edge, name):
        for i in range(edge):
            body(DEPTH + i)
            body(DEPTH + nx - 1 - i)
        send(name, X_FACES)

        def step(x, carry):
            body(x)
            return carry

        lax.fori_loop(DEPTH + edge, DEPTH + nx - edge, step, 0, unroll=nx // 2 - edge)
        send(name, REST)

    loads[0].wait()
    wait("kappa")
    rows(coefficients_mid, 0)
    loads[1].wait()
    loads[2].wait()
    wait("init")
    arrive(T_INIT)

    def sweep_first(x):
        g, f = faces_mid(x), factor[0, x, mid, :]
        running = before[x - DEPTH]
        for t in range(steps):
            here, near = beside(ini, t, x, g)
            running = keep_weight * here + f * (src[t, x, mid, :] + near + running)
            first[t, x, mid, :] = running

    phase(sweep_first, 1, "first")
    pass_on(T_LAST)
    wait("kappa_far")
    rows(coefficients, 5)
    send("first_far")
    wait("first")

    def down_one(x):
        g, f, c = faces_mid(x), factor[0, x, mid, :], coupling[x, mid, :]
        f_one = factor[1, x, mid, :]
        diagonal = 1.0 + c
        earlier = None
        ahead_value = None
        running = None
        pair_zero = None
        for m in range(2):
            both = None
            for t in (2 * m, 2 * m + 1):
                here, near = beside(first, t, x, g)
                supply = src[t, x, mid, :] + near
                value = supply - diagonal * here
                if earlier is not None:
                    value = value + earlier
                both = value if both is None else both + value
                ahead_value = keep_weight * here + f * (supply if ahead_value is None else supply + ahead_value)
                earlier = here
            running = f_one * both if running is None else f_one * (both + running)
            err[m, x, mid, :] = running
            pair_zero = running if m == 0 else pair_zero
        both = pair_zero + running
        pair[1, x, mid, :] = both
        pair[0, x, mid, :] = both + at_zero * ((f_one + f_one * f_one) * earlier)
        pair[2, x, mid, :] = at_zero * running
        guess[x - DEPTH] = ahead_value

    phase(down_one, 2, "pair")
    pass_on(T_ONE)
    pass_on(T_ZERO)
    send("err")
    arrive(T_LAST)

    @pl.when(tm > 0)
    def _():
        send("last")

    wait("pair")

    def down_two(x):
        here, near = beside(pair, 0, x, faces(x))
        value = 0.25 * (1.0 + 2.0 * coupling[x, win, :]) * here + 2.0 * near + pair[2, x, win, :]
        fr[0, x, win, :] = factor[2, x, win, :] * value

    rows(down_two, 1)

    def down_three(x):
        g, c = faces_mid(x), coupling[x, mid, :]
        here, near = beside(fr, 0, x, g)
        value = 0.25 * (1.0 + 4.0 * c) * here + 4.0 * near
        here, near = beside(pair, 1, x, g)
        base = factor[2, x, mid, :] * (0.25 * (1.0 + 2.0 * c) * here + 2.0 * near)
        mine[x - DEPTH] = value + at_zero * base

    rows(down_three, 0)
    across(T_MINE, 0).start()
    across(T_MINE, 1).start()
    pass_on(T_GUESS)
    arrive(T_ONE)

    @pl.when(tm > 0)
    def _():
        send("prev_one")

    arrive(T_ZERO)

    @pl.when(tm > 0)
    def _():
        send("prev_zero")

    across(T_MINE, 0).wait_recv()
    across(T_MINE, 1).wait_recv()

    def add_up(x):
        rhs3[0, x, mid, :] = mine[x - DEPTH] + theirs[x - DEPTH]

    rows(add_up, 0)
    send("rhs3")

    wait("err")
    wait("first_far")

    @pl.when(tm > 0)
    def _():
        wait("last")
        wait("prev_one")
        wait("prev_zero")

    def gather_far(x):
        f = factor[1, x]
        sums[0, x] = err[0, x] + err[1, x] + (f + f * f) * last[0, x]
        sums[1, x] = prev[0, x] + prev[1, x]

    rows(gather_far, 5)

    def level_two(x):
        g, f, weight = faces(x), factor[2, x, win, :], 0.25 * (1.0 + 2.0 * coupling[x, win, :])
        here, near = beside(sums, 0, x, g)
        err2[0, x, win, :] = f * (weight * here + 2.0 * near + prev[1, x, win, :])
        here, near = beside(sums, 1, x, g)
        err2[1, x, win, :] = f * (weight * here + 2.0 * near)

    rows(level_two, 4)

    def own_errors(x):
        f = factor[1, x, win, :]
        carried = f * last[0, x, win, :]
        return err[0, x, win, :] + carried, err[1, x, win, :] + f * carried

    def fix_two(x):
        g, f = faces(x), factor[2, x, win, :]
        own, near = beside(err2, 0, x, g)
        past, near_past = beside(err2, 1, x, g)
        value = (2.0 - relax_weight) * own + f * (4.0 * near + past)
        value_past = (2.0 - relax_weight) * past + 4.0 * (f * near_past)
        zero, first_one = own_errors(x)
        fix[0, x, win, :] = zero + value
        fix[1, x, win, :] = first_one + value
        fix[2, x, win, :] = prev[0, x, win, :] + value_past
        fix[3, x, win, :] = prev[1, x, win, :] + value_past

    rows(fix_two, 3)

    def fix_one(x):
        g, f = faces(x), factor[1, x, win, :]
        here, near = [], []
        for i in range(4):
            a, b = beside(fix, i, x, g)
            here.append(a)
            near.append(keep_weight * a + 2.0 * (f * b))
        zero, first_one = own_errors(x)
        value = near[0] + zero + f * here[3]
        vee[0, x, win, :] = value
        vee[1, x, win, :] = near[1] + first_one + f * (value - zero)
        value = near[2] + prev[0, x, win, :]
        vee[2, x, win, :] = value
        vee[3, x, win, :] = near[3] + prev[1, x, win, :] + f * (value - prev[0, x, win, :])

    rows(fix_one, 2)
    wait("rhs3")

    def coarse_one(x):
        one[0, x] = factor[3, x] * rhs3[0, x]

    rows(coarse_one, 5)

    def coarse_two(x):
        here, near = beside(one, 0, x, faces(x))
        err3[0, x, win, :] = keep_weight * here + factor[3, x, win, :] * (rhs3[0, x, win, :] + 8.0 * near)

    rows(coarse_two, 4)

    def up_two(x):
        f = factor[2, x, win, :]
        here, near = beside(err3, 0, x, faces(x))
        value = keep_weight * here + 4.0 * (f * near)
        wave[0, x, win, :] = value + at_one * (f * here)
        wave[1, x, win, :] = value

    rows(up_two, 3)

    def up_one(x):
        g, f = faces(x), factor[1, x, win, :]
        here, near = beside(wave, 0, x, g)
        past, near_past = beside(wave, 1, x, g)
        own = keep_weight * here + 2.0 * (f * near)
        shadow = at_one * (keep_weight * past + 2.0 * (f * near_past))
        zero = own + at_one * (f * past)
        gain = (vee[0, x, win, :] + zero, vee[1, x, win, :] + own + f * zero)
        for t in range(steps):
            total[t, x, win, :] = first[t, x, win, :] + gain[t // 2]
        vee[2, x, win, :] = vee[2, x, win, :] + shadow
        vee[3, x, win, :] = vee[3, x, win, :] + shadow + f * shadow

    rows(up_one, 2)
    wait("source")

    def up_zero(x):
        g, f = faces(x), factor[0, x, win, :]
        running = last[0, x, win, :] + vee[3, x, win, :]
        for t in range(steps):
            here, near = beside(total, t, x, g)
            running = keep_weight * here + f * (src[t, x, win, :] + near + running)
            sol[t, x, win, :] = running

    rows(up_zero, 1)
    arrive(T_GUESS)

    def finish(x):
        g, f = faces_mid(x), factor[0, x, mid, :]
        diagonal = 1.0 + coupling[x, mid, :]
        lifted = []
        for i in (2, 3):
            here, near = beside(vee, i, x, g)
            lifted.append(keep_weight * here + f * near)
        earlier = ahead[x - DEPTH] + (1.0 + f) * (f * f * lifted[0] + lifted[1])
        for t in range(steps):
            here, near = beside(sol, t, x, g)
            sol_out[t, x - DEPTH] = here
            res_out[t, x - DEPTH] = src[t, x, mid, :] + earlier - (diagonal * here - near)
            earlier = here

    rows(finish, 0)

    for name in NAMES:
        if name in ("last", "prev_one", "prev_zero"):
            @pl.when(tm > 0)
            def _(name=name):
                wait_sent(name)
        else:
            wait_sent(name)

    @pl.when(tm == 0)
    def _():
        for which in (T_INIT, T_LAST, T_ONE, T_ZERO, T_GUESS):
            for part in range(2):
                across(which, part).wait_send()

    across(T_MINE, 0).wait_send()
    across(T_MINE, 1).wait_send()


def wide_scratch(steps, nx, ny, nz):
    f32, dma = jnp.float32, pltpu.SemaphoreType.DMA
    depths = (1, steps, steps, steps, 3, 2, 1, 2, 2, 1, 1, 1, 1, 2, 2, 4, 4, steps, steps, 6)
    large = (nx + 2 * DEPTH, ny + 2 * EDGE, nz)
    scratch = [pltpu.VMEM((d,) + large, f32) for d in depths]
    scratch += [pltpu.VMEM(large, f32), pltpu.VMEM((4,) + large, f32)]
    scratch += [pltpu.VMEM((nx, ny, nz), f32)] * 5
    scratch += [dma((len(NAMES), 12)), dma((len(NAMES), 12)), dma((6, 2)), dma((6, 2)), dma((3,))]
    return scratch


def store(one, two, one_hbm, two_hbm, sem):
    copies = [pltpu.make_async_copy(one, one_hbm, sem.at[0]), pltpu.make_async_copy(two, two_hbm, sem.at[1])]
    for copy in copies:
        copy.start()
    for copy in copies:
        copy.wait()


def solution(mesh):
    n_tm, n_sx, n_sy = (mesh.shape[axis] for axis in ("tm", "sx", "sy"))
    f32 = jnp.float32

    def per_device(heat_source, conductivity, initial_iterate):
        steps, nx, ny, nz = heat_source.shape
        depth = (1, steps, steps, steps // 2, 1, 1, 1, steps // 2, steps, steps, 1, 1, 1, 1)
        scratch = [pltpu.VMEM((d, nx + 2, ny, nz), f32) for d in depth]
        scratch += [pltpu.VMEM((2, d, nx, nz), f32) for d in depth] * 2
        cells = (nx, ny, nz)
        dma = pltpu.SemaphoreType.DMA
        scratch += [
            pltpu.VMEM((steps,) + cells, f32),
            pltpu.VMEM((steps,) + cells, f32),
            pltpu.VMEM((7,) + cells, f32),
            pltpu.VMEM(cells, f32),
            pltpu.VMEM((steps // 2,) + cells, f32),
            pltpu.VMEM(cells, f32),
            pltpu.VMEM(cells, f32),
            pltpu.VMEM(cells, f32),
            pltpu.VMEM(cells, f32),
            pltpu.VMEM((2,) + cells, f32),
            pltpu.VMEM((6,) + cells, f32),
            pltpu.VMEM(cells, f32),
            pltpu.VMEM((4,) + cells, f32),
            dma((FIELDS, 4)), dma((FIELDS, 4)), dma((7, 2)), dma((7, 2)),
            dma((2,)), dma((2,)), dma((2,)), dma((2,)), dma((5,)),
        ]
        field = jax.ShapeDtypeStruct(heat_source.shape, f32)
        small = n_tm == 2 and steps == 4 and nx >= DEPTH and ny >= EDGE and ny % EDGE == 0
        if small:
            scratch = wide_scratch(steps, nx, ny, nz)
        one, two = pl.pallas_call(
            functools.partial(wide_kernel, n_sx, n_sy) if small else functools.partial(kernel, n_tm, n_sx, n_sy),
            out_shape=(pltpu.VMEM(heat_source.shape, f32),) * 2,
            in_specs=[pl.BlockSpec(memory_space=pltpu.HBM)] * 3,
            out_specs=(pl.BlockSpec(memory_space=pltpu.VMEM),) * 2,
            scratch_shapes=scratch,
            compiler_params=pltpu.CompilerParams(
                collective_id=0, has_side_effects=True, vmem_limit_bytes=40000000
            ),
            name="vcycle",
        )(*(pltpu.with_memory_space_constraint(x, pltpu.HBM) for x in (heat_source, conductivity, initial_iterate)))
        return pl.pallas_call(
            store,
            out_shape=(field, field),
            in_specs=[pl.BlockSpec(memory_space=pltpu.VMEM)] * 2,
            out_specs=(pl.BlockSpec(memory_space=pltpu.HBM),) * 2,
            scratch_shapes=[dma((2,))],
            name="store",
        )(*(pltpu.with_memory_space_constraint(x, pltpu.VMEM) for x in (one, two)))

    placed = (P("tm", "sx", "sy", None), P("sx", "sy", None), P("tm", "sx", "sy", None))
    return jax.shard_map(
        per_device,
        mesh=mesh,
        in_specs=placed,
        out_specs=(P("tm", "sx", "sy", None), P("tm", "sx", "sy", None)),
        check_vma=False,
    )
```

```python
import functools

import jax
import jax.numpy as jnp
from jax import lax
from jax.experimental import pallas as pl
from jax.experimental.pallas import tpu as pltpu
from jax.sharding import PartitionSpec as P

relax_weight = 0.8
keep_weight = 1.0 - relax_weight
MESH = pl.DeviceIdType.MESH

KAPPA, INIT, FIRST, ERR1, ERR2, ERR3, FIX2, FIX1, SUM0, SOL, PART, PAIR, PART2, PAIR2 = range(14)
FIELDS = 14
P_INIT, P_FIRST, P_ERR1, P_ERR2, P_FIX1, P_SUM0, P_SOL = range(7)
XLO, XHI, YLO, YHI = range(4)


def kernel(n_tm, n_sx, n_sy, hs_hbm, k_hbm, in_hbm, sol_hbm, res_hbm, *scratch):
    fields = scratch[:FIELDS]
    yrecv = scratch[FIELDS:2 * FIELDS]
    ysend = scratch[2 * FIELDS:3 * FIELDS]
    (hs, res, before, second, rhs1, rhs2, rhs3, mine, theirs, chain,
     face, coupling, factor, send_sem, recv_sem, tsend, trecv,
     qsend, qrecv, csend, crecv, local) = scratch[3 * FIELDS:]
    steps, nx, ny, nz = hs.shape
    tm, sx, sy = lax.axis_index("tm"), lax.axis_index("sx"), lax.axis_index("sy")
    has = (sx > 0, sx < n_sx - 1, sy > 0, sy < n_sy - 1)
    partner = tm + 1 - 2 * lax.rem(tm, 2)
    even = lax.rem(tm, 2) == 0

    loads = [
        pltpu.make_async_copy(k_hbm, fields[KAPPA].at[0, pl.ds(1, nx)], local.at[0]),
        pltpu.make_async_copy(in_hbm, fields[INIT].at[:, pl.ds(1, nx)], local.at[1]),
        pltpu.make_async_copy(hs_hbm, hs, local.at[2]),
    ]
    for load in loads:
        load.start()

    barrier = pltpu.get_barrier_semaphore()
    greet = [
        (has[XLO], {"sx": sx - 1}), (has[XHI], {"sx": sx + 1}),
        (has[YLO], {"sy": sy - 1}), (has[YHI], {"sy": sy + 1}),
        (tm > 0, {"tm": tm - 1}), (tm < n_tm - 1, {"tm": tm + 1}),
    ]
    if n_tm == 2:
        greet += [
            (has[XLO], {"tm": partner, "sx": sx - 1}), (has[XHI], {"tm": partner, "sx": sx + 1}),
            (has[YLO], {"tm": partner, "sy": sy - 1}), (has[YHI], {"tm": partner, "sy": sy + 1}),
        ]
    if n_tm > 2:
        greet += [(tm > 1, {"tm": tm - 2}), (tm < n_tm - 2, {"tm": tm + 2})]
    count = jnp.int32(0)
    for there, device in greet:
        count = count + jnp.where(there, 1, 0)

        @pl.when(there)
        def _(device=device):
            pl.semaphore_signal(barrier, inc=1, device_id=device, device_id_type=MESH)

    pl.semaphore_wait(barrier, count)

    def face_copy(i, side, pair=False):
        field = fields[i]
        to = i + 1 if pair else i
        land = fields[to]
        if side == XLO:
            if i == INIT:
                src = in_hbm.at[:, pl.ds(0, 1)]
            elif i == KAPPA:
                src = k_hbm.at[pl.ds(0, 1)]
            else:
                src = field.at[:, pl.ds(1, 1)]
            dst, device = land.at[:, pl.ds(nx + 1, 1)], {"sx": sx - 1}
        elif side == XHI:
            if i == INIT:
                src = in_hbm.at[:, pl.ds(nx - 1, 1)]
            elif i == KAPPA:
                src = k_hbm.at[pl.ds(nx - 1, 1)]
            else:
                src = field.at[:, pl.ds(nx, 1)]
            dst, device = land.at[:, pl.ds(0, 1)], {"sx": sx + 1}
        elif side == YLO:
            src, dst, device = ysend[i].at[0], yrecv[to].at[1], {"sy": sy - 1}
        else:
            src, dst, device = ysend[i].at[1], yrecv[to].at[0], {"sy": sy + 1}
        if i == KAPPA and side in (XLO, XHI):
            dst = field.at[0, pl.ds(nx + 1 if side == XLO else 0, 1)]
        if pair:
            device["tm"] = partner
        return pltpu.make_async_remote_copy(
            src_ref=src, dst_ref=dst, send_sem=send_sem.at[to, side],
            recv_sem=recv_sem.at[to, side], device_id=device, device_id_type=MESH)

    def send_faces(i, sides, pair=False):
        for side in sides:
            @pl.when(has[side])
            def _(side=side):
                face_copy(i, side).start()
                if pair:
                    face_copy(i, side, True).start()

    def wait_faces(i, pair=False):
        for side in (YLO, YHI, XLO, XHI):
            @pl.when(has[side ^ 1])
            def _(side=side):
                face_copy(i, side, pair).wait_recv()

    half = nx // 2
    halves = (pl.ds(0, half), pl.ds(half, nx - half))

    def last_copy(i, part):
        field = fields[lasts[i]]
        if i == P_INIT:
            src = in_hbm.at[steps - 1, halves[part]]
        else:
            src = field.at[field.shape[0] - 1, (pl.ds(1, half), pl.ds(1 + half, nx - half))[part]]
        return pltpu.make_async_remote_copy(
            src_ref=src, dst_ref=before.at[i, halves[part]],
            send_sem=tsend.at[i, part], recv_sem=trecv.at[i, part],
            device_id={"tm": tm + 1}, device_id_type=MESH)

    lasts = (INIT, FIRST, ERR1, ERR2, FIX1, SUM0, SOL)

    def send_last(i, part):
        @pl.when(tm < n_tm - 1)
        def _():
            last_copy(i, part).start()

    def wait_last(i, parts=(0, 1)):
        @pl.when(tm > 0)
        def _():
            for part in parts:
                last_copy(i, part).wait_recv()

    send_faces(KAPPA, (XLO, XHI))
    send_faces(INIT, (XLO, XHI))
    send_last(P_INIT, 0)
    send_last(P_INIT, 1)

    def over_rows(body, by=8, start=0, stop=nx):
        def step(x, carry):
            body(x)
            return carry

        lax.fori_loop(start, stop, step, 0, unroll=by)

    def phase(body, i, send_part=None, pair=False, awaited=None):
        if awaited is not None:
            wait_last(awaited, (0,))
        body(0)
        if awaited is None:
            body(nx - 1)
            send_faces(i, (XLO, XHI), pair)
        else:
            send_faces(i, (XLO,), pair)
        over_rows(body, half - 1, 1, half)
        if send_part is not None:
            send_part(0)
        if awaited is not None:
            wait_last(awaited, (1,))
            body(nx - 1)
            send_faces(i, (XHI,), pair)
        over_rows(body, half - 1, half, nx - 1)
        send_faces(i, (YLO, YHI), pair)
        if send_part is not None:
            send_part(1)

    def put_faces(i, t, x, value):
        ysend[i][0, t, pl.ds(x, 1), :] = value[0:1, :]
        ysend[i][1, t, pl.ds(x, 1), :] = value[ny - 1:ny, :]

    def put(i, t, x, value):
        fields[i][t, x + 1] = value
        put_faces(i, t, x, value)

    loads[0].wait()
    loads[1].wait()

    def pack(x):
        put_faces(KAPPA, 0, x, fields[KAPPA][0, x + 1])
        for t in range(steps):
            put_faces(INIT, t, x, fields[INIT][t, x + 1])

    over_rows(pack)
    send_faces(KAPPA, (YLO, YHI))
    send_faces(INIT, (YLO, YHI))

    @pl.when(sx == 0)
    def _():
        for i in range(FIELDS):
            for t in range(fields[i].shape[0]):
                fields[i][t, 0] = jnp.zeros((ny, nz), jnp.float32)

    @pl.when(sx == n_sx - 1)
    def _():
        for i in range(FIELDS):
            for t in range(fields[i].shape[0]):
                fields[i][t, nx + 1] = jnp.zeros((ny, nz), jnp.float32)

    @pl.when(sy == 0)
    def _():
        for i in range(FIELDS):
            yrecv[i][0] = jnp.zeros(yrecv[i].shape[1:], jnp.float32)

    @pl.when(sy == n_sy - 1)
    def _():
        for i in range(FIELDS):
            yrecv[i][1] = jnp.zeros(yrecv[i].shape[1:], jnp.float32)

    @pl.when(tm == 0)
    def _():
        def clear(x):
            for i in range(7):
                before[i, x] = jnp.zeros((ny, nz), jnp.float32)

        over_rows(clear, 1)

    row = lax.broadcasted_iota(jnp.int32, (ny, nz), 0)
    column = lax.broadcasted_iota(jnp.int32, (ny, nz), 1)

    def around(i, t, x):
        field = fields[i]
        here = field[t, x + 1]
        return here, (
            field[t, x + 2],
            field[t, x],
            jnp.where(row == ny - 1, yrecv[i][1, t, pl.ds(x, 1), :], pltpu.roll(here, ny - 1, 0)),
            jnp.where(row == 0, yrecv[i][0, t, pl.ds(x, 1), :], pltpu.roll(here, 1, 0)),
            pltpu.roll(here, nz - 1, 1),
            pltpu.roll(here, 1, 1),
        )

    def beside(i, t, x, g):
        here, sides = around(i, t, x)
        terms = [g[j] * sides[j] for j in range(6)]
        return here, (terms[0] + terms[1]) + (terms[2] + terms[3]) + (terms[4] + terms[5])

    def faces_at(x):
        return [face[j, x] for j in range(6)]

    wait_faces(KAPPA)

    def coefficients(x):
        here, sides = around(KAPPA, 0, x)
        sides = list(sides)
        sides[4] = jnp.where(column == nz - 1, 0.0, sides[4])
        sides[5] = jnp.where(column == 0, 0.0, sides[5])
        g = [0.5 * (here + side) for side in sides]
        total = (g[0] + g[1]) + (g[2] + g[3]) + (g[4] + g[5])
        coupling[x] = total
        g[4] = jnp.where(column == nz - 1, 0.0, g[4])
        g[5] = jnp.where(column == 0, 0.0, g[5])
        for j in range(6):
            face[j, x] = g[j]
        for level in range(4):
            factor[level, x] = relax_weight / (1.0 + (2.0 ** level) * total)

    over_rows(coefficients)
    loads[2].wait()
    wait_faces(INIT)

    def sweep_first(x):
        g, f = faces_at(x), factor[0, x]
        running = before[P_INIT, x]
        for t in range(steps):
            here, near = beside(INIT, t, x, g)
            running = keep_weight * here + f * (hs[t, x] + near + running)
            put(FIRST, t, x, running)

    phase(sweep_first, FIRST, functools.partial(send_last, P_FIRST), awaited=P_INIT)
    wait_faces(FIRST)

    def down_one(x):
        g, diagonal, f = faces_at(x), 1.0 + coupling[x], factor[1, x]
        earlier = before[P_FIRST, x]
        running = None
        for m in range(steps // 2):
            total = None
            for t in (2 * m, 2 * m + 1):
                here, near = beside(FIRST, t, x, g)
                value = hs[t, x] + earlier - (diagonal * here - near)
                total = value if total is None else total + value
                earlier = here
            rhs1[m, x] = total
            running = f * total if running is None else f * (total + running)
            put(ERR1, m, x, running)

    phase(down_one, ERR1, functools.partial(send_last, P_ERR1), awaited=P_FIRST)
    wait_faces(ERR1)
    wait_last(P_ERR1)

    def down_two(x):
        g, diagonal, f = faces_at(x), 1.0 + 2.0 * coupling[x], factor[2, x]
        earlier = before[P_ERR1, x]
        total = None
        for t in range(2):
            here, near = beside(ERR1, t, x, g)
            value = rhs1[t, x] + earlier - (diagonal * here - 2.0 * near)
            total = value if total is None else total + value
            earlier = here
        rhs2[x] = total
        put(ERR2, 0, x, f * total)

    phase(down_two, ERR2, functools.partial(send_last, P_ERR2))
    wait_faces(ERR2)
    if n_tm > 2:
        wait_last(P_ERR2)

    def down_three(x):
        g, diagonal = faces_at(x), 1.0 + 4.0 * coupling[x]
        here, near = beside(ERR2, 0, x, g)
        earlier = here + before[P_ERR2, x] if n_tm > 2 else here
        value = rhs2[x] + jnp.where(even, earlier, 0.0) - (diagonal * here - 4.0 * near)
        mine[x] = value
        if n_tm == 2:
            put(PART, 0, x, factor[3, x] * value)

    def swap(part):
        return pltpu.make_async_remote_copy(
            src_ref=mine.at[halves[part]], dst_ref=theirs.at[halves[part]],
            send_sem=qsend.at[part], recv_sem=qrecv.at[part],
            device_id={"tm": partner}, device_id_type=MESH)

    if n_tm == 2:
        phase(down_three, PART, lambda part: swap(part).start(), True)
        wait_faces(PART)

        def part_two(x):
            here, near = beside(PART, 0, x, faces_at(x))
            put(PART2, 0, x, keep_weight * here + factor[3, x] * (mine[x] + 8.0 * near))

        phase(part_two, PART2, None, True)
    else:
        over_rows(down_three)
        swap(0).start()
        swap(1).start()
    swap(0).wait_recv()
    swap(1).wait_recv()

    def chain_copy(i, field):
        src = field.at[0, pl.ds(1, nx)] if i == 0 else second
        return pltpu.make_async_remote_copy(
            src_ref=src, dst_ref=chain.at[i], send_sem=csend.at[i],
            recv_sem=crecv.at[i], device_id={"tm": tm + 2}, device_id_type=MESH)

    def chain_wait(i):
        if n_tm > 2:
            @pl.when(tm > 1)
            def _():
                chain_copy(i, fields[ERR3]).wait_recv()

            @pl.when(tm < 2)
            def _():
                def clear(x):
                    chain[i, x] = jnp.zeros((ny, nz), jnp.float32)

                over_rows(clear, 1)

    def chain_send(i):
        if n_tm > 2:
            @pl.when(tm < n_tm - 2)
            def _():
                chain_copy(i, fields[ERR3]).start()

    chain_wait(0)

    def coarse_one(x):
        total = mine[x] + theirs[x]
        rhs3[x] = total
        if n_tm > 2:
            total = total + chain[0, x]
        value = factor[3, x] * total
        if n_tm > 2:
            put(ERR3, 0, x, value)
        else:
            fields[ERR3][0, x + 1] = value

    if n_tm > 2:
        phase(coarse_one, ERR3)
        chain_send(0)
        wait_faces(ERR3)
    else:
        over_rows(coarse_one)
        wait_faces(PART, True)
        for edge in (0, nx + 1):
            fields[ERR3][0, edge] = fields[PART][0, edge] + fields[PAIR][0, edge]
        for edge in range(2):
            yrecv[ERR3][edge, 0] = yrecv[PART][edge, 0] + yrecv[PAIR][edge, 0]
    if n_tm == 2:
        wait_last(P_ERR2)
    chain_wait(1)

    def coarse_two(x):
        here, near = beside(ERR3, 0, x, faces_at(x))
        total = rhs3[x] + 8.0 * near
        if n_tm > 2:
            total = total + chain[1, x]
        value = keep_weight * here + factor[3, x] * total
        if n_tm > 2:
            second[x] = value
            earlier = jnp.where(even, chain[1, x], value)
        else:
            earlier = jnp.where(even, 0.0, value)
        mine_next[x] = before[P_ERR2, x] + earlier
        value = fields[ERR2][0, x + 1] + value
        if n_tm > 2:
            put(FIX2, 0, x, value)
        else:
            fields[FIX2][0, x + 1] = value

    mine_next = res.at[0]
    if n_tm > 2:
        phase(coarse_two, FIX2)
        chain_send(1)
        wait_faces(FIX2)
    else:
        over_rows(coarse_two)
        wait_faces(PART2)
        wait_faces(PART2, True)
        for edge in (0, nx + 1):
            fields[FIX2][0, edge] = fields[ERR2][0, edge] + (
                fields[PART2][0, edge] + fields[PAIR2][0, edge])
        for edge in range(2):
            yrecv[FIX2][edge, 0] = yrecv[ERR2][edge, 0] + (
                yrecv[PART2][edge, 0] + yrecv[PAIR2][edge, 0])

    def up_two(x):
        here, near = beside(FIX2, 0, x, faces_at(x))
        value = keep_weight * here + factor[2, x] * (rhs2[x] + 4.0 * near + mine_next[x])
        for m in range(2):
            put(FIX1, m, x, fields[ERR1][m, x + 1] + value)

    phase(up_two, FIX1, functools.partial(send_last, P_FIX1))
    wait_faces(FIX1)

    def up_one(x):
        g, f = faces_at(x), factor[1, x]
        running = before[P_FIX1, x]
        for m in range(2):
            here, near = beside(FIX1, m, x, g)
            running = keep_weight * here + f * (rhs1[m, x] + 2.0 * near + running)
            for t in (2 * m, 2 * m + 1):
                put(SUM0, t, x, fields[FIRST][t, x + 1] + running)

    phase(up_one, SUM0, functools.partial(send_last, P_SUM0), awaited=P_FIX1)
    wait_faces(SUM0)
    wait_last(P_SUM0)

    def up_zero(x):
        g, f = faces_at(x), factor[0, x]
        running = before[P_SUM0, x]
        for t in range(steps):
            here, near = beside(SUM0, t, x, g)
            running = keep_weight * here + f * (hs[t, x] + near + running)
            put(SOL, t, x, running)
            sol_hbm[t, x] = running

    phase(up_zero, SOL, functools.partial(send_last, P_SOL))
    wait_faces(SOL)
    wait_last(P_SOL)

    def last_defect(x):
        g, diagonal = faces_at(x), 1.0 + coupling[x]
        earlier = before[P_SOL, x]
        for t in range(steps):
            here, near = beside(SOL, t, x, g)
            res_hbm[t, x] = hs[t, x] + earlier - (diagonal * here - near)
            earlier = here

    over_rows(last_defect)

    for i in range(FIELDS):
        if i in ((PAIR, PAIR2, ERR3, FIX2) if n_tm == 2 else (PART, PAIR, PART2, PAIR2)):
            continue
        for side in (XLO, XHI, YLO, YHI):
            @pl.when(has[side])
            def _(i=i, side=side):
                face_copy(i, side).wait_send()
                if i in (PART, PART2):
                    face_copy(i, side, True).wait_send()

    @pl.when(tm < n_tm - 1)
    def _():
        for i in range(7):
            for part in range(2):
                last_copy(i, part).wait_send()

    swap(0).wait_send()
    swap(1).wait_send()
    if n_tm > 2:
        @pl.when(tm < n_tm - 2)
        def _():
            for i in range(2):
                chain_copy(i, fields[ERR3]).wait_send()


DEPTH = 6
EDGE = 8
REACH = 4
EXCHANGES = {
    "kappa": ("k", (0, 1), ()),
    "kappa_far": ("k", (1, 6), ((0, 5, 0, 5),)),
    "init": ("in", (0, 1), ()),
    "source": ("hs", (0, 1), ()),
    "first": ("first", (0, 1), ()),
    "first_far": ("first", (1, 2), ((0, 1, 0, 1),)),
    "pair": ("pair", (0, 2), ((0, 1, 0, 1),)),
    "err": ("err", (0, 5), ((0, 4, 0, 4),)),
    "last": ("last", (0, 5), ((0, 4, 0, 4),)),
    "prev_one": ("prev", (0, 5), ((0, 4, 0, 4),)),
    "prev_zero": ("prev", (0, 5), ((0, 4, 0, 4),)),
    "rhs3": ("rhs3", (0, 5), ((0, 4, 0, 4),)),
}
NAMES = tuple(EXCHANGES)
X_FACES = ((-1, 0), (1, 0))
REST = ((0, -1), (0, 1), (-1, -1), (-1, 1), (1, -1), (1, 1))
ALL = X_FACES + REST
T_INIT, T_LAST, T_ONE, T_ZERO, T_MINE, T_GUESS = range(6)


def wide_kernel(n_sx, n_sy, hs_hbm, k_hbm, in_hbm, sol_out, res_out,
                kap, ini, src, first, pair, err, last, prev, sums, fr, rhs3, one, err3, wave,
                err2, fix, vee, total, sol, face, coupling, factor,
                before, mine, theirs, guess, ahead,
                send_sem, recv_sem, tsend, trecv, local):
    nx, ny, nz = k_hbm.shape
    steps = in_hbm.shape[0]
    wide = ny + 2 * EDGE
    tm, sx, sy = lax.axis_index("tm"), lax.axis_index("sx"), lax.axis_index("sy")
    at_one = jnp.where(tm > 0, 1.0, 0.0)
    at_zero = 1.0 - at_one
    mid = pl.ds(EDGE, ny)
    win = pl.ds(EDGE - REACH, ny + 2 * REACH)
    inner = pl.ds(DEPTH, nx)
    homes = {"k": kap, "in": ini, "hs": src, "first": first, "pair": pair, "err": err,
             "last": last, "prev": prev, "rhs3": rhs3}

    loads = [
        pltpu.make_async_copy(k_hbm, kap.at[0, inner, mid], local.at[0]),
        pltpu.make_async_copy(in_hbm, ini.at[:, inner, mid], local.at[1]),
        pltpu.make_async_copy(hs_hbm, src.at[:, inner, mid], local.at[2]),
    ]
    for load in loads:
        load.start()

    def there(way, sign=1):
        ok = None
        for step, at, size in ((sign * way[0], sx, n_sx), (sign * way[1], sy, n_sy)):
            if step:
                here = at > 0 if step < 0 else at < size - 1
                ok = here if ok is None else jnp.logical_and(ok, here)
        return ok

    def target(way):
        device = {}
        if way[0]:
            device["sx"] = sx + way[0]
        if way[1]:
            device["sy"] = sy + way[1]
        return device

    barrier = pltpu.get_barrier_semaphore()
    count = jnp.int32(1)
    for way in ALL:
        count = count + jnp.where(there(way), 1, 0)

        @pl.when(there(way))
        def _(way=way):
            pl.semaphore_signal(barrier, inc=1, device_id=target(way), device_id_type=MESH)

    pl.semaphore_signal(barrier, inc=1, device_id={"tm": 1 - tm}, device_id_type=MESH)

    def rows(body, depth, by=None):
        def step(x, carry):
            body(x)
            return carry

        if by is None:
            by = (nx + 2 * depth) // (2 if depth else 1)
        lax.fori_loop(DEPTH - depth, DEPTH + nx + depth, step, 0, unroll=by)

    filled = ((kap, 6), (ini, 1), (src, 1), (first, 2), (pair, 2), (err, 5), (last, 5), (prev, 5), (rhs3, 5))
    plane = jnp.zeros((wide, nz), jnp.float32)
    strip = jnp.zeros((EDGE, nz), jnp.float32)

    def fill(edge_rows):
        for array, depth in filled:
            for t in range(array.shape[0]):
                for i in range(depth):
                    array[t, DEPTH - 1 - i if edge_rows < 0 else DEPTH + nx + i] = plane

    def fill_side(start):
        for array, depth in filled:
            def body(x):
                for t in range(array.shape[0]):
                    array[t, x, pl.ds(start, EDGE), :] = strip

            rows(body, depth, 2)

    @pl.when(sx == 0)
    def _():
        fill(-1)

    @pl.when(sx == n_sx - 1)
    def _():
        fill(1)

    @pl.when(sy == 0)
    def _():
        fill_side(0)

    @pl.when(sy == n_sy - 1)
    def _():
        fill_side(EDGE + ny)

    @pl.when(tm == 0)
    def _():
        def body(x):
            last[0, x] = plane
            prev[0, x] = plane
            prev[1, x] = plane

        rows(body, 5, 2)

        def empty(x):
            before[x - DEPTH] = jnp.zeros((ny, nz), jnp.float32)
            ahead[x - DEPTH] = jnp.zeros((ny, nz), jnp.float32)

        rows(empty, 0, 2)

    pl.semaphore_wait(barrier, count)

    def span(step, size, low, high):
        if step == 0:
            return 0, size, 0
        if step < 0:
            return low, high - low, size + low
        return size - high, high - low, -high

    def pieces(name, ways):
        kind, (low, high), corners = EXCHANGES[name]
        slot = 0
        for way in ALL:
            boxes = corners if way[0] and way[1] else ((low, high, low, high),)
            for box in boxes:
                if way in ways:
                    yield way, box, slot
                slot += 1

    def copy_of(name, way, box, slot):
        kind = EXCHANGES[name][0]
        land = homes[kind]
        fx, wx, tx = span(way[0], nx, box[0], box[1])
        fy, wy, ty = span(way[1], ny, box[2], box[3])
        steps_at = {"prev_zero": pl.ds(0, 1), "prev_one": pl.ds(1, 1)}.get(name, slice(None))
        if kind == "k":
            source = land.at[0, pl.ds(DEPTH + fx, wx), pl.ds(EDGE + fy, wy)]
            dest = land.at[0, pl.ds(DEPTH + tx, wx), pl.ds(EDGE + ty, wy)]
        else:
            source = land.at[steps_at, pl.ds(DEPTH + fx, wx), pl.ds(EDGE + fy, wy)]
            dest = land.at[steps_at, pl.ds(DEPTH + tx, wx), pl.ds(EDGE + ty, wy)]
        number = NAMES.index(name)
        return pltpu.make_async_remote_copy(
            src_ref=source, dst_ref=dest, send_sem=send_sem.at[number, slot],
            recv_sem=recv_sem.at[number, slot], device_id=target(way), device_id_type=MESH)

    def send(name, ways=ALL):
        for way, box, slot in pieces(name, ways):
            @pl.when(there(way))
            def _(way=way, box=box, slot=slot):
                copy_of(name, way, box, slot).start()

    def wait(name):
        for way, box, slot in pieces(name, REST + X_FACES):
            @pl.when(there(way, -1))
            def _(way=way, box=box, slot=slot):
                copy_of(name, way, box, slot).wait_recv()

    def wait_sent(name):
        for way, box, slot in pieces(name, ALL):
            @pl.when(there(way))
            def _(way=way, box=box, slot=slot):
                copy_of(name, way, box, slot).wait_send()

    half = nx // 2
    ends = ((0, half), (half, nx - half))
    thirds = ((0, DEPTH - 1), (nx - DEPTH + 1, DEPTH - 1), (DEPTH - 1, nx - 2 * DEPTH + 2))

    def across(which, part):
        low, size = (thirds if which == T_MINE else ends)[part]
        near, far = pl.ds(low, size), pl.ds(DEPTH + low, size)
        source, dest = {
            T_INIT: lambda: (ini.at[steps - 1, far, mid], before.at[near]),
            T_LAST: lambda: (first.at[steps - 1, far, mid], last.at[0, far, mid]),
            T_ONE: lambda: (err.at[1, far, mid], prev.at[1, far, mid]),
            T_ZERO: lambda: (err.at[0, far, mid], prev.at[0, far, mid]),
            T_MINE: lambda: (mine.at[near], theirs.at[near]),
            T_GUESS: lambda: (guess.at[near], ahead.at[near]),
        }[which]()
        return pltpu.make_async_remote_copy(
            src_ref=source, dst_ref=dest, send_sem=tsend.at[which, part],
            recv_sem=trecv.at[which, part], device_id={"tm": 1 - tm}, device_id_type=MESH)

    def pass_on(which, parts=(0, 1)):
        @pl.when(tm == 0)
        def _():
            for part in parts:
                across(which, part).start()

    def arrive(which, parts=(0, 1)):
        @pl.when(tm > 0)
        def _():
            for part in parts:
                across(which, part).wait_recv()

    loads[0].wait()
    send("kappa")
    loads[1].wait()
    send("init")
    pass_on(T_INIT)
    loads[2].wait()
    send("source")
    send("kappa_far")

    column = lax.broadcasted_iota(jnp.int32, (wide, nz), 1)
    height = lax.broadcasted_iota(jnp.int32, (wide, nz), 0)
    low_side = jnp.where(sy == 0, EDGE, 0)
    high_side = jnp.where(sy == n_sy - 1, EDGE + ny, wide)
    within = jnp.logical_and(height >= low_side, height < high_side)
    low_row = jnp.where(sx == 0, DEPTH, 0)
    high_row = jnp.where(sx == n_sx - 1, DEPTH + nx, nx + 2 * DEPTH)

    def around(ref, t, x):
        here = ref[t, x]
        return here, (
            ref[t, x + 1], ref[t, x - 1],
            pltpu.roll(here, wide - 1, 0), pltpu.roll(here, 1, 0),
            pltpu.roll(here, nz - 1, 1), pltpu.roll(here, 1, 1),
        )

    def around_part(ref, t, x, size):
        low = EDGE - (size - ny) // 2
        part = pl.ds(low, size)
        here = ref[t, x, part, :]
        return here, (
            ref[t, x + 1, part, :], ref[t, x - 1, part, :],
            ref[t, x, pl.ds(low + 1, size), :], ref[t, x, pl.ds(low - 1, size), :],
            pltpu.roll(here, nz - 1, 1), pltpu.roll(here, 1, 1),
        )

    def beside(ref, t, x, g):
        here, sides = around_part(ref, t, x, g[0].shape[0])
        terms = [g[j] * sides[j] for j in range(6)]
        return here, (terms[0] + terms[1]) + (terms[2] + terms[3]) + (terms[4] + terms[5])

    def faces(x):
        return [face[j, x, win, :] for j in range(6)]

    def faces_mid(x):
        return [face[j, x, mid, :] for j in range(6)]

    def couple(here, sides, col):
        sides = list(sides)
        top, bottom = col == nz - 1, col == 0
        sides[4] = jnp.where(top, 0.0, sides[4])
        sides[5] = jnp.where(bottom, 0.0, sides[5])
        g = [0.5 * (here + side) for side in sides]
        whole = (g[0] + g[1]) + (g[2] + g[3]) + (g[4] + g[5])
        g[4] = jnp.where(top, 0.0, g[4])
        g[5] = jnp.where(bottom, 0.0, g[5])
        return g, whole

    def coefficients_mid(x):
        g, whole = couple(*around_part(kap, 0, x, ny), column[:ny])
        coupling[x, mid, :] = whole
        for j in range(6):
            face[j, x, mid, :] = g[j]
        for level in range(2):
            factor[level, x, mid, :] = relax_weight / (1.0 + (2.0 ** level) * whole)

    def coefficients(x):
        g, whole = couple(*around(kap, 0, x), column)
        coupling[x] = whole
        inside = jnp.logical_and(within, jnp.logical_and(x >= low_row, x < high_row))
        for j in range(6):
            face[j, x] = g[j]
        for level in range(4):
            factor[level, x] = jnp.where(inside, relax_weight / (1.0 + (2.0 ** level) * whole), 0.0)

    def phase(body, edge, name):
        for i in range(edge):
            body(DEPTH + i)
            body(DEPTH + nx - 1 - i)
        send(name, X_FACES)

        def step(x, carry):
            body(x)
            return carry

        lax.fori_loop(DEPTH + edge, DEPTH + nx - edge, step, 0, unroll=nx // 2 - edge)
        send(name, REST)

    wait("kappa")
    rows(coefficients_mid, 0)
    wait("init")
    arrive(T_INIT)

    def sweep_first(x):
        g, f = faces_mid(x), factor[0, x, mid, :]
        running = before[x - DEPTH]
        for t in range(steps):
            here, near = beside(ini, t, x, g)
            running = keep_weight * here + f * (src[t, x, mid, :] + near + running)
            first[t, x, mid, :] = running

    phase(sweep_first, 1, "first")
    pass_on(T_LAST)
    wait("kappa_far")
    rows(coefficients, 5)
    send("first_far")
    wait("first")

    def down_one(x):
        g, f, c = faces_mid(x), factor[0, x, mid, :], coupling[x, mid, :]
        f_one = factor[1, x, mid, :]
        diagonal = 1.0 + c
        earlier = None
        ahead_value = None
        running = None
        pair_zero = None
        for m in range(2):
            both = None
            for t in (2 * m, 2 * m + 1):
                here, near = beside(first, t, x, g)
                supply = src[t, x, mid, :] + near
                value = supply - diagonal * here
                if earlier is not None:
                    value = value + earlier
                both = value if both is None else both + value
                ahead_value = keep_weight * here + f * (supply if ahead_value is None else supply + ahead_value)
                earlier = here
            running = f_one * both if running is None else f_one * (both + running)
            err[m, x, mid, :] = running
            pair_zero = running if m == 0 else pair_zero
        both = pair_zero + running
        pair[1, x, mid, :] = both
        pair[0, x, mid, :] = both + at_zero * ((f_one + f_one * f_one) * earlier)
        pair[2, x, mid, :] = at_zero * running
        guess[x - DEPTH] = ahead_value

    phase(down_one, 2, "pair")
    pass_on(T_ONE)
    pass_on(T_ZERO)
    send("err")
    arrive(T_LAST)

    @pl.when(tm > 0)
    def _():
        send("last")

    wait("pair")

    def down_two(x):
        here, near = beside(pair, 0, x, faces(x))
        value = 0.25 * (1.0 + 2.0 * coupling[x, win, :]) * here + 2.0 * near + pair[2, x, win, :]
        fr[0, x, win, :] = factor[2, x, win, :] * value

    rows(down_two, 1)

    def down_three(x):
        g, c = faces_mid(x), coupling[x, mid, :]
        here, near = beside(fr, 0, x, g)
        value = 0.25 * (1.0 + 4.0 * c) * here + 4.0 * near
        here, near = beside(pair, 1, x, g)
        base = factor[2, x, mid, :] * (0.25 * (1.0 + 2.0 * c) * here + 2.0 * near)
        mine[x - DEPTH] = value + at_zero * base

    def part_rows(body, part):
        low, size = thirds[part]

        def step(x, carry):
            body(x)
            return carry

        lax.fori_loop(DEPTH + low, DEPTH + low + size, step, 0, unroll=size)

    for part in range(3):
        part_rows(down_three, part)
        across(T_MINE, part).start()
    pass_on(T_GUESS)
    arrive(T_ONE)

    @pl.when(tm > 0)
    def _():
        send("prev_one")

    arrive(T_ZERO)

    @pl.when(tm > 0)
    def _():
        send("prev_zero")

    def add_up(x):
        rhs3[0, x, mid, :] = mine[x - DEPTH] + theirs[x - DEPTH]

    for part in range(2):
        across(T_MINE, part).wait_recv()
        part_rows(add_up, part)
        send("rhs3", ((2 * part - 1, 0), (2 * part - 1, -1), (2 * part - 1, 1)))
    across(T_MINE, 2).wait_recv()
    part_rows(add_up, 2)
    send("rhs3", ((0, -1), (0, 1)))

    wait("err")
    wait("first_far")

    @pl.when(tm > 0)
    def _():
        wait("last")
        wait("prev_one")
        wait("prev_zero")

    def gather_far(x):
        f = factor[1, x]
        sums[0, x] = err[0, x] + err[1, x] + (f + f * f) * last[0, x]
        sums[1, x] = prev[0, x] + prev[1, x]

    rows(gather_far, 5)

    def level_two(x):
        g, f, weight = faces(x), factor[2, x, win, :], 0.25 * (1.0 + 2.0 * coupling[x, win, :])
        here, near = beside(sums, 0, x, g)
        err2[0, x, win, :] = f * (weight * here + 2.0 * near + prev[1, x, win, :])
        here, near = beside(sums, 1, x, g)
        err2[1, x, win, :] = f * (weight * here + 2.0 * near)

    rows(level_two, 4)

    def own_errors(x):
        f = factor[1, x, win, :]
        carried = f * last[0, x, win, :]
        return err[0, x, win, :] + carried, err[1, x, win, :] + f * carried

    def fix_two(x):
        g, f = faces(x), factor[2, x, win, :]
        own, near = beside(err2, 0, x, g)
        past, near_past = beside(err2, 1, x, g)
        value = (2.0 - relax_weight) * own + f * (4.0 * near + past)
        value_past = (2.0 - relax_weight) * past + 4.0 * (f * near_past)
        zero, first_one = own_errors(x)
        fix[0, x, win, :] = zero + value
        fix[1, x, win, :] = first_one + value
        fix[2, x, win, :] = prev[0, x, win, :] + value_past
        fix[3, x, win, :] = prev[1, x, win, :] + value_past

    rows(fix_two, 3)

    def fix_one(x):
        g, f = faces(x), factor[1, x, win, :]
        here, near = [], []
        for i in range(4):
            a, b = beside(fix, i, x, g)
            here.append(a)
            near.append(keep_weight * a + 2.0 * (f * b))
        zero, first_one = own_errors(x)
        value = near[0] + zero + f * here[3]
        vee[0, x, win, :] = value
        vee[1, x, win, :] = near[1] + first_one + f * (value - zero)
        value = near[2] + prev[0, x, win, :]
        vee[2, x, win, :] = value
        vee[3, x, win, :] = near[3] + prev[1, x, win, :] + f * (value - prev[0, x, win, :])

    rows(fix_one, 2)
    wait("rhs3")

    def coarse_one(x):
        one[0, x] = factor[3, x] * rhs3[0, x]

    rows(coarse_one, 5)

    def coarse_two(x):
        here, near = beside(one, 0, x, faces(x))
        err3[0, x, win, :] = keep_weight * here + factor[3, x, win, :] * (rhs3[0, x, win, :] + 8.0 * near)

    rows(coarse_two, 4)

    def up_two(x):
        f = factor[2, x, win, :]
        here, near = beside(err3, 0, x, faces(x))
        value = keep_weight * here + 4.0 * (f * near)
        wave[0, x, win, :] = value + at_one * (f * here)
        wave[1, x, win, :] = value

    rows(up_two, 3)

    def up_one(x):
        g, f = faces(x), factor[1, x, win, :]
        here, near = beside(wave, 0, x, g)
        past, near_past = beside(wave, 1, x, g)
        own = keep_weight * here + 2.0 * (f * near)
        shadow = at_one * (keep_weight * past + 2.0 * (f * near_past))
        zero = own + at_one * (f * past)
        gain = (vee[0, x, win, :] + zero, vee[1, x, win, :] + own + f * zero)
        for t in range(steps):
            total[t, x, win, :] = first[t, x, win, :] + gain[t // 2]
        vee[2, x, win, :] = vee[2, x, win, :] + shadow
        vee[3, x, win, :] = vee[3, x, win, :] + shadow + f * shadow

    rows(up_one, 2)
    wait("source")

    def up_zero(x):
        g, f = faces(x), factor[0, x, win, :]
        running = last[0, x, win, :] + vee[3, x, win, :]
        for t in range(steps):
            here, near = beside(total, t, x, g)
            running = keep_weight * here + f * (src[t, x, win, :] + near + running)
            sol[t, x, win, :] = running

    rows(up_zero, 1)
    arrive(T_GUESS)

    def finish(x):
        g, f = faces_mid(x), factor[0, x, mid, :]
        diagonal = 1.0 + coupling[x, mid, :]
        lifted = []
        for i in (2, 3):
            here, near = beside(vee, i, x, g)
            lifted.append(keep_weight * here + f * near)
        earlier = ahead[x - DEPTH] + (1.0 + f) * (f * f * lifted[0] + lifted[1])
        for t in range(steps):
            here, near = beside(sol, t, x, g)
            sol_out[t, x - DEPTH] = here
            res_out[t, x - DEPTH] = src[t, x, mid, :] + earlier - (diagonal * here - near)
            earlier = here

    rows(finish, 0)

    for name in NAMES:
        if name in ("last", "prev_one", "prev_zero"):
            @pl.when(tm > 0)
            def _(name=name):
                wait_sent(name)
        else:
            wait_sent(name)

    @pl.when(tm == 0)
    def _():
        for which in (T_INIT, T_LAST, T_ONE, T_ZERO, T_GUESS):
            for part in range(2):
                across(which, part).wait_send()

    for part in range(3):
        across(T_MINE, part).wait_send()


def wide_scratch(steps, nx, ny, nz):
    f32, dma = jnp.float32, pltpu.SemaphoreType.DMA
    depths = (1, steps, steps, steps, 3, 2, 1, 2, 2, 1, 1, 1, 1, 2, 2, 4, 4, steps, steps, 6)
    large = (nx + 2 * DEPTH, ny + 2 * EDGE, nz)
    scratch = [pltpu.VMEM((d,) + large, f32) for d in depths]
    scratch += [pltpu.VMEM(large, f32), pltpu.VMEM((4,) + large, f32)]
    scratch += [pltpu.VMEM((nx, ny, nz), f32)] * 5
    scratch += [dma((len(NAMES), 12)), dma((len(NAMES), 12)), dma((6, 3)), dma((6, 3)), dma((3,))]
    return scratch


def store(one, two, one_hbm, two_hbm, sem):
    copies = [pltpu.make_async_copy(one, one_hbm, sem.at[0]), pltpu.make_async_copy(two, two_hbm, sem.at[1])]
    for copy in copies:
        copy.start()
    for copy in copies:
        copy.wait()


def solution(mesh):
    n_tm, n_sx, n_sy = (mesh.shape[axis] for axis in ("tm", "sx", "sy"))
    f32 = jnp.float32

    def per_device(heat_source, conductivity, initial_iterate):
        steps, nx, ny, nz = heat_source.shape
        depth = (1, steps, steps, steps // 2, 1, 1, 1, steps // 2, steps, steps, 1, 1, 1, 1)
        scratch = [pltpu.VMEM((d, nx + 2, ny, nz), f32) for d in depth]
        scratch += [pltpu.VMEM((2, d, nx, nz), f32) for d in depth] * 2
        cells = (nx, ny, nz)
        dma = pltpu.SemaphoreType.DMA
        scratch += [
            pltpu.VMEM((steps,) + cells, f32),
            pltpu.VMEM((steps,) + cells, f32),
            pltpu.VMEM((7,) + cells, f32),
            pltpu.VMEM(cells, f32),
            pltpu.VMEM((steps // 2,) + cells, f32),
            pltpu.VMEM(cells, f32),
            pltpu.VMEM(cells, f32),
            pltpu.VMEM(cells, f32),
            pltpu.VMEM(cells, f32),
            pltpu.VMEM((2,) + cells, f32),
            pltpu.VMEM((6,) + cells, f32),
            pltpu.VMEM(cells, f32),
            pltpu.VMEM((4,) + cells, f32),
            dma((FIELDS, 4)), dma((FIELDS, 4)), dma((7, 2)), dma((7, 2)),
            dma((2,)), dma((2,)), dma((2,)), dma((2,)), dma((5,)),
        ]
        field = jax.ShapeDtypeStruct(heat_source.shape, f32)
        small = n_tm == 2 and steps == 4 and nx >= 2 * DEPTH and ny >= EDGE and ny % EDGE == 0
        if small:
            scratch = wide_scratch(steps, nx, ny, nz)
        one, two = pl.pallas_call(
            functools.partial(wide_kernel, n_sx, n_sy) if small else functools.partial(kernel, n_tm, n_sx, n_sy),
            out_shape=(pltpu.VMEM(heat_source.shape, f32),) * 2,
            in_specs=[pl.BlockSpec(memory_space=pltpu.HBM)] * 3,
            out_specs=(pl.BlockSpec(memory_space=pltpu.VMEM),) * 2,
            scratch_shapes=scratch,
            compiler_params=pltpu.CompilerParams(
                collective_id=0, has_side_effects=True, vmem_limit_bytes=40000000
            ),
            name="vcycle",
        )(*(pltpu.with_memory_space_constraint(x, pltpu.HBM) for x in (heat_source, conductivity, initial_iterate)))
        return pl.pallas_call(
            store,
            out_shape=(field, field),
            in_specs=[pl.BlockSpec(memory_space=pltpu.VMEM)] * 2,
            out_specs=(pl.BlockSpec(memory_space=pltpu.HBM),) * 2,
            scratch_shapes=[dma((2,))],
            name="store",
        )(*(pltpu.with_memory_space_constraint(x, pltpu.VMEM) for x in (one, two)))

    placed = (P("tm", "sx", "sy", None), P("sx", "sy", None), P("tm", "sx", "sy", None))
    return jax.shard_map(
        per_device,
        mesh=mesh,
        in_specs=placed,
        out_specs=(P("tm", "sx", "sy", None), P("tm", "sx", "sy", None)),
        check_vma=False,
    )
```

```python
import functools

import jax
import jax.numpy as jnp
from jax import lax
from jax.experimental import pallas as pl
from jax.experimental.pallas import tpu as pltpu
from jax.sharding import PartitionSpec as P

relax_weight = 0.8
keep_weight = 1.0 - relax_weight
MESH = pl.DeviceIdType.MESH

KAPPA, INIT, FIRST, ERR1, ERR2, ERR3, FIX2, FIX1, SUM0, SOL, PART, PAIR, PART2, PAIR2 = range(14)
FIELDS = 14
P_INIT, P_FIRST, P_ERR1, P_ERR2, P_FIX1, P_SUM0, P_SOL = range(7)
XLO, XHI, YLO, YHI = range(4)


def kernel(n_tm, n_sx, n_sy, hs_hbm, k_hbm, in_hbm, sol_hbm, res_hbm, *scratch):
    fields = scratch[:FIELDS]
    yrecv = scratch[FIELDS:2 * FIELDS]
    ysend = scratch[2 * FIELDS:3 * FIELDS]
    (hs, res, before, second, rhs1, rhs2, rhs3, mine, theirs, chain,
     face, coupling, factor, send_sem, recv_sem, tsend, trecv,
     qsend, qrecv, csend, crecv, local) = scratch[3 * FIELDS:]
    steps, nx, ny, nz = hs.shape
    tm, sx, sy = lax.axis_index("tm"), lax.axis_index("sx"), lax.axis_index("sy")
    has = (sx > 0, sx < n_sx - 1, sy > 0, sy < n_sy - 1)
    partner = tm + 1 - 2 * lax.rem(tm, 2)
    even = lax.rem(tm, 2) == 0

    loads = [
        pltpu.make_async_copy(k_hbm, fields[KAPPA].at[0, pl.ds(1, nx)], local.at[0]),
        pltpu.make_async_copy(in_hbm, fields[INIT].at[:, pl.ds(1, nx)], local.at[1]),
        pltpu.make_async_copy(hs_hbm, hs, local.at[2]),
    ]
    for load in loads:
        load.start()

    barrier = pltpu.get_barrier_semaphore()
    greet = [
        (has[XLO], {"sx": sx - 1}), (has[XHI], {"sx": sx + 1}),
        (has[YLO], {"sy": sy - 1}), (has[YHI], {"sy": sy + 1}),
        (tm > 0, {"tm": tm - 1}), (tm < n_tm - 1, {"tm": tm + 1}),
    ]
    if n_tm == 2:
        greet += [
            (has[XLO], {"tm": partner, "sx": sx - 1}), (has[XHI], {"tm": partner, "sx": sx + 1}),
            (has[YLO], {"tm": partner, "sy": sy - 1}), (has[YHI], {"tm": partner, "sy": sy + 1}),
        ]
    if n_tm > 2:
        greet += [(tm > 1, {"tm": tm - 2}), (tm < n_tm - 2, {"tm": tm + 2})]
    count = jnp.int32(0)
    for there, device in greet:
        count = count + jnp.where(there, 1, 0)

        @pl.when(there)
        def _(device=device):
            pl.semaphore_signal(barrier, inc=1, device_id=device, device_id_type=MESH)

    pl.semaphore_wait(barrier, count)

    def face_copy(i, side, pair=False):
        field = fields[i]
        to = i + 1 if pair else i
        land = fields[to]
        if side == XLO:
            if i == INIT:
                src = in_hbm.at[:, pl.ds(0, 1)]
            elif i == KAPPA:
                src = k_hbm.at[pl.ds(0, 1)]
            else:
                src = field.at[:, pl.ds(1, 1)]
            dst, device = land.at[:, pl.ds(nx + 1, 1)], {"sx": sx - 1}
        elif side == XHI:
            if i == INIT:
                src = in_hbm.at[:, pl.ds(nx - 1, 1)]
            elif i == KAPPA:
                src = k_hbm.at[pl.ds(nx - 1, 1)]
            else:
                src = field.at[:, pl.ds(nx, 1)]
            dst, device = land.at[:, pl.ds(0, 1)], {"sx": sx + 1}
        elif side == YLO:
            src, dst, device = ysend[i].at[0], yrecv[to].at[1], {"sy": sy - 1}
        else:
            src, dst, device = ysend[i].at[1], yrecv[to].at[0], {"sy": sy + 1}
        if i == KAPPA and side in (XLO, XHI):
            dst = field.at[0, pl.ds(nx + 1 if side == XLO else 0, 1)]
        if pair:
            device["tm"] = partner
        return pltpu.make_async_remote_copy(
            src_ref=src, dst_ref=dst, send_sem=send_sem.at[to, side],
            recv_sem=recv_sem.at[to, side], device_id=device, device_id_type=MESH)

    def send_faces(i, sides, pair=False):
        for side in sides:
            @pl.when(has[side])
            def _(side=side):
                face_copy(i, side).start()
                if pair:
                    face_copy(i, side, True).start()

    def wait_faces(i, pair=False):
        for side in (YLO, YHI, XLO, XHI):
            @pl.when(has[side ^ 1])
            def _(side=side):
                face_copy(i, side, pair).wait_recv()

    half = nx // 2
    halves = (pl.ds(0, half), pl.ds(half, nx - half))

    def last_copy(i, part):
        field = fields[lasts[i]]
        if i == P_INIT:
            src = in_hbm.at[steps - 1, halves[part]]
        else:
            src = field.at[field.shape[0] - 1, (pl.ds(1, half), pl.ds(1 + half, nx - half))[part]]
        return pltpu.make_async_remote_copy(
            src_ref=src, dst_ref=before.at[i, halves[part]],
            send_sem=tsend.at[i, part], recv_sem=trecv.at[i, part],
            device_id={"tm": tm + 1}, device_id_type=MESH)

    lasts = (INIT, FIRST, ERR1, ERR2, FIX1, SUM0, SOL)

    def send_last(i, part):
        @pl.when(tm < n_tm - 1)
        def _():
            last_copy(i, part).start()

    def wait_last(i, parts=(0, 1)):
        @pl.when(tm > 0)
        def _():
            for part in parts:
                last_copy(i, part).wait_recv()

    send_faces(KAPPA, (XLO, XHI))
    send_faces(INIT, (XLO, XHI))
    send_last(P_INIT, 0)
    send_last(P_INIT, 1)

    def over_rows(body, by=8, start=0, stop=nx):
        def step(x, carry):
            body(x)
            return carry

        lax.fori_loop(start, stop, step, 0, unroll=by)

    def phase(body, i, send_part=None, pair=False, awaited=None):
        if awaited is not None:
            wait_last(awaited, (0,))
        body(0)
        if awaited is None:
            body(nx - 1)
            send_faces(i, (XLO, XHI), pair)
        else:
            send_faces(i, (XLO,), pair)
        over_rows(body, half - 1, 1, half)
        if send_part is not None:
            send_part(0)
        if awaited is not None:
            wait_last(awaited, (1,))
            body(nx - 1)
            send_faces(i, (XHI,), pair)
        over_rows(body, half - 1, half, nx - 1)
        send_faces(i, (YLO, YHI), pair)
        if send_part is not None:
            send_part(1)

    def put_faces(i, t, x, value):
        ysend[i][0, t, pl.ds(x, 1), :] = value[0:1, :]
        ysend[i][1, t, pl.ds(x, 1), :] = value[ny - 1:ny, :]

    def put(i, t, x, value):
        fields[i][t, x + 1] = value
        put_faces(i, t, x, value)

    loads[0].wait()
    loads[1].wait()

    def pack(x):
        put_faces(KAPPA, 0, x, fields[KAPPA][0, x + 1])
        for t in range(steps):
            put_faces(INIT, t, x, fields[INIT][t, x + 1])

    over_rows(pack)
    send_faces(KAPPA, (YLO, YHI))
    send_faces(INIT, (YLO, YHI))

    @pl.when(sx == 0)
    def _():
        for i in range(FIELDS):
            for t in range(fields[i].shape[0]):
                fields[i][t, 0] = jnp.zeros((ny, nz), jnp.float32)

    @pl.when(sx == n_sx - 1)
    def _():
        for i in range(FIELDS):
            for t in range(fields[i].shape[0]):
                fields[i][t, nx + 1] = jnp.zeros((ny, nz), jnp.float32)

    @pl.when(sy == 0)
    def _():
        for i in range(FIELDS):
            yrecv[i][0] = jnp.zeros(yrecv[i].shape[1:], jnp.float32)

    @pl.when(sy == n_sy - 1)
    def _():
        for i in range(FIELDS):
            yrecv[i][1] = jnp.zeros(yrecv[i].shape[1:], jnp.float32)

    @pl.when(tm == 0)
    def _():
        def clear(x):
            for i in range(7):
                before[i, x] = jnp.zeros((ny, nz), jnp.float32)

        over_rows(clear, 1)

    row = lax.broadcasted_iota(jnp.int32, (ny, nz), 0)
    column = lax.broadcasted_iota(jnp.int32, (ny, nz), 1)

    def around(i, t, x):
        field = fields[i]
        here = field[t, x + 1]
        return here, (
            field[t, x + 2],
            field[t, x],
            jnp.where(row == ny - 1, yrecv[i][1, t, pl.ds(x, 1), :], pltpu.roll(here, ny - 1, 0)),
            jnp.where(row == 0, yrecv[i][0, t, pl.ds(x, 1), :], pltpu.roll(here, 1, 0)),
            pltpu.roll(here, nz - 1, 1),
            pltpu.roll(here, 1, 1),
        )

    def beside(i, t, x, g):
        here, sides = around(i, t, x)
        terms = [g[j] * sides[j] for j in range(6)]
        return here, (terms[0] + terms[1]) + (terms[2] + terms[3]) + (terms[4] + terms[5])

    def faces_at(x):
        return [face[j, x] for j in range(6)]

    wait_faces(KAPPA)

    def coefficients(x):
        here, sides = around(KAPPA, 0, x)
        sides = list(sides)
        sides[4] = jnp.where(column == nz - 1, 0.0, sides[4])
        sides[5] = jnp.where(column == 0, 0.0, sides[5])
        g = [0.5 * (here + side) for side in sides]
        total = (g[0] + g[1]) + (g[2] + g[3]) + (g[4] + g[5])
        coupling[x] = total
        g[4] = jnp.where(column == nz - 1, 0.0, g[4])
        g[5] = jnp.where(column == 0, 0.0, g[5])
        for j in range(6):
            face[j, x] = g[j]
        for level in range(4):
            factor[level, x] = relax_weight / (1.0 + (2.0 ** level) * total)

    over_rows(coefficients)
    loads[2].wait()
    wait_faces(INIT)

    def sweep_first(x):
        g, f = faces_at(x), factor[0, x]
        running = before[P_INIT, x]
        for t in range(steps):
            here, near = beside(INIT, t, x, g)
            running = keep_weight * here + f * (hs[t, x] + near + running)
            put(FIRST, t, x, running)

    phase(sweep_first, FIRST, functools.partial(send_last, P_FIRST), awaited=P_INIT)
    wait_faces(FIRST)

    def down_one(x):
        g, diagonal, f = faces_at(x), 1.0 + coupling[x], factor[1, x]
        earlier = before[P_FIRST, x]
        running = None
        for m in range(steps // 2):
            total = None
            for t in (2 * m, 2 * m + 1):
                here, near = beside(FIRST, t, x, g)
                value = hs[t, x] + earlier - (diagonal * here - near)
                total = value if total is None else total + value
                earlier = here
            rhs1[m, x] = total
            running = f * total if running is None else f * (total + running)
            put(ERR1, m, x, running)

    phase(down_one, ERR1, functools.partial(send_last, P_ERR1), awaited=P_FIRST)
    wait_faces(ERR1)
    wait_last(P_ERR1)

    def down_two(x):
        g, diagonal, f = faces_at(x), 1.0 + 2.0 * coupling[x], factor[2, x]
        earlier = before[P_ERR1, x]
        total = None
        for t in range(2):
            here, near = beside(ERR1, t, x, g)
            value = rhs1[t, x] + earlier - (diagonal * here - 2.0 * near)
            total = value if total is None else total + value
            earlier = here
        rhs2[x] = total
        put(ERR2, 0, x, f * total)

    phase(down_two, ERR2, functools.partial(send_last, P_ERR2))
    wait_faces(ERR2)
    if n_tm > 2:
        wait_last(P_ERR2)

    def down_three(x):
        g, diagonal = faces_at(x), 1.0 + 4.0 * coupling[x]
        here, near = beside(ERR2, 0, x, g)
        earlier = here + before[P_ERR2, x] if n_tm > 2 else here
        value = rhs2[x] + jnp.where(even, earlier, 0.0) - (diagonal * here - 4.0 * near)
        mine[x] = value
        if n_tm == 2:
            put(PART, 0, x, factor[3, x] * value)

    def swap(part):
        return pltpu.make_async_remote_copy(
            src_ref=mine.at[halves[part]], dst_ref=theirs.at[halves[part]],
            send_sem=qsend.at[part], recv_sem=qrecv.at[part],
            device_id={"tm": partner}, device_id_type=MESH)

    if n_tm == 2:
        phase(down_three, PART, lambda part: swap(part).start(), True)
        wait_faces(PART)

        def part_two(x):
            here, near = beside(PART, 0, x, faces_at(x))
            put(PART2, 0, x, keep_weight * here + factor[3, x] * (mine[x] + 8.0 * near))

        phase(part_two, PART2, None, True)
    else:
        over_rows(down_three)
        swap(0).start()
        swap(1).start()
    swap(0).wait_recv()
    swap(1).wait_recv()

    def chain_copy(i, field):
        src = field.at[0, pl.ds(1, nx)] if i == 0 else second
        return pltpu.make_async_remote_copy(
            src_ref=src, dst_ref=chain.at[i], send_sem=csend.at[i],
            recv_sem=crecv.at[i], device_id={"tm": tm + 2}, device_id_type=MESH)

    def chain_wait(i):
        if n_tm > 2:
            @pl.when(tm > 1)
            def _():
                chain_copy(i, fields[ERR3]).wait_recv()

            @pl.when(tm < 2)
            def _():
                def clear(x):
                    chain[i, x] = jnp.zeros((ny, nz), jnp.float32)

                over_rows(clear, 1)

    def chain_send(i):
        if n_tm > 2:
            @pl.when(tm < n_tm - 2)
            def _():
                chain_copy(i, fields[ERR3]).start()

    chain_wait(0)

    def coarse_one(x):
        total = mine[x] + theirs[x]
        rhs3[x] = total
        if n_tm > 2:
            total = total + chain[0, x]
        value = factor[3, x] * total
        if n_tm > 2:
            put(ERR3, 0, x, value)
        else:
            fields[ERR3][0, x + 1] = value

    if n_tm > 2:
        phase(coarse_one, ERR3)
        chain_send(0)
        wait_faces(ERR3)
    else:
        over_rows(coarse_one)
        wait_faces(PART, True)
        for edge in (0, nx + 1):
            fields[ERR3][0, edge] = fields[PART][0, edge] + fields[PAIR][0, edge]
        for edge in range(2):
            yrecv[ERR3][edge, 0] = yrecv[PART][edge, 0] + yrecv[PAIR][edge, 0]
    if n_tm == 2:
        wait_last(P_ERR2)
    chain_wait(1)

    def coarse_two(x):
        here, near = beside(ERR3, 0, x, faces_at(x))
        total = rhs3[x] + 8.0 * near
        if n_tm > 2:
            total = total + chain[1, x]
        value = keep_weight * here + factor[3, x] * total
        if n_tm > 2:
            second[x] = value
            earlier = jnp.where(even, chain[1, x], value)
        else:
            earlier = jnp.where(even, 0.0, value)
        mine_next[x] = before[P_ERR2, x] + earlier
        value = fields[ERR2][0, x + 1] + value
        if n_tm > 2:
            put(FIX2, 0, x, value)
        else:
            fields[FIX2][0, x + 1] = value

    mine_next = res.at[0]
    if n_tm > 2:
        phase(coarse_two, FIX2)
        chain_send(1)
        wait_faces(FIX2)
    else:
        over_rows(coarse_two)
        wait_faces(PART2)
        wait_faces(PART2, True)
        for edge in (0, nx + 1):
            fields[FIX2][0, edge] = fields[ERR2][0, edge] + (
                fields[PART2][0, edge] + fields[PAIR2][0, edge])
        for edge in range(2):
            yrecv[FIX2][edge, 0] = yrecv[ERR2][edge, 0] + (
                yrecv[PART2][edge, 0] + yrecv[PAIR2][edge, 0])

    def up_two(x):
        here, near = beside(FIX2, 0, x, faces_at(x))
        value = keep_weight * here + factor[2, x] * (rhs2[x] + 4.0 * near + mine_next[x])
        for m in range(2):
            put(FIX1, m, x, fields[ERR1][m, x + 1] + value)

    phase(up_two, FIX1, functools.partial(send_last, P_FIX1))
    wait_faces(FIX1)

    def up_one(x):
        g, f = faces_at(x), factor[1, x]
        running = before[P_FIX1, x]
        for m in range(2):
            here, near = beside(FIX1, m, x, g)
            running = keep_weight * here + f * (rhs1[m, x] + 2.0 * near + running)
            for t in (2 * m, 2 * m + 1):
                put(SUM0, t, x, fields[FIRST][t, x + 1] + running)

    phase(up_one, SUM0, functools.partial(send_last, P_SUM0), awaited=P_FIX1)
    wait_faces(SUM0)
    wait_last(P_SUM0)

    def up_zero(x):
        g, f = faces_at(x), factor[0, x]
        running = before[P_SUM0, x]
        for t in range(steps):
            here, near = beside(SUM0, t, x, g)
            running = keep_weight * here + f * (hs[t, x] + near + running)
            put(SOL, t, x, running)
            sol_hbm[t, x] = running

    phase(up_zero, SOL, functools.partial(send_last, P_SOL))
    wait_faces(SOL)
    wait_last(P_SOL)

    def last_defect(x):
        g, diagonal = faces_at(x), 1.0 + coupling[x]
        earlier = before[P_SOL, x]
        for t in range(steps):
            here, near = beside(SOL, t, x, g)
            res_hbm[t, x] = hs[t, x] + earlier - (diagonal * here - near)
            earlier = here

    over_rows(last_defect)

    for i in range(FIELDS):
        if i in ((PAIR, PAIR2, ERR3, FIX2) if n_tm == 2 else (PART, PAIR, PART2, PAIR2)):
            continue
        for side in (XLO, XHI, YLO, YHI):
            @pl.when(has[side])
            def _(i=i, side=side):
                face_copy(i, side).wait_send()
                if i in (PART, PART2):
                    face_copy(i, side, True).wait_send()

    @pl.when(tm < n_tm - 1)
    def _():
        for i in range(7):
            for part in range(2):
                last_copy(i, part).wait_send()

    swap(0).wait_send()
    swap(1).wait_send()
    if n_tm > 2:
        @pl.when(tm < n_tm - 2)
        def _():
            for i in range(2):
                chain_copy(i, fields[ERR3]).wait_send()


DEPTH = 6
EDGE = 8
REACH = 4
EXCHANGES = {
    "kappa": ("k", (0, 1), ()),
    "kappa_far": ("k", (1, 6), ((0, 5, 0, 5),)),
    "init": ("in", (0, 1), ()),
    "source": ("hs", (0, 1), ()),
    "first": ("first", (0, 1), ()),
    "first_far": ("first", (1, 2), ((0, 1, 0, 1),)),
    "pair": ("pair", (0, 2), ((0, 1, 0, 1),)),
    "err": ("err", (0, 5), ((0, 4, 0, 4),)),
    "last": ("last", (0, 5), ((0, 4, 0, 4),)),
    "prev_one": ("prev", (0, 5), ((0, 4, 0, 4),)),
    "prev_zero": ("prev", (0, 5), ((0, 4, 0, 4),)),
    "rhs3": ("rhs3", (0, 5), ((0, 4, 0, 4),)),
}
NAMES = tuple(EXCHANGES)
X_FACES = ((-1, 0), (1, 0))
REST = ((0, -1), (0, 1), (-1, -1), (-1, 1), (1, -1), (1, 1))
ALL = X_FACES + REST
T_INIT, T_LAST, T_ONE, T_ZERO, T_MINE, T_GUESS = range(6)


def wide_kernel(n_sx, n_sy, hs_hbm, k_hbm, in_hbm, sol_out, res_out,
                kap, ini, src, first, pair, err, last, prev, sums, fr, rhs3, one, err3, wave,
                err2, fix, vee, total, sol, face, coupling, factor,
                before, mine, theirs, guess, ahead,
                send_sem, recv_sem, tsend, trecv, local):
    nx, ny, nz = k_hbm.shape
    steps = in_hbm.shape[0]
    wide = ny + 2 * EDGE
    tm, sx, sy = lax.axis_index("tm"), lax.axis_index("sx"), lax.axis_index("sy")
    at_one = jnp.where(tm > 0, 1.0, 0.0)
    at_zero = 1.0 - at_one
    mid = pl.ds(EDGE, ny)
    win = pl.ds(EDGE - REACH, ny + 2 * REACH)
    inner = pl.ds(DEPTH, nx)
    homes = {"k": kap, "in": ini, "hs": src, "first": first, "pair": pair, "err": err,
             "last": last, "prev": prev, "rhs3": rhs3}

    loads = [
        pltpu.make_async_copy(k_hbm, kap.at[0, inner, mid], local.at[0]),
        pltpu.make_async_copy(in_hbm, ini.at[:, inner, mid], local.at[1]),
        pltpu.make_async_copy(hs_hbm, src.at[:, inner, mid], local.at[2]),
    ]
    for load in loads:
        load.start()

    def there(way, sign=1):
        ok = None
        for step, at, size in ((sign * way[0], sx, n_sx), (sign * way[1], sy, n_sy)):
            if step:
                here = at > 0 if step < 0 else at < size - 1
                ok = here if ok is None else jnp.logical_and(ok, here)
        return ok

    def target(way):
        device = {}
        if way[0]:
            device["sx"] = sx + way[0]
        if way[1]:
            device["sy"] = sy + way[1]
        return device

    barrier = pltpu.get_barrier_semaphore()
    count = jnp.int32(1)
    for way in ALL:
        count = count + jnp.where(there(way), 1, 0)

        @pl.when(there(way))
        def _(way=way):
            pl.semaphore_signal(barrier, inc=1, device_id=target(way), device_id_type=MESH)

    pl.semaphore_signal(barrier, inc=1, device_id={"tm": 1 - tm}, device_id_type=MESH)

    def rows(body, depth, by=None):
        def step(x, carry):
            body(x)
            return carry

        if by is None:
            by = (nx + 2 * depth) // (2 if depth else 1)
        lax.fori_loop(DEPTH - depth, DEPTH + nx + depth, step, 0, unroll=by)

    filled = ((kap, 6), (ini, 1), (src, 1), (first, 2), (pair, 2), (err, 5), (last, 5), (prev, 5), (rhs3, 5))
    plane = jnp.zeros((wide, nz), jnp.float32)
    strip = jnp.zeros((EDGE, nz), jnp.float32)

    def fill(edge_rows):
        for array, depth in filled:
            for t in range(array.shape[0]):
                for i in range(depth):
                    array[t, DEPTH - 1 - i if edge_rows < 0 else DEPTH + nx + i] = plane

    def fill_side(start):
        for array, depth in filled:
            def body(x):
                for t in range(array.shape[0]):
                    array[t, x, pl.ds(start, EDGE), :] = strip

            rows(body, depth, 2)

    @pl.when(sx == 0)
    def _():
        fill(-1)

    @pl.when(sx == n_sx - 1)
    def _():
        fill(1)

    @pl.when(sy == 0)
    def _():
        fill_side(0)

    @pl.when(sy == n_sy - 1)
    def _():
        fill_side(EDGE + ny)

    @pl.when(tm == 0)
    def _():
        def body(x):
            last[0, x] = plane
            prev[0, x] = plane
            prev[1, x] = plane

        rows(body, 5, 2)

        def empty(x):
            before[x - DEPTH] = jnp.zeros((ny, nz), jnp.float32)
            ahead[x - DEPTH] = jnp.zeros((ny, nz), jnp.float32)

        rows(empty, 0, 2)

    pl.semaphore_wait(barrier, count)

    def span(step, size, low, high):
        if step == 0:
            return 0, size, 0
        if step < 0:
            return low, high - low, size + low
        return size - high, high - low, -high

    def pieces(name, ways):
        kind, (low, high), corners = EXCHANGES[name]
        slot = 0
        for way in ALL:
            boxes = corners if way[0] and way[1] else ((low, high, low, high),)
            for box in boxes:
                if way in ways:
                    yield way, box, slot
                slot += 1

    def copy_of(name, way, box, slot):
        kind = EXCHANGES[name][0]
        land = homes[kind]
        fx, wx, tx = span(way[0], nx, box[0], box[1])
        fy, wy, ty = span(way[1], ny, box[2], box[3])
        steps_at = {"prev_zero": pl.ds(0, 1), "prev_one": pl.ds(1, 1)}.get(name, slice(None))
        if kind == "k":
            source = land.at[0, pl.ds(DEPTH + fx, wx), pl.ds(EDGE + fy, wy)]
            dest = land.at[0, pl.ds(DEPTH + tx, wx), pl.ds(EDGE + ty, wy)]
        else:
            source = land.at[steps_at, pl.ds(DEPTH + fx, wx), pl.ds(EDGE + fy, wy)]
            dest = land.at[steps_at, pl.ds(DEPTH + tx, wx), pl.ds(EDGE + ty, wy)]
        number = NAMES.index(name)
        return pltpu.make_async_remote_copy(
            src_ref=source, dst_ref=dest, send_sem=send_sem.at[number, slot],
            recv_sem=recv_sem.at[number, slot], device_id=target(way), device_id_type=MESH)

    def send(name, ways=ALL):
        for way, box, slot in pieces(name, ways):
            @pl.when(there(way))
            def _(way=way, box=box, slot=slot):
                copy_of(name, way, box, slot).start()

    def wait(name):
        for way, box, slot in pieces(name, REST + X_FACES):
            @pl.when(there(way, -1))
            def _(way=way, box=box, slot=slot):
                copy_of(name, way, box, slot).wait_recv()

    def wait_sent(name):
        for way, box, slot in pieces(name, ALL):
            @pl.when(there(way))
            def _(way=way, box=box, slot=slot):
                copy_of(name, way, box, slot).wait_send()

    half = nx // 2
    ends = ((0, half), (half, nx - half))
    thirds = ((0, DEPTH - 1), (nx - DEPTH + 1, DEPTH - 1), (DEPTH - 1, nx - 2 * DEPTH + 2))

    def across(which, part):
        low, size = (thirds if which == T_MINE else ends)[part]
        near, far = pl.ds(low, size), pl.ds(DEPTH + low, size)
        source, dest = {
            T_INIT: lambda: (ini.at[steps - 1, far, mid], before.at[near]),
            T_LAST: lambda: (first.at[steps - 1, far, mid], last.at[0, far, mid]),
            T_ONE: lambda: (err.at[1, far, mid], prev.at[1, far, mid]),
            T_ZERO: lambda: (err.at[0, far, mid], prev.at[0, far, mid]),
            T_MINE: lambda: (mine.at[near], theirs.at[near]),
            T_GUESS: lambda: (guess.at[near], ahead.at[near]),
        }[which]()
        return pltpu.make_async_remote_copy(
            src_ref=source, dst_ref=dest, send_sem=tsend.at[which, part],
            recv_sem=trecv.at[which, part], device_id={"tm": 1 - tm}, device_id_type=MESH)

    def pass_on(which, parts=(0, 1)):
        @pl.when(tm == 0)
        def _():
            for part in parts:
                across(which, part).start()

    def arrive(which, parts=(0, 1)):
        @pl.when(tm > 0)
        def _():
            for part in parts:
                across(which, part).wait_recv()

    loads[0].wait()
    send("kappa")
    loads[1].wait()
    send("init")
    pass_on(T_INIT)
    loads[2].wait()
    send("source")
    send("kappa_far")

    column = lax.broadcasted_iota(jnp.int32, (wide, nz), 1)
    height = lax.broadcasted_iota(jnp.int32, (wide, nz), 0)
    low_side = jnp.where(sy == 0, EDGE, 0)
    high_side = jnp.where(sy == n_sy - 1, EDGE + ny, wide)
    within = jnp.logical_and(height >= low_side, height < high_side)
    low_row = jnp.where(sx == 0, DEPTH, 0)
    high_row = jnp.where(sx == n_sx - 1, DEPTH + nx, nx + 2 * DEPTH)

    def around(ref, t, x):
        here = ref[t, x]
        return here, (
            ref[t, x + 1], ref[t, x - 1],
            pltpu.roll(here, wide - 1, 0), pltpu.roll(here, 1, 0),
            pltpu.roll(here, nz - 1, 1), pltpu.roll(here, 1, 1),
        )

    def around_part(ref, t, x, size):
        low = EDGE - (size - ny) // 2
        part = pl.ds(low, size)
        here = ref[t, x, part, :]
        return here, (
            ref[t, x + 1, part, :], ref[t, x - 1, part, :],
            ref[t, x, pl.ds(low + 1, size), :], ref[t, x, pl.ds(low - 1, size), :],
            pltpu.roll(here, nz - 1, 1), pltpu.roll(here, 1, 1),
        )

    def beside(ref, t, x, g):
        here, sides = around_part(ref, t, x, g[0].shape[0])
        terms = [g[j] * sides[j] for j in range(6)]
        return here, (terms[0] + terms[1]) + (terms[2] + terms[3]) + (terms[4] + terms[5])

    def faces(x):
        return [face[j, x, win, :] for j in range(6)]

    def faces_mid(x):
        return [face[j, x, mid, :] for j in range(6)]

    def couple(here, sides, col):
        sides = list(sides)
        top, bottom = col == nz - 1, col == 0
        sides[4] = jnp.where(top, 0.0, sides[4])
        sides[5] = jnp.where(bottom, 0.0, sides[5])
        g = [0.5 * (here + side) for side in sides]
        whole = (g[0] + g[1]) + (g[2] + g[3]) + (g[4] + g[5])
        g[4] = jnp.where(top, 0.0, g[4])
        g[5] = jnp.where(bottom, 0.0, g[5])
        return g, whole

    def coefficients_mid(x):
        g, whole = couple(*around_part(kap, 0, x, ny), column[:ny])
        coupling[x, mid, :] = whole
        for j in range(6):
            face[j, x, mid, :] = g[j]
        for level in range(2):
            factor[level, x, mid, :] = relax_weight / (1.0 + (2.0 ** level) * whole)

    def coefficients(x):
        g, whole = couple(*around(kap, 0, x), column)
        coupling[x] = whole
        inside = jnp.logical_and(within, jnp.logical_and(x >= low_row, x < high_row))
        for j in range(6):
            face[j, x] = g[j]
        for level in range(4):
            factor[level, x] = jnp.where(inside, relax_weight / (1.0 + (2.0 ** level) * whole), 0.0)

    def phase(body, edge, name):
        for i in range(edge):
            body(DEPTH + i)
            body(DEPTH + nx - 1 - i)
        send(name, X_FACES)

        def step(x, carry):
            body(x)
            return carry

        lax.fori_loop(DEPTH + edge, DEPTH + nx - edge, step, 0, unroll=nx // 2 - edge)
        send(name, REST)

    wait("kappa")
    rows(coefficients_mid, 0)
    wait("init")
    arrive(T_INIT)

    def sweep_first(x):
        g, f = faces_mid(x), factor[0, x, mid, :]
        running = before[x - DEPTH]
        for t in range(steps):
            here, near = beside(ini, t, x, g)
            running = keep_weight * here + f * (src[t, x, mid, :] + near + running)
            first[t, x, mid, :] = running

    phase(sweep_first, 1, "first")
    pass_on(T_LAST)
    wait("kappa_far")
    rows(coefficients, 5)
    send("first_far")
    wait("first")

    def down_one(x):
        g, f, c = faces_mid(x), factor[0, x, mid, :], coupling[x, mid, :]
        f_one = factor[1, x, mid, :]
        diagonal = 1.0 + c
        earlier = None
        ahead_value = None
        running = None
        pair_zero = None
        for m in range(2):
            both = None
            for t in (2 * m, 2 * m + 1):
                here, near = beside(first, t, x, g)
                supply = src[t, x, mid, :] + near
                value = supply - diagonal * here
                if earlier is not None:
                    value = value + earlier
                both = value if both is None else both + value
                ahead_value = keep_weight * here + f * (supply if ahead_value is None else supply + ahead_value)
                earlier = here
            running = f_one * both if running is None else f_one * (both + running)
            err[m, x, mid, :] = running
            pair_zero = running if m == 0 else pair_zero
        both = pair_zero + running
        pair[1, x, mid, :] = both
        pair[0, x, mid, :] = both + at_zero * ((f_one + f_one * f_one) * earlier)
        pair[2, x, mid, :] = at_zero * running
        guess[x - DEPTH] = ahead_value

    phase(down_one, 2, "pair")
    pass_on(T_ONE)
    pass_on(T_ZERO)
    send("err")
    arrive(T_LAST)

    @pl.when(tm > 0)
    def _():
        send("last")

    wait("pair")

    def down_two(x):
        here, near = beside(pair, 0, x, faces(x))
        value = 0.25 * (1.0 + 2.0 * coupling[x, win, :]) * here + 2.0 * near + pair[2, x, win, :]
        fr[0, x, win, :] = factor[2, x, win, :] * value

    rows(down_two, 1)

    def down_three(x):
        g, c = faces_mid(x), coupling[x, mid, :]
        here, near = beside(fr, 0, x, g)
        value = 0.25 * (1.0 + 4.0 * c) * here + 4.0 * near
        here, near = beside(pair, 1, x, g)
        base = factor[2, x, mid, :] * (0.25 * (1.0 + 2.0 * c) * here + 2.0 * near)
        mine[x - DEPTH] = value + at_zero * base

    def part_rows(body, part):
        low, size = thirds[part]

        def step(x, carry):
            body(x)
            return carry

        lax.fori_loop(DEPTH + low, DEPTH + low + size, step, 0, unroll=size)

    for part in range(3):
        part_rows(down_three, part)
        across(T_MINE, part).start()
    pass_on(T_GUESS)
    arrive(T_ONE)

    @pl.when(tm > 0)
    def _():
        send("prev_one")

    arrive(T_ZERO)

    @pl.when(tm > 0)
    def _():
        send("prev_zero")

    def add_up(x):
        rhs3[0, x, mid, :] = mine[x - DEPTH] + theirs[x - DEPTH]

    for part in range(2):
        across(T_MINE, part).wait_recv()
        part_rows(add_up, part)
        send("rhs3", ((2 * part - 1, 0), (2 * part - 1, -1), (2 * part - 1, 1)))
    across(T_MINE, 2).wait_recv()
    part_rows(add_up, 2)
    send("rhs3", ((0, -1), (0, 1)))

    wait("err")
    wait("first_far")

    @pl.when(tm > 0)
    def _():
        wait("last")
        wait("prev_one")
        wait("prev_zero")

    def gather_far(x):
        f = factor[1, x]
        sums[0, x] = err[0, x] + err[1, x] + (f + f * f) * last[0, x]
        sums[1, x] = prev[0, x] + prev[1, x]

    rows(gather_far, 5)

    def level_two(x):
        g, f, weight = faces(x), factor[2, x, win, :], 0.25 * (1.0 + 2.0 * coupling[x, win, :])
        here, near = beside(sums, 0, x, g)
        err2[0, x, win, :] = f * (weight * here + 2.0 * near + prev[1, x, win, :])
        here, near = beside(sums, 1, x, g)
        err2[1, x, win, :] = f * (weight * here + 2.0 * near)

    rows(level_two, 4)

    def own_errors(x):
        f = factor[1, x, win, :]
        carried = f * last[0, x, win, :]
        return err[0, x, win, :] + carried, err[1, x, win, :] + f * carried

    def fix_two(x):
        g, f = faces(x), factor[2, x, win, :]
        own, near = beside(err2, 0, x, g)
        past, near_past = beside(err2, 1, x, g)
        value = (2.0 - relax_weight) * own + f * (4.0 * near + past)
        value_past = (2.0 - relax_weight) * past + 4.0 * (f * near_past)
        zero, first_one = own_errors(x)
        fix[0, x, win, :] = zero + value
        fix[1, x, win, :] = first_one + value
        fix[2, x, win, :] = prev[0, x, win, :] + value_past
        fix[3, x, win, :] = prev[1, x, win, :] + value_past

    rows(fix_two, 3)

    def fix_one(x):
        g, f = faces(x), factor[1, x, win, :]
        here, near = [], []
        for i in range(4):
            a, b = beside(fix, i, x, g)
            here.append(a)
            near.append(keep_weight * a + 2.0 * (f * b))
        zero, first_one = own_errors(x)
        value = near[0] + zero + f * here[3]
        vee[0, x, win, :] = value
        vee[1, x, win, :] = near[1] + first_one + f * (value - zero)
        value = near[2] + prev[0, x, win, :]
        vee[2, x, win, :] = value
        vee[3, x, win, :] = near[3] + prev[1, x, win, :] + f * (value - prev[0, x, win, :])

    rows(fix_one, 2)
    for name in NAMES:
        if name in ("last", "prev_one", "prev_zero"):
            @pl.when(tm > 0)
            def _(name=name):
                wait_sent(name)
        elif name != "rhs3":
            wait_sent(name)

    @pl.when(tm == 0)
    def _():
        for which in (T_INIT, T_LAST, T_ONE, T_ZERO):
            for part in range(2):
                across(which, part).wait_send()

    for part in range(3):
        across(T_MINE, part).wait_send()

    wait("source")
    wait("rhs3")

    def coarse_one(x):
        one[0, x] = factor[3, x] * rhs3[0, x]

    rows(coarse_one, 5)

    def coarse_two(x):
        here, near = beside(one, 0, x, faces(x))
        err3[0, x, win, :] = keep_weight * here + factor[3, x, win, :] * (rhs3[0, x, win, :] + 8.0 * near)

    rows(coarse_two, 4)

    def up_two(x):
        f = factor[2, x, win, :]
        here, near = beside(err3, 0, x, faces(x))
        value = keep_weight * here + 4.0 * (f * near)
        wave[0, x, win, :] = value + at_one * (f * here)
        wave[1, x, win, :] = value

    rows(up_two, 3)

    def up_one(x):
        g, f = faces(x), factor[1, x, win, :]
        here, near = beside(wave, 0, x, g)
        past, near_past = beside(wave, 1, x, g)
        own = keep_weight * here + 2.0 * (f * near)
        shadow = at_one * (keep_weight * past + 2.0 * (f * near_past))
        zero = own + at_one * (f * past)
        gain = (vee[0, x, win, :] + zero, vee[1, x, win, :] + own + f * zero)
        for t in range(steps):
            total[t, x, win, :] = first[t, x, win, :] + gain[t // 2]
        vee[2, x, win, :] = vee[2, x, win, :] + shadow
        vee[3, x, win, :] = vee[3, x, win, :] + shadow + f * shadow

    rows(up_one, 2)

    def up_zero(x):
        g, f = faces(x), factor[0, x, win, :]
        running = last[0, x, win, :] + vee[3, x, win, :]
        for t in range(steps):
            here, near = beside(total, t, x, g)
            running = keep_weight * here + f * (src[t, x, win, :] + near + running)
            sol[t, x, win, :] = running

    rows(up_zero, 1)
    arrive(T_GUESS)

    def finish(x):
        g, f = faces_mid(x), factor[0, x, mid, :]
        diagonal = 1.0 + coupling[x, mid, :]
        lifted = []
        for i in (2, 3):
            here, near = beside(vee, i, x, g)
            lifted.append(keep_weight * here + f * near)
        earlier = ahead[x - DEPTH] + (1.0 + f) * (f * f * lifted[0] + lifted[1])
        for t in range(steps):
            here, near = beside(sol, t, x, g)
            sol_out[t, x - DEPTH] = here
            res_out[t, x - DEPTH] = src[t, x, mid, :] + earlier - (diagonal * here - near)
            earlier = here

    rows(finish, 0)

    wait_sent("rhs3")

    @pl.when(tm == 0)
    def _():
        for part in range(2):
            across(T_GUESS, part).wait_send()


def wide_scratch(steps, nx, ny, nz):
    f32, dma = jnp.float32, pltpu.SemaphoreType.DMA
    depths = (1, steps, steps, steps, 3, 2, 1, 2, 2, 1, 1, 1, 1, 2, 2, 4, 4, steps, steps, 6)
    large = (nx + 2 * DEPTH, ny + 2 * EDGE, nz)
    scratch = [pltpu.VMEM((d,) + large, f32) for d in depths]
    scratch += [pltpu.VMEM(large, f32), pltpu.VMEM((4,) + large, f32)]
    scratch += [pltpu.VMEM((nx, ny, nz), f32)] * 5
    scratch += [dma((len(NAMES), 12)), dma((len(NAMES), 12)), dma((6, 3)), dma((6, 3)), dma((3,))]
    return scratch


def store(one, two, one_hbm, two_hbm, sem):
    copies = [pltpu.make_async_copy(one, one_hbm, sem.at[0]), pltpu.make_async_copy(two, two_hbm, sem.at[1])]
    for copy in copies:
        copy.start()
    for copy in copies:
        copy.wait()


def solution(mesh):
    n_tm, n_sx, n_sy = (mesh.shape[axis] for axis in ("tm", "sx", "sy"))
    f32 = jnp.float32

    def per_device(heat_source, conductivity, initial_iterate):
        steps, nx, ny, nz = heat_source.shape
        depth = (1, steps, steps, steps // 2, 1, 1, 1, steps // 2, steps, steps, 1, 1, 1, 1)
        scratch = [pltpu.VMEM((d, nx + 2, ny, nz), f32) for d in depth]
        scratch += [pltpu.VMEM((2, d, nx, nz), f32) for d in depth] * 2
        cells = (nx, ny, nz)
        dma = pltpu.SemaphoreType.DMA
        scratch += [
            pltpu.VMEM((steps,) + cells, f32),
            pltpu.VMEM((steps,) + cells, f32),
            pltpu.VMEM((7,) + cells, f32),
            pltpu.VMEM(cells, f32),
            pltpu.VMEM((steps // 2,) + cells, f32),
            pltpu.VMEM(cells, f32),
            pltpu.VMEM(cells, f32),
            pltpu.VMEM(cells, f32),
            pltpu.VMEM(cells, f32),
            pltpu.VMEM((2,) + cells, f32),
            pltpu.VMEM((6,) + cells, f32),
            pltpu.VMEM(cells, f32),
            pltpu.VMEM((4,) + cells, f32),
            dma((FIELDS, 4)), dma((FIELDS, 4)), dma((7, 2)), dma((7, 2)),
            dma((2,)), dma((2,)), dma((2,)), dma((2,)), dma((5,)),
        ]
        field = jax.ShapeDtypeStruct(heat_source.shape, f32)
        small = n_tm == 2 and steps == 4 and nx >= 2 * DEPTH and ny >= EDGE and ny % EDGE == 0
        if small:
            scratch = wide_scratch(steps, nx, ny, nz)
        one, two = pl.pallas_call(
            functools.partial(wide_kernel, n_sx, n_sy) if small else functools.partial(kernel, n_tm, n_sx, n_sy),
            out_shape=(pltpu.VMEM(heat_source.shape, f32),) * 2,
            in_specs=[pl.BlockSpec(memory_space=pltpu.HBM)] * 3,
            out_specs=(pl.BlockSpec(memory_space=pltpu.VMEM),) * 2,
            scratch_shapes=scratch,
            compiler_params=pltpu.CompilerParams(
                collective_id=0, has_side_effects=True, vmem_limit_bytes=40000000
            ),
            name="vcycle",
        )(*(pltpu.with_memory_space_constraint(x, pltpu.HBM) for x in (heat_source, conductivity, initial_iterate)))
        return pl.pallas_call(
            store,
            out_shape=(field, field),
            in_specs=[pl.BlockSpec(memory_space=pltpu.VMEM)] * 2,
            out_specs=(pl.BlockSpec(memory_space=pltpu.HBM),) * 2,
            scratch_shapes=[dma((2,))],
            name="store",
        )(*(pltpu.with_memory_space_constraint(x, pltpu.VMEM) for x in (one, two)))

    placed = (P("tm", "sx", "sy", None), P("sx", "sy", None), P("tm", "sx", "sy", None))
    return jax.shard_map(
        per_device,
        mesh=mesh,
        in_specs=placed,
        out_specs=(P("tm", "sx", "sy", None), P("tm", "sx", "sy", None)),
        check_vma=False,
    )
```

```python
import functools

import jax
import jax.numpy as jnp
from jax import lax
from jax.experimental import pallas as pl
from jax.experimental.pallas import tpu as pltpu
from jax.sharding import PartitionSpec as P

relax_weight = 0.8
keep_weight = 1.0 - relax_weight
MESH = pl.DeviceIdType.MESH

KAPPA, INIT, FIRST, ERR1, ERR2, ERR3, FIX2, FIX1, SUM0, SOL, PART, PAIR, PART2, PAIR2 = range(14)
FIELDS = 14
P_INIT, P_FIRST, P_ERR1, P_ERR2, P_FIX1, P_SUM0, P_SOL = range(7)
XLO, XHI, YLO, YHI = range(4)


def kernel(n_tm, n_sx, n_sy, hs_hbm, k_hbm, in_hbm, sol_hbm, res_hbm, *scratch):
    fields = scratch[:FIELDS]
    yrecv = scratch[FIELDS:2 * FIELDS]
    ysend = scratch[2 * FIELDS:3 * FIELDS]
    (hs, res, before, second, rhs1, rhs2, rhs3, mine, theirs, chain,
     face, coupling, factor, send_sem, recv_sem, tsend, trecv,
     qsend, qrecv, csend, crecv, local) = scratch[3 * FIELDS:]
    steps, nx, ny, nz = hs.shape
    tm, sx, sy = lax.axis_index("tm"), lax.axis_index("sx"), lax.axis_index("sy")
    has = (sx > 0, sx < n_sx - 1, sy > 0, sy < n_sy - 1)
    partner = tm + 1 - 2 * lax.rem(tm, 2)
    even = lax.rem(tm, 2) == 0

    loads = [
        pltpu.make_async_copy(k_hbm, fields[KAPPA].at[0, pl.ds(1, nx)], local.at[0]),
        pltpu.make_async_copy(in_hbm, fields[INIT].at[:, pl.ds(1, nx)], local.at[1]),
        pltpu.make_async_copy(hs_hbm, hs, local.at[2]),
    ]
    for load in loads:
        load.start()

    barrier = pltpu.get_barrier_semaphore()
    greet = [
        (has[XLO], {"sx": sx - 1}), (has[XHI], {"sx": sx + 1}),
        (has[YLO], {"sy": sy - 1}), (has[YHI], {"sy": sy + 1}),
        (tm > 0, {"tm": tm - 1}), (tm < n_tm - 1, {"tm": tm + 1}),
    ]
    if n_tm == 2:
        greet += [
            (has[XLO], {"tm": partner, "sx": sx - 1}), (has[XHI], {"tm": partner, "sx": sx + 1}),
            (has[YLO], {"tm": partner, "sy": sy - 1}), (has[YHI], {"tm": partner, "sy": sy + 1}),
        ]
    if n_tm > 2:
        greet += [(tm > 1, {"tm": tm - 2}), (tm < n_tm - 2, {"tm": tm + 2})]
    count = jnp.int32(0)
    for there, device in greet:
        count = count + jnp.where(there, 1, 0)

        @pl.when(there)
        def _(device=device):
            pl.semaphore_signal(barrier, inc=1, device_id=device, device_id_type=MESH)

    pl.semaphore_wait(barrier, count)

    def face_copy(i, side, pair=False):
        field = fields[i]
        to = i + 1 if pair else i
        land = fields[to]
        if side == XLO:
            if i == INIT:
                src = in_hbm.at[:, pl.ds(0, 1)]
            elif i == KAPPA:
                src = k_hbm.at[pl.ds(0, 1)]
            else:
                src = field.at[:, pl.ds(1, 1)]
            dst, device = land.at[:, pl.ds(nx + 1, 1)], {"sx": sx - 1}
        elif side == XHI:
            if i == INIT:
                src = in_hbm.at[:, pl.ds(nx - 1, 1)]
            elif i == KAPPA:
                src = k_hbm.at[pl.ds(nx - 1, 1)]
            else:
                src = field.at[:, pl.ds(nx, 1)]
            dst, device = land.at[:, pl.ds(0, 1)], {"sx": sx + 1}
        elif side == YLO:
            src, dst, device = ysend[i].at[0], yrecv[to].at[1], {"sy": sy - 1}
        else:
            src, dst, device = ysend[i].at[1], yrecv[to].at[0], {"sy": sy + 1}
        if i == KAPPA and side in (XLO, XHI):
            dst = field.at[0, pl.ds(nx + 1 if side == XLO else 0, 1)]
        if pair:
            device["tm"] = partner
        return pltpu.make_async_remote_copy(
            src_ref=src, dst_ref=dst, send_sem=send_sem.at[to, side],
            recv_sem=recv_sem.at[to, side], device_id=device, device_id_type=MESH)

    def send_faces(i, sides, pair=False):
        for side in sides:
            @pl.when(has[side])
            def _(side=side):
                face_copy(i, side).start()
                if pair:
                    face_copy(i, side, True).start()

    def wait_faces(i, pair=False):
        for side in (YLO, YHI, XLO, XHI):
            @pl.when(has[side ^ 1])
            def _(side=side):
                face_copy(i, side, pair).wait_recv()

    half = nx // 2
    halves = (pl.ds(0, half), pl.ds(half, nx - half))

    def last_copy(i, part):
        field = fields[lasts[i]]
        if i == P_INIT:
            src = in_hbm.at[steps - 1, halves[part]]
        else:
            src = field.at[field.shape[0] - 1, (pl.ds(1, half), pl.ds(1 + half, nx - half))[part]]
        return pltpu.make_async_remote_copy(
            src_ref=src, dst_ref=before.at[i, halves[part]],
            send_sem=tsend.at[i, part], recv_sem=trecv.at[i, part],
            device_id={"tm": tm + 1}, device_id_type=MESH)

    lasts = (INIT, FIRST, ERR1, ERR2, FIX1, SUM0, SOL)

    def send_last(i, part):
        @pl.when(tm < n_tm - 1)
        def _():
            last_copy(i, part).start()

    def wait_last(i, parts=(0, 1)):
        @pl.when(tm > 0)
        def _():
            for part in parts:
                last_copy(i, part).wait_recv()

    send_faces(KAPPA, (XLO, XHI))
    send_faces(INIT, (XLO, XHI))
    send_last(P_INIT, 0)
    send_last(P_INIT, 1)

    def over_rows(body, by=8, start=0, stop=nx):
        def step(x, carry):
            body(x)
            return carry

        lax.fori_loop(start, stop, step, 0, unroll=by)

    def phase(body, i, send_part=None, pair=False, awaited=None):
        if awaited is not None:
            wait_last(awaited, (0,))
        body(0)
        if awaited is None:
            body(nx - 1)
            send_faces(i, (XLO, XHI), pair)
        else:
            send_faces(i, (XLO,), pair)
        over_rows(body, half - 1, 1, half)
        if send_part is not None:
            send_part(0)
        if awaited is not None:
            wait_last(awaited, (1,))
            body(nx - 1)
            send_faces(i, (XHI,), pair)
        over_rows(body, half - 1, half, nx - 1)
        send_faces(i, (YLO, YHI), pair)
        if send_part is not None:
            send_part(1)

    def put_faces(i, t, x, value):
        ysend[i][0, t, pl.ds(x, 1), :] = value[0:1, :]
        ysend[i][1, t, pl.ds(x, 1), :] = value[ny - 1:ny, :]

    def put(i, t, x, value):
        fields[i][t, x + 1] = value
        put_faces(i, t, x, value)

    loads[0].wait()
    loads[1].wait()

    def pack(x):
        put_faces(KAPPA, 0, x, fields[KAPPA][0, x + 1])
        for t in range(steps):
            put_faces(INIT, t, x, fields[INIT][t, x + 1])

    over_rows(pack)
    send_faces(KAPPA, (YLO, YHI))
    send_faces(INIT, (YLO, YHI))

    @pl.when(sx == 0)
    def _():
        for i in range(FIELDS):
            for t in range(fields[i].shape[0]):
                fields[i][t, 0] = jnp.zeros((ny, nz), jnp.float32)

    @pl.when(sx == n_sx - 1)
    def _():
        for i in range(FIELDS):
            for t in range(fields[i].shape[0]):
                fields[i][t, nx + 1] = jnp.zeros((ny, nz), jnp.float32)

    @pl.when(sy == 0)
    def _():
        for i in range(FIELDS):
            yrecv[i][0] = jnp.zeros(yrecv[i].shape[1:], jnp.float32)

    @pl.when(sy == n_sy - 1)
    def _():
        for i in range(FIELDS):
            yrecv[i][1] = jnp.zeros(yrecv[i].shape[1:], jnp.float32)

    @pl.when(tm == 0)
    def _():
        def clear(x):
            for i in range(7):
                before[i, x] = jnp.zeros((ny, nz), jnp.float32)

        over_rows(clear, 1)

    row = lax.broadcasted_iota(jnp.int32, (ny, nz), 0)
    column = lax.broadcasted_iota(jnp.int32, (ny, nz), 1)

    def around(i, t, x):
        field = fields[i]
        here = field[t, x + 1]
        return here, (
            field[t, x + 2],
            field[t, x],
            jnp.where(row == ny - 1, yrecv[i][1, t, pl.ds(x, 1), :], pltpu.roll(here, ny - 1, 0)),
            jnp.where(row == 0, yrecv[i][0, t, pl.ds(x, 1), :], pltpu.roll(here, 1, 0)),
            pltpu.roll(here, nz - 1, 1),
            pltpu.roll(here, 1, 1),
        )

    def beside(i, t, x, g):
        here, sides = around(i, t, x)
        terms = [g[j] * sides[j] for j in range(6)]
        return here, (terms[0] + terms[1]) + (terms[2] + terms[3]) + (terms[4] + terms[5])

    def faces_at(x):
        return [face[j, x] for j in range(6)]

    wait_faces(KAPPA)

    def coefficients(x):
        here, sides = around(KAPPA, 0, x)
        sides = list(sides)
        sides[4] = jnp.where(column == nz - 1, 0.0, sides[4])
        sides[5] = jnp.where(column == 0, 0.0, sides[5])
        g = [0.5 * (here + side) for side in sides]
        total = (g[0] + g[1]) + (g[2] + g[3]) + (g[4] + g[5])
        coupling[x] = total
        g[4] = jnp.where(column == nz - 1, 0.0, g[4])
        g[5] = jnp.where(column == 0, 0.0, g[5])
        for j in range(6):
            face[j, x] = g[j]
        for level in range(4):
            factor[level, x] = relax_weight / (1.0 + (2.0 ** level) * total)

    over_rows(coefficients)
    loads[2].wait()
    wait_faces(INIT)

    def sweep_first(x):
        g, f = faces_at(x), factor[0, x]
        running = before[P_INIT, x]
        for t in range(steps):
            here, near = beside(INIT, t, x, g)
            running = keep_weight * here + f * (hs[t, x] + near + running)
            put(FIRST, t, x, running)

    phase(sweep_first, FIRST, functools.partial(send_last, P_FIRST), awaited=P_INIT)
    wait_faces(FIRST)

    def down_one(x):
        g, diagonal, f = faces_at(x), 1.0 + coupling[x], factor[1, x]
        earlier = before[P_FIRST, x]
        running = None
        for m in range(steps // 2):
            total = None
            for t in (2 * m, 2 * m + 1):
                here, near = beside(FIRST, t, x, g)
                value = hs[t, x] + earlier - (diagonal * here - near)
                total = value if total is None else total + value
                earlier = here
            rhs1[m, x] = total
            running = f * total if running is None else f * (total + running)
            put(ERR1, m, x, running)

    phase(down_one, ERR1, functools.partial(send_last, P_ERR1), awaited=P_FIRST)
    wait_faces(ERR1)
    wait_last(P_ERR1)

    def down_two(x):
        g, diagonal, f = faces_at(x), 1.0 + 2.0 * coupling[x], factor[2, x]
        earlier = before[P_ERR1, x]
        total = None
        for t in range(2):
            here, near = beside(ERR1, t, x, g)
            value = rhs1[t, x] + earlier - (diagonal * here - 2.0 * near)
            total = value if total is None else total + value
            earlier = here
        rhs2[x] = total
        put(ERR2, 0, x, f * total)

    phase(down_two, ERR2, functools.partial(send_last, P_ERR2))
    wait_faces(ERR2)
    if n_tm > 2:
        wait_last(P_ERR2)

    def down_three(x):
        g, diagonal = faces_at(x), 1.0 + 4.0 * coupling[x]
        here, near = beside(ERR2, 0, x, g)
        earlier = here + before[P_ERR2, x] if n_tm > 2 else here
        value = rhs2[x] + jnp.where(even, earlier, 0.0) - (diagonal * here - 4.0 * near)
        mine[x] = value
        if n_tm == 2:
            put(PART, 0, x, factor[3, x] * value)

    def swap(part):
        return pltpu.make_async_remote_copy(
            src_ref=mine.at[halves[part]], dst_ref=theirs.at[halves[part]],
            send_sem=qsend.at[part], recv_sem=qrecv.at[part],
            device_id={"tm": partner}, device_id_type=MESH)

    if n_tm == 2:
        phase(down_three, PART, lambda part: swap(part).start(), True)
        wait_faces(PART)

        def part_two(x):
            here, near = beside(PART, 0, x, faces_at(x))
            put(PART2, 0, x, keep_weight * here + factor[3, x] * (mine[x] + 8.0 * near))

        phase(part_two, PART2, None, True)
    else:
        over_rows(down_three)
        swap(0).start()
        swap(1).start()
    swap(0).wait_recv()
    swap(1).wait_recv()

    def chain_copy(i, field):
        src = field.at[0, pl.ds(1, nx)] if i == 0 else second
        return pltpu.make_async_remote_copy(
            src_ref=src, dst_ref=chain.at[i], send_sem=csend.at[i],
            recv_sem=crecv.at[i], device_id={"tm": tm + 2}, device_id_type=MESH)

    def chain_wait(i):
        if n_tm > 2:
            @pl.when(tm > 1)
            def _():
                chain_copy(i, fields[ERR3]).wait_recv()

            @pl.when(tm < 2)
            def _():
                def clear(x):
                    chain[i, x] = jnp.zeros((ny, nz), jnp.float32)

                over_rows(clear, 1)

    def chain_send(i):
        if n_tm > 2:
            @pl.when(tm < n_tm - 2)
            def _():
                chain_copy(i, fields[ERR3]).start()

    chain_wait(0)

    def coarse_one(x):
        total = mine[x] + theirs[x]
        rhs3[x] = total
        if n_tm > 2:
            total = total + chain[0, x]
        value = factor[3, x] * total
        if n_tm > 2:
            put(ERR3, 0, x, value)
        else:
            fields[ERR3][0, x + 1] = value

    if n_tm > 2:
        phase(coarse_one, ERR3)
        chain_send(0)
        wait_faces(ERR3)
    else:
        over_rows(coarse_one)
        wait_faces(PART, True)
        for edge in (0, nx + 1):
            fields[ERR3][0, edge] = fields[PART][0, edge] + fields[PAIR][0, edge]
        for edge in range(2):
            yrecv[ERR3][edge, 0] = yrecv[PART][edge, 0] + yrecv[PAIR][edge, 0]
    if n_tm == 2:
        wait_last(P_ERR2)
    chain_wait(1)

    def coarse_two(x):
        here, near = beside(ERR3, 0, x, faces_at(x))
        total = rhs3[x] + 8.0 * near
        if n_tm > 2:
            total = total + chain[1, x]
        value = keep_weight * here + factor[3, x] * total
        if n_tm > 2:
            second[x] = value
            earlier = jnp.where(even, chain[1, x], value)
        else:
            earlier = jnp.where(even, 0.0, value)
        mine_next[x] = before[P_ERR2, x] + earlier
        value = fields[ERR2][0, x + 1] + value
        if n_tm > 2:
            put(FIX2, 0, x, value)
        else:
            fields[FIX2][0, x + 1] = value

    mine_next = res.at[0]
    if n_tm > 2:
        phase(coarse_two, FIX2)
        chain_send(1)
        wait_faces(FIX2)
    else:
        over_rows(coarse_two)
        wait_faces(PART2)
        wait_faces(PART2, True)
        for edge in (0, nx + 1):
            fields[FIX2][0, edge] = fields[ERR2][0, edge] + (
                fields[PART2][0, edge] + fields[PAIR2][0, edge])
        for edge in range(2):
            yrecv[FIX2][edge, 0] = yrecv[ERR2][edge, 0] + (
                yrecv[PART2][edge, 0] + yrecv[PAIR2][edge, 0])

    def up_two(x):
        here, near = beside(FIX2, 0, x, faces_at(x))
        value = keep_weight * here + factor[2, x] * (rhs2[x] + 4.0 * near + mine_next[x])
        for m in range(2):
            put(FIX1, m, x, fields[ERR1][m, x + 1] + value)

    phase(up_two, FIX1, functools.partial(send_last, P_FIX1))
    wait_faces(FIX1)

    def up_one(x):
        g, f = faces_at(x), factor[1, x]
        running = before[P_FIX1, x]
        for m in range(2):
            here, near = beside(FIX1, m, x, g)
            running = keep_weight * here + f * (rhs1[m, x] + 2.0 * near + running)
            for t in (2 * m, 2 * m + 1):
                put(SUM0, t, x, fields[FIRST][t, x + 1] + running)

    phase(up_one, SUM0, functools.partial(send_last, P_SUM0), awaited=P_FIX1)
    wait_faces(SUM0)
    wait_last(P_SUM0)

    def up_zero(x):
        g, f = faces_at(x), factor[0, x]
        running = before[P_SUM0, x]
        for t in range(steps):
            here, near = beside(SUM0, t, x, g)
            running = keep_weight * here + f * (hs[t, x] + near + running)
            put(SOL, t, x, running)
            sol_hbm[t, x] = running

    phase(up_zero, SOL, functools.partial(send_last, P_SOL))
    wait_faces(SOL)
    wait_last(P_SOL)

    def last_defect(x):
        g, diagonal = faces_at(x), 1.0 + coupling[x]
        earlier = before[P_SOL, x]
        for t in range(steps):
            here, near = beside(SOL, t, x, g)
            res_hbm[t, x] = hs[t, x] + earlier - (diagonal * here - near)
            earlier = here

    over_rows(last_defect)

    for i in range(FIELDS):
        if i in ((PAIR, PAIR2, ERR3, FIX2) if n_tm == 2 else (PART, PAIR, PART2, PAIR2)):
            continue
        for side in (XLO, XHI, YLO, YHI):
            @pl.when(has[side])
            def _(i=i, side=side):
                face_copy(i, side).wait_send()
                if i in (PART, PART2):
                    face_copy(i, side, True).wait_send()

    @pl.when(tm < n_tm - 1)
    def _():
        for i in range(7):
            for part in range(2):
                last_copy(i, part).wait_send()

    swap(0).wait_send()
    swap(1).wait_send()
    if n_tm > 2:
        @pl.when(tm < n_tm - 2)
        def _():
            for i in range(2):
                chain_copy(i, fields[ERR3]).wait_send()


DEPTH = 6
EDGE = 8
REACH = 4
EXCHANGES = {
    "kappa": ("k", (0, 1), ()),
    "kappa_far": ("k", (1, 6), ((0, 5, 0, 5),)),
    "init": ("in", (0, 1), ()),
    "source": ("hs", (0, 1), ()),
    "first": ("first", (0, 1), ()),
    "first_far": ("first", (1, 2), ((0, 1, 0, 1),)),
    "pair": ("pair", (0, 2), ((0, 1, 0, 1),)),
    "pair_near": ("pair", (0, 1), ()),
    "err": ("err", (0, 5), ((0, 4, 0, 4),)),
    "last": ("last", (0, 5), ((0, 4, 0, 4),)),
    "prev_one": ("prev", (0, 5), ((0, 4, 0, 4),)),
    "prev_zero": ("prev", (0, 5), ((0, 4, 0, 4),)),
    "rhs3": ("rhs3", (0, 5), ((0, 4, 0, 4),)),
}
NAMES = tuple(EXCHANGES)
X_FACES = ((-1, 0), (1, 0))
REST = ((0, -1), (0, 1), (-1, -1), (-1, 1), (1, -1), (1, 1))
ALL = X_FACES + REST
T_INIT, T_LAST, T_ONE, T_ZERO, T_MINE, T_GUESS = range(6)


def wide_kernel(n_sx, n_sy, hs_hbm, k_hbm, in_hbm, sol_out, res_out,
                kap, ini, src, first, pair, err, last, prev, sums, fr, rhs3, one, err3, wave,
                err2, fix, vee, total, sol, face, coupling, factor,
                before, mine, theirs, guess, ahead,
                send_sem, recv_sem, tsend, trecv, local):
    nx, ny, nz = k_hbm.shape
    steps = in_hbm.shape[0]
    wide = ny + 2 * EDGE
    tm, sx, sy = lax.axis_index("tm"), lax.axis_index("sx"), lax.axis_index("sy")
    at_one = jnp.where(tm > 0, 1.0, 0.0)
    at_zero = 1.0 - at_one
    mid = pl.ds(EDGE, ny)
    win = pl.ds(EDGE - REACH, ny + 2 * REACH)
    inner = pl.ds(DEPTH, nx)
    homes = {"k": kap, "in": ini, "hs": src, "first": first, "pair": pair, "err": err,
             "last": last, "prev": prev, "rhs3": rhs3}

    loads = [
        pltpu.make_async_copy(k_hbm, kap.at[0, inner, mid], local.at[0]),
        pltpu.make_async_copy(in_hbm, ini.at[:, inner, mid], local.at[1]),
        pltpu.make_async_copy(hs_hbm, src.at[:, inner, mid], local.at[2]),
    ]
    for load in loads:
        load.start()

    def there(way, sign=1):
        ok = None
        for step, at, size in ((sign * way[0], sx, n_sx), (sign * way[1], sy, n_sy)):
            if step:
                here = at > 0 if step < 0 else at < size - 1
                ok = here if ok is None else jnp.logical_and(ok, here)
        return ok

    def target(way):
        device = {}
        if way[0]:
            device["sx"] = sx + way[0]
        if way[1]:
            device["sy"] = sy + way[1]
        return device

    barrier = pltpu.get_barrier_semaphore()
    count = jnp.int32(1)
    for way in ALL:
        count = count + jnp.where(there(way), 1, 0)

        @pl.when(there(way))
        def _(way=way):
            pl.semaphore_signal(barrier, inc=1, device_id=target(way), device_id_type=MESH)

    pl.semaphore_signal(barrier, inc=1, device_id={"tm": 1 - tm}, device_id_type=MESH)

    def rows(body, depth, by=None):
        def step(x, carry):
            body(x)
            return carry

        if by is None:
            by = (nx + 2 * depth) // (2 if depth else 1)
        lax.fori_loop(DEPTH - depth, DEPTH + nx + depth, step, 0, unroll=by)

    filled = ((kap, 6), (ini, 1), (src, 1), (first, 2), (pair, 2), (err, 5), (last, 5), (prev, 5), (rhs3, 5))
    plane = jnp.zeros((wide, nz), jnp.float32)
    strip = jnp.zeros((EDGE, nz), jnp.float32)

    def fill(edge_rows):
        for array, depth in filled:
            for t in range(array.shape[0]):
                for i in range(depth):
                    array[t, DEPTH - 1 - i if edge_rows < 0 else DEPTH + nx + i] = plane

    def fill_side(start):
        for array, depth in filled:
            def body(x):
                for t in range(array.shape[0]):
                    array[t, x, pl.ds(start, EDGE), :] = strip

            rows(body, depth, 2)

    @pl.when(sx == 0)
    def _():
        fill(-1)

    @pl.when(sx == n_sx - 1)
    def _():
        fill(1)

    @pl.when(sy == 0)
    def _():
        fill_side(0)

    @pl.when(sy == n_sy - 1)
    def _():
        fill_side(EDGE + ny)

    @pl.when(tm == 0)
    def _():
        def body(x):
            last[0, x] = plane
            prev[0, x] = plane
            prev[1, x] = plane

        rows(body, 5, 2)

        def empty(x):
            before[x - DEPTH] = jnp.zeros((ny, nz), jnp.float32)
            ahead[x - DEPTH] = jnp.zeros((ny, nz), jnp.float32)

        rows(empty, 0, 2)

    pl.semaphore_wait(barrier, count)

    def span(step, size, low, high):
        if step == 0:
            return 0, size, 0
        if step < 0:
            return low, high - low, size + low
        return size - high, high - low, -high

    def pieces(name, ways):
        kind, (low, high), corners = EXCHANGES[name]
        slot = 0
        for way in ALL:
            boxes = corners if way[0] and way[1] else ((low, high, low, high),)
            for box in boxes:
                if way in ways:
                    yield way, box, slot
                slot += 1

    def copy_of(name, way, box, slot):
        kind = EXCHANGES[name][0]
        land = homes[kind]
        fx, wx, tx = span(way[0], nx, box[0], box[1])
        fy, wy, ty = span(way[1], ny, box[2], box[3])
        steps_at = {"prev_zero": pl.ds(0, 1), "prev_one": pl.ds(1, 1),
                    "pair": pl.ds(0, 1), "pair_near": pl.ds(1, 2)}.get(name, slice(None))
        if kind == "k":
            source = land.at[0, pl.ds(DEPTH + fx, wx), pl.ds(EDGE + fy, wy)]
            dest = land.at[0, pl.ds(DEPTH + tx, wx), pl.ds(EDGE + ty, wy)]
        else:
            source = land.at[steps_at, pl.ds(DEPTH + fx, wx), pl.ds(EDGE + fy, wy)]
            dest = land.at[steps_at, pl.ds(DEPTH + tx, wx), pl.ds(EDGE + ty, wy)]
        number = NAMES.index(name)
        return pltpu.make_async_remote_copy(
            src_ref=source, dst_ref=dest, send_sem=send_sem.at[number, slot],
            recv_sem=recv_sem.at[number, slot], device_id=target(way), device_id_type=MESH)

    def send(name, ways=ALL):
        for way, box, slot in pieces(name, ways):
            @pl.when(there(way))
            def _(way=way, box=box, slot=slot):
                copy_of(name, way, box, slot).start()

    def wait(name):
        for way, box, slot in pieces(name, REST + X_FACES):
            @pl.when(there(way, -1))
            def _(way=way, box=box, slot=slot):
                copy_of(name, way, box, slot).wait_recv()

    def wait_sent(name):
        for way, box, slot in pieces(name, ALL):
            @pl.when(there(way))
            def _(way=way, box=box, slot=slot):
                copy_of(name, way, box, slot).wait_send()

    half = nx // 2
    ends = ((0, half), (half, nx - half))
    thirds = ((0, DEPTH - 1), (nx - DEPTH + 1, DEPTH - 1), (DEPTH - 1, nx - 2 * DEPTH + 2))

    def across(which, part):
        low, size = (thirds if which == T_MINE else ends)[part]
        near, far = pl.ds(low, size), pl.ds(DEPTH + low, size)
        source, dest = {
            T_INIT: lambda: (ini.at[steps - 1, far, mid], before.at[near]),
            T_LAST: lambda: (first.at[steps - 1, far, mid], last.at[0, far, mid]),
            T_ONE: lambda: (err.at[1, far, mid], prev.at[1, far, mid]),
            T_ZERO: lambda: (err.at[0, far, mid], prev.at[0, far, mid]),
            T_MINE: lambda: (mine.at[near], theirs.at[near]),
            T_GUESS: lambda: (guess.at[near], ahead.at[near]),
        }[which]()
        return pltpu.make_async_remote_copy(
            src_ref=source, dst_ref=dest, send_sem=tsend.at[which, part],
            recv_sem=trecv.at[which, part], device_id={"tm": 1 - tm}, device_id_type=MESH)

    def pass_on(which, parts=(0, 1)):
        @pl.when(tm == 0)
        def _():
            for part in parts:
                across(which, part).start()

    def arrive(which, parts=(0, 1)):
        @pl.when(tm > 0)
        def _():
            for part in parts:
                across(which, part).wait_recv()

    loads[0].wait()
    send("kappa")
    loads[1].wait()
    send("init")
    pass_on(T_INIT)
    loads[2].wait()
    send("source")
    send("kappa_far")

    column = lax.broadcasted_iota(jnp.int32, (wide, nz), 1)
    height = lax.broadcasted_iota(jnp.int32, (wide, nz), 0)
    low_side = jnp.where(sy == 0, EDGE, 0)
    high_side = jnp.where(sy == n_sy - 1, EDGE + ny, wide)
    within = jnp.logical_and(height >= low_side, height < high_side)
    low_row = jnp.where(sx == 0, DEPTH, 0)
    high_row = jnp.where(sx == n_sx - 1, DEPTH + nx, nx + 2 * DEPTH)

    def around(ref, t, x):
        here = ref[t, x]
        return here, (
            ref[t, x + 1], ref[t, x - 1],
            pltpu.roll(here, wide - 1, 0), pltpu.roll(here, 1, 0),
            pltpu.roll(here, nz - 1, 1), pltpu.roll(here, 1, 1),
        )

    def around_part(ref, t, x, size):
        low = EDGE - (size - ny) // 2
        part = pl.ds(low, size)
        here = ref[t, x, part, :]
        return here, (
            ref[t, x + 1, part, :], ref[t, x - 1, part, :],
            ref[t, x, pl.ds(low + 1, size), :], ref[t, x, pl.ds(low - 1, size), :],
            pltpu.roll(here, nz - 1, 1), pltpu.roll(here, 1, 1),
        )

    def beside(ref, t, x, g):
        here, sides = around_part(ref, t, x, g[0].shape[0])
        terms = [g[j] * sides[j] for j in range(6)]
        return here, (terms[0] + terms[1]) + (terms[2] + terms[3]) + (terms[4] + terms[5])

    def faces(x):
        return [face[j, x, win, :] for j in range(6)]

    def faces_mid(x):
        return [face[j, x, mid, :] for j in range(6)]

    def couple(here, sides, col):
        sides = list(sides)
        top, bottom = col == nz - 1, col == 0
        sides[4] = jnp.where(top, 0.0, sides[4])
        sides[5] = jnp.where(bottom, 0.0, sides[5])
        g = [0.5 * (here + side) for side in sides]
        whole = (g[0] + g[1]) + (g[2] + g[3]) + (g[4] + g[5])
        g[4] = jnp.where(top, 0.0, g[4])
        g[5] = jnp.where(bottom, 0.0, g[5])
        return g, whole

    def coefficients_mid(x):
        g, whole = couple(*around_part(kap, 0, x, ny), column[:ny])
        coupling[x, mid, :] = whole
        for j in range(6):
            face[j, x, mid, :] = g[j]
        for level in range(2):
            factor[level, x, mid, :] = relax_weight / (1.0 + (2.0 ** level) * whole)

    def coefficients(x):
        g, whole = couple(*around(kap, 0, x), column)
        coupling[x] = whole
        inside = jnp.logical_and(within, jnp.logical_and(x >= low_row, x < high_row))
        for j in range(6):
            face[j, x] = g[j]
        for level in range(4):
            factor[level, x] = jnp.where(inside, relax_weight / (1.0 + (2.0 ** level) * whole), 0.0)

    def phase(body, edge, name, passing=()):
        for i in range(edge):
            body(DEPTH + i)
            body(DEPTH + nx - 1 - i)
        names = (name, "pair_near") if name == "pair" else (name,)
        for each in names:
            send(each, X_FACES)

        def step(x, carry):
            body(x)
            return carry

        if passing:
            for part, (low, high) in enumerate(((edge, half), (half, nx - edge))):
                lax.fori_loop(DEPTH + low, DEPTH + high, step, 0, unroll=high - low)
                for which in passing:
                    pass_on(which, (part,))
        else:
            lax.fori_loop(DEPTH + edge, DEPTH + nx - edge, step, 0, unroll=nx // 2 - edge)
        for each in names:
            send(each, REST)

    wait("kappa")
    rows(coefficients_mid, 0)
    wait("init")
    arrive(T_INIT)

    def sweep_first(x):
        g, f = faces_mid(x), factor[0, x, mid, :]
        running = before[x - DEPTH]
        for t in range(steps):
            here, near = beside(ini, t, x, g)
            running = keep_weight * here + f * (src[t, x, mid, :] + near + running)
            first[t, x, mid, :] = running

    phase(sweep_first, 1, "first")
    pass_on(T_LAST)
    wait("kappa_far")
    rows(coefficients, 5)
    send("first_far")
    wait("first")

    def down_one(x):
        g, f, c = faces_mid(x), factor[0, x, mid, :], coupling[x, mid, :]
        f_one = factor[1, x, mid, :]
        diagonal = 1.0 + c
        earlier = None
        ahead_value = None
        running = None
        pair_zero = None
        for m in range(2):
            both = None
            for t in (2 * m, 2 * m + 1):
                here, near = beside(first, t, x, g)
                supply = src[t, x, mid, :] + near
                value = supply - diagonal * here
                if earlier is not None:
                    value = value + earlier
                both = value if both is None else both + value
                ahead_value = keep_weight * here + f * (supply if ahead_value is None else supply + ahead_value)
                earlier = here
            running = f_one * both if running is None else f_one * (both + running)
            err[m, x, mid, :] = running
            pair_zero = running if m == 0 else pair_zero
        both = pair_zero + running
        pair[1, x, mid, :] = both
        pair[0, x, mid, :] = both + at_zero * ((f_one + f_one * f_one) * earlier)
        pair[2, x, mid, :] = at_zero * running
        guess[x - DEPTH] = ahead_value

    phase(down_one, 2, "pair", (T_ONE, T_ZERO))
    send("err")
    arrive(T_LAST)

    @pl.when(tm > 0)
    def _():
        send("last")

    wait("pair")
    wait("pair_near")

    def down_two(x):
        here, near = beside(pair, 0, x, faces(x))
        value = 0.25 * (1.0 + 2.0 * coupling[x, win, :]) * here + 2.0 * near + pair[2, x, win, :]
        fr[0, x, win, :] = factor[2, x, win, :] * value

    rows(down_two, 1)

    def down_three(x):
        g, c = faces_mid(x), coupling[x, mid, :]
        here, near = beside(fr, 0, x, g)
        value = 0.25 * (1.0 + 4.0 * c) * here + 4.0 * near
        here, near = beside(pair, 1, x, g)
        base = factor[2, x, mid, :] * (0.25 * (1.0 + 2.0 * c) * here + 2.0 * near)
        mine[x - DEPTH] = value + at_zero * base

    def part_rows(body, part):
        low, size = thirds[part]

        def step(x, carry):
            body(x)
            return carry

        lax.fori_loop(DEPTH + low, DEPTH + low + size, step, 0, unroll=size)

    for part in range(3):
        part_rows(down_three, part)
        across(T_MINE, part).start()
    pass_on(T_GUESS)
    arrive(T_ONE)

    @pl.when(tm > 0)
    def _():
        send("prev_one")

    arrive(T_ZERO)

    @pl.when(tm > 0)
    def _():
        send("prev_zero")

    def add_up(x):
        rhs3[0, x, mid, :] = mine[x - DEPTH] + theirs[x - DEPTH]

    for part in range(2):
        across(T_MINE, part).wait_recv()
        part_rows(add_up, part)
        send("rhs3", ((2 * part - 1, 0), (2 * part - 1, -1), (2 * part - 1, 1)))
    across(T_MINE, 2).wait_recv()
    part_rows(add_up, 2)
    send("rhs3", ((0, -1), (0, 1)))

    wait("err")
    wait("first_far")

    @pl.when(tm > 0)
    def _():
        wait("last")
        wait("prev_one")
        wait("prev_zero")

    def gather_far(x):
        f = factor[1, x]
        sums[0, x] = err[0, x] + err[1, x] + (f + f * f) * last[0, x]
        sums[1, x] = prev[0, x] + prev[1, x]

    rows(gather_far, 5)

    def level_two(x):
        g, f, weight = faces(x), factor[2, x, win, :], 0.25 * (1.0 + 2.0 * coupling[x, win, :])
        here, near = beside(sums, 0, x, g)
        err2[0, x, win, :] = f * (weight * here + 2.0 * near + prev[1, x, win, :])
        here, near = beside(sums, 1, x, g)
        err2[1, x, win, :] = f * (weight * here + 2.0 * near)

    rows(level_two, 4)

    def own_errors(x):
        f = factor[1, x, win, :]
        carried = f * last[0, x, win, :]
        return err[0, x, win, :] + carried, err[1, x, win, :] + f * carried

    def fix_two(x):
        g, f = faces(x), factor[2, x, win, :]
        own, near = beside(err2, 0, x, g)
        past, near_past = beside(err2, 1, x, g)
        value = (2.0 - relax_weight) * own + f * (4.0 * near + past)
        value_past = (2.0 - relax_weight) * past + 4.0 * (f * near_past)
        zero, first_one = own_errors(x)
        fix[0, x, win, :] = zero + value
        fix[1, x, win, :] = first_one + value
        fix[2, x, win, :] = prev[0, x, win, :] + value_past
        fix[3, x, win, :] = prev[1, x, win, :] + value_past

    rows(fix_two, 3)

    def fix_one(x):
        g, f = faces(x), factor[1, x, win, :]
        here, near = [], []
        for i in range(4):
            a, b = beside(fix, i, x, g)
            here.append(a)
            near.append(keep_weight * a + 2.0 * (f * b))
        zero, first_one = own_errors(x)
        value = near[0] + zero + f * here[3]
        vee[0, x, win, :] = value
        vee[1, x, win, :] = near[1] + first_one + f * (value - zero)
        value = near[2] + prev[0, x, win, :]
        vee[2, x, win, :] = value
        vee[3, x, win, :] = near[3] + prev[1, x, win, :] + f * (value - prev[0, x, win, :])

    rows(fix_one, 2)
    for name in NAMES:
        if name in ("last", "prev_one", "prev_zero"):
            @pl.when(tm > 0)
            def _(name=name):
                wait_sent(name)
        elif name != "rhs3":
            wait_sent(name)

    @pl.when(tm == 0)
    def _():
        for which in (T_INIT, T_LAST, T_ONE, T_ZERO):
            for part in range(2):
                across(which, part).wait_send()

    for part in range(3):
        across(T_MINE, part).wait_send()

    wait("source")
    wait("rhs3")

    def coarse_one(x):
        one[0, x] = factor[3, x] * rhs3[0, x]

    rows(coarse_one, 5)

    def coarse_two(x):
        here, near = beside(one, 0, x, faces(x))
        err3[0, x, win, :] = keep_weight * here + factor[3, x, win, :] * (rhs3[0, x, win, :] + 8.0 * near)

    rows(coarse_two, 4)

    def up_two(x):
        f = factor[2, x, win, :]
        here, near = beside(err3, 0, x, faces(x))
        value = keep_weight * here + 4.0 * (f * near)
        wave[0, x, win, :] = value + at_one * (f * here)
        wave[1, x, win, :] = value

    rows(up_two, 3)

    def up_one(x):
        g, f = faces(x), factor[1, x, win, :]
        here, near = beside(wave, 0, x, g)
        past, near_past = beside(wave, 1, x, g)
        own = keep_weight * here + 2.0 * (f * near)
        shadow = at_one * (keep_weight * past + 2.0 * (f * near_past))
        zero = own + at_one * (f * past)
        gain = (vee[0, x, win, :] + zero, vee[1, x, win, :] + own + f * zero)
        for t in range(steps):
            total[t, x, win, :] = first[t, x, win, :] + gain[t // 2]
        vee[2, x, win, :] = vee[2, x, win, :] + shadow
        vee[3, x, win, :] = vee[3, x, win, :] + shadow + f * shadow

    rows(up_one, 2)

    def up_zero(x):
        g, f = faces(x), factor[0, x, win, :]
        running = last[0, x, win, :] + vee[3, x, win, :]
        for t in range(steps):
            here, near = beside(total, t, x, g)
            running = keep_weight * here + f * (src[t, x, win, :] + near + running)
            sol[t, x, win, :] = running

    rows(up_zero, 1)
    arrive(T_GUESS)

    def finish(x):
        g, f = faces_mid(x), factor[0, x, mid, :]
        diagonal = 1.0 + coupling[x, mid, :]
        lifted = []
        for i in (2, 3):
            here, near = beside(vee, i, x, g)
            lifted.append(keep_weight * here + f * near)
        earlier = ahead[x - DEPTH] + (1.0 + f) * (f * f * lifted[0] + lifted[1])
        for t in range(steps):
            here, near = beside(sol, t, x, g)
            sol_out[t, x - DEPTH] = here
            res_out[t, x - DEPTH] = src[t, x, mid, :] + earlier - (diagonal * here - near)
            earlier = here

    rows(finish, 0)

    wait_sent("rhs3")

    @pl.when(tm == 0)
    def _():
        for part in range(2):
            across(T_GUESS, part).wait_send()


def wide_scratch(steps, nx, ny, nz):
    f32, dma = jnp.float32, pltpu.SemaphoreType.DMA
    depths = (1, steps, steps, steps, 3, 2, 1, 2, 2, 1, 1, 1, 1, 2, 2, 4, 4, steps, steps, 6)
    large = (nx + 2 * DEPTH, ny + 2 * EDGE, nz)
    scratch = [pltpu.VMEM((d,) + large, f32) for d in depths]
    scratch += [pltpu.VMEM(large, f32), pltpu.VMEM((4,) + large, f32)]
    scratch += [pltpu.VMEM((nx, ny, nz), f32)] * 5
    scratch += [dma((len(NAMES), 12)), dma((len(NAMES), 12)), dma((6, 3)), dma((6, 3)), dma((3,))]
    return scratch


def store(one, two, one_hbm, two_hbm, sem):
    copies = [
        pltpu.make_async_copy(held.at[t], hbm.at[t], sem.at[i, t])
        for i, (held, hbm) in enumerate(((one, one_hbm), (two, two_hbm)))
        for t in range(one.shape[0])
    ]
    for copy in copies:
        copy.start()
    for copy in copies:
        copy.wait()


def solution(mesh):
    n_tm, n_sx, n_sy = (mesh.shape[axis] for axis in ("tm", "sx", "sy"))
    f32 = jnp.float32

    def per_device(heat_source, conductivity, initial_iterate):
        steps, nx, ny, nz = heat_source.shape
        depth = (1, steps, steps, steps // 2, 1, 1, 1, steps // 2, steps, steps, 1, 1, 1, 1)
        scratch = [pltpu.VMEM((d, nx + 2, ny, nz), f32) for d in depth]
        scratch += [pltpu.VMEM((2, d, nx, nz), f32) for d in depth] * 2
        cells = (nx, ny, nz)
        dma = pltpu.SemaphoreType.DMA
        scratch += [
            pltpu.VMEM((steps,) + cells, f32),
            pltpu.VMEM((steps,) + cells, f32),
            pltpu.VMEM((7,) + cells, f32),
            pltpu.VMEM(cells, f32),
            pltpu.VMEM((steps // 2,) + cells, f32),
            pltpu.VMEM(cells, f32),
            pltpu.VMEM(cells, f32),
            pltpu.VMEM(cells, f32),
            pltpu.VMEM(cells, f32),
            pltpu.VMEM((2,) + cells, f32),
            pltpu.VMEM((6,) + cells, f32),
            pltpu.VMEM(cells, f32),
            pltpu.VMEM((4,) + cells, f32),
            dma((FIELDS, 4)), dma((FIELDS, 4)), dma((7, 2)), dma((7, 2)),
            dma((2,)), dma((2,)), dma((2,)), dma((2,)), dma((5,)),
        ]
        field = jax.ShapeDtypeStruct(heat_source.shape, f32)
        small = n_tm == 2 and steps == 4 and nx >= 2 * DEPTH and ny >= EDGE and ny % EDGE == 0
        if small:
            scratch = wide_scratch(steps, nx, ny, nz)
        one, two = pl.pallas_call(
            functools.partial(wide_kernel, n_sx, n_sy) if small else functools.partial(kernel, n_tm, n_sx, n_sy),
            out_shape=(pltpu.VMEM(heat_source.shape, f32),) * 2,
            in_specs=[pl.BlockSpec(memory_space=pltpu.HBM)] * 3,
            out_specs=(pl.BlockSpec(memory_space=pltpu.VMEM),) * 2,
            scratch_shapes=scratch,
            compiler_params=pltpu.CompilerParams(
                collective_id=0, has_side_effects=True, vmem_limit_bytes=40000000
            ),
            name="vcycle",
        )(*(pltpu.with_memory_space_constraint(x, pltpu.HBM) for x in (heat_source, conductivity, initial_iterate)))
        return pl.pallas_call(
            store,
            out_shape=(field, field),
            in_specs=[pl.BlockSpec(memory_space=pltpu.VMEM)] * 2,
            out_specs=(pl.BlockSpec(memory_space=pltpu.HBM),) * 2,
            scratch_shapes=[dma((2, steps))],
            name="store",
        )(*(pltpu.with_memory_space_constraint(x, pltpu.VMEM) for x in (one, two)))

    placed = (P("tm", "sx", "sy", None), P("sx", "sy", None), P("tm", "sx", "sy", None))
    return jax.shard_map(
        per_device,
        mesh=mesh,
        in_specs=placed,
        out_specs=(P("tm", "sx", "sy", None), P("tm", "sx", "sy", None)),
        check_vma=False,
    )
```

```python
import functools

import jax
import jax.numpy as jnp
from jax import lax
from jax.experimental import pallas as pl
from jax.experimental.pallas import tpu as pltpu
from jax.sharding import PartitionSpec as P

relax_weight = 0.8
keep_weight = 1.0 - relax_weight
MESH = pl.DeviceIdType.MESH

KAPPA, INIT, FIRST, ERR1, ERR2, ERR3, FIX2, FIX1, SUM0, SOL, PART, PAIR, PART2, PAIR2 = range(14)
FIELDS = 14
P_INIT, P_FIRST, P_ERR1, P_ERR2, P_FIX1, P_SUM0, P_SOL = range(7)
XLO, XHI, YLO, YHI = range(4)


def kernel(n_tm, n_sx, n_sy, hs_hbm, k_hbm, in_hbm, sol_hbm, res_hbm, *scratch):
    fields = scratch[:FIELDS]
    yrecv = scratch[FIELDS:2 * FIELDS]
    ysend = scratch[2 * FIELDS:3 * FIELDS]
    (hs, res, before, second, rhs1, rhs2, rhs3, mine, theirs, chain,
     face, coupling, factor, send_sem, recv_sem, tsend, trecv,
     qsend, qrecv, csend, crecv, local) = scratch[3 * FIELDS:]
    steps, nx, ny, nz = hs.shape
    tm, sx, sy = lax.axis_index("tm"), lax.axis_index("sx"), lax.axis_index("sy")
    has = (sx > 0, sx < n_sx - 1, sy > 0, sy < n_sy - 1)
    partner = tm + 1 - 2 * lax.rem(tm, 2)
    even = lax.rem(tm, 2) == 0

    loads = [
        pltpu.make_async_copy(k_hbm, fields[KAPPA].at[0, pl.ds(1, nx)], local.at[0]),
        pltpu.make_async_copy(in_hbm, fields[INIT].at[:, pl.ds(1, nx)], local.at[1]),
        pltpu.make_async_copy(hs_hbm, hs, local.at[2]),
    ]
    for load in loads:
        load.start()

    barrier = pltpu.get_barrier_semaphore()
    greet = [
        (has[XLO], {"sx": sx - 1}), (has[XHI], {"sx": sx + 1}),
        (has[YLO], {"sy": sy - 1}), (has[YHI], {"sy": sy + 1}),
        (tm > 0, {"tm": tm - 1}), (tm < n_tm - 1, {"tm": tm + 1}),
    ]
    if n_tm == 2:
        greet += [
            (has[XLO], {"tm": partner, "sx": sx - 1}), (has[XHI], {"tm": partner, "sx": sx + 1}),
            (has[YLO], {"tm": partner, "sy": sy - 1}), (has[YHI], {"tm": partner, "sy": sy + 1}),
        ]
    if n_tm > 2:
        greet += [(tm > 1, {"tm": tm - 2}), (tm < n_tm - 2, {"tm": tm + 2})]
    count = jnp.int32(0)
    for there, device in greet:
        count = count + jnp.where(there, 1, 0)

        @pl.when(there)
        def _(device=device):
            pl.semaphore_signal(barrier, inc=1, device_id=device, device_id_type=MESH)

    pl.semaphore_wait(barrier, count)

    def face_copy(i, side, pair=False):
        field = fields[i]
        to = i + 1 if pair else i
        land = fields[to]
        if side == XLO:
            if i == INIT:
                src = in_hbm.at[:, pl.ds(0, 1)]
            elif i == KAPPA:
                src = k_hbm.at[pl.ds(0, 1)]
            else:
                src = field.at[:, pl.ds(1, 1)]
            dst, device = land.at[:, pl.ds(nx + 1, 1)], {"sx": sx - 1}
        elif side == XHI:
            if i == INIT:
                src = in_hbm.at[:, pl.ds(nx - 1, 1)]
            elif i == KAPPA:
                src = k_hbm.at[pl.ds(nx - 1, 1)]
            else:
                src = field.at[:, pl.ds(nx, 1)]
            dst, device = land.at[:, pl.ds(0, 1)], {"sx": sx + 1}
        elif side == YLO:
            src, dst, device = ysend[i].at[0], yrecv[to].at[1], {"sy": sy - 1}
        else:
            src, dst, device = ysend[i].at[1], yrecv[to].at[0], {"sy": sy + 1}
        if i == KAPPA and side in (XLO, XHI):
            dst = field.at[0, pl.ds(nx + 1 if side == XLO else 0, 1)]
        if pair:
            device["tm"] = partner
        return pltpu.make_async_remote_copy(
            src_ref=src, dst_ref=dst, send_sem=send_sem.at[to, side],
            recv_sem=recv_sem.at[to, side], device_id=device, device_id_type=MESH)

    def send_faces(i, sides, pair=False):
        for side in sides:
            @pl.when(has[side])
            def _(side=side):
                face_copy(i, side).start()
                if pair:
                    face_copy(i, side, True).start()

    def wait_faces(i, pair=False):
        for side in (YLO, YHI, XLO, XHI):
            @pl.when(has[side ^ 1])
            def _(side=side):
                face_copy(i, side, pair).wait_recv()

    half = nx // 2
    halves = (pl.ds(0, half), pl.ds(half, nx - half))

    def last_copy(i, part):
        field = fields[lasts[i]]
        if i == P_INIT:
            src = in_hbm.at[steps - 1, halves[part]]
        else:
            src = field.at[field.shape[0] - 1, (pl.ds(1, half), pl.ds(1 + half, nx - half))[part]]
        return pltpu.make_async_remote_copy(
            src_ref=src, dst_ref=before.at[i, halves[part]],
            send_sem=tsend.at[i, part], recv_sem=trecv.at[i, part],
            device_id={"tm": tm + 1}, device_id_type=MESH)

    lasts = (INIT, FIRST, ERR1, ERR2, FIX1, SUM0, SOL)

    def send_last(i, part):
        @pl.when(tm < n_tm - 1)
        def _():
            last_copy(i, part).start()

    def wait_last(i, parts=(0, 1)):
        @pl.when(tm > 0)
        def _():
            for part in parts:
                last_copy(i, part).wait_recv()

    send_faces(KAPPA, (XLO, XHI))
    send_faces(INIT, (XLO, XHI))
    send_last(P_INIT, 0)
    send_last(P_INIT, 1)

    def over_rows(body, by=8, start=0, stop=nx):
        def step(x, carry):
            body(x)
            return carry

        lax.fori_loop(start, stop, step, 0, unroll=by)

    def phase(body, i, send_part=None, pair=False, awaited=None):
        if awaited is not None:
            wait_last(awaited, (0,))
        body(0)
        if awaited is None:
            body(nx - 1)
            send_faces(i, (XLO, XHI), pair)
        else:
            send_faces(i, (XLO,), pair)
        over_rows(body, half - 1, 1, half)
        if send_part is not None:
            send_part(0)
        if awaited is not None:
            wait_last(awaited, (1,))
            body(nx - 1)
            send_faces(i, (XHI,), pair)
        over_rows(body, half - 1, half, nx - 1)
        send_faces(i, (YLO, YHI), pair)
        if send_part is not None:
            send_part(1)

    def put_faces(i, t, x, value):
        ysend[i][0, t, pl.ds(x, 1), :] = value[0:1, :]
        ysend[i][1, t, pl.ds(x, 1), :] = value[ny - 1:ny, :]

    def put(i, t, x, value):
        fields[i][t, x + 1] = value
        put_faces(i, t, x, value)

    loads[0].wait()
    loads[1].wait()

    def pack(x):
        put_faces(KAPPA, 0, x, fields[KAPPA][0, x + 1])
        for t in range(steps):
            put_faces(INIT, t, x, fields[INIT][t, x + 1])

    over_rows(pack)
    send_faces(KAPPA, (YLO, YHI))
    send_faces(INIT, (YLO, YHI))

    @pl.when(sx == 0)
    def _():
        for i in range(FIELDS):
            for t in range(fields[i].shape[0]):
                fields[i][t, 0] = jnp.zeros((ny, nz), jnp.float32)

    @pl.when(sx == n_sx - 1)
    def _():
        for i in range(FIELDS):
            for t in range(fields[i].shape[0]):
                fields[i][t, nx + 1] = jnp.zeros((ny, nz), jnp.float32)

    @pl.when(sy == 0)
    def _():
        for i in range(FIELDS):
            yrecv[i][0] = jnp.zeros(yrecv[i].shape[1:], jnp.float32)

    @pl.when(sy == n_sy - 1)
    def _():
        for i in range(FIELDS):
            yrecv[i][1] = jnp.zeros(yrecv[i].shape[1:], jnp.float32)

    @pl.when(tm == 0)
    def _():
        def clear(x):
            for i in range(7):
                before[i, x] = jnp.zeros((ny, nz), jnp.float32)

        over_rows(clear, 1)

    row = lax.broadcasted_iota(jnp.int32, (ny, nz), 0)
    column = lax.broadcasted_iota(jnp.int32, (ny, nz), 1)

    def around(i, t, x):
        field = fields[i]
        here = field[t, x + 1]
        return here, (
            field[t, x + 2],
            field[t, x],
            jnp.where(row == ny - 1, yrecv[i][1, t, pl.ds(x, 1), :], pltpu.roll(here, ny - 1, 0)),
            jnp.where(row == 0, yrecv[i][0, t, pl.ds(x, 1), :], pltpu.roll(here, 1, 0)),
            pltpu.roll(here, nz - 1, 1),
            pltpu.roll(here, 1, 1),
        )

    def beside(i, t, x, g):
        here, sides = around(i, t, x)
        terms = [g[j] * sides[j] for j in range(6)]
        return here, (terms[0] + terms[1]) + (terms[2] + terms[3]) + (terms[4] + terms[5])

    def faces_at(x):
        return [face[j, x] for j in range(6)]

    wait_faces(KAPPA)

    def coefficients(x):
        here, sides = around(KAPPA, 0, x)
        sides = list(sides)
        sides[4] = jnp.where(column == nz - 1, 0.0, sides[4])
        sides[5] = jnp.where(column == 0, 0.0, sides[5])
        g = [0.5 * (here + side) for side in sides]
        total = (g[0] + g[1]) + (g[2] + g[3]) + (g[4] + g[5])
        coupling[x] = total
        g[4] = jnp.where(column == nz - 1, 0.0, g[4])
        g[5] = jnp.where(column == 0, 0.0, g[5])
        for j in range(6):
            face[j, x] = g[j]
        for level in range(4):
            factor[level, x] = relax_weight / (1.0 + (2.0 ** level) * total)

    over_rows(coefficients)
    loads[2].wait()
    wait_faces(INIT)

    def sweep_first(x):
        g, f = faces_at(x), factor[0, x]
        running = before[P_INIT, x]
        for t in range(steps):
            here, near = beside(INIT, t, x, g)
            running = keep_weight * here + f * (hs[t, x] + near + running)
            put(FIRST, t, x, running)

    phase(sweep_first, FIRST, functools.partial(send_last, P_FIRST), awaited=P_INIT)
    wait_faces(FIRST)

    def down_one(x):
        g, diagonal, f = faces_at(x), 1.0 + coupling[x], factor[1, x]
        earlier = before[P_FIRST, x]
        running = None
        for m in range(steps // 2):
            total = None
            for t in (2 * m, 2 * m + 1):
                here, near = beside(FIRST, t, x, g)
                value = hs[t, x] + earlier - (diagonal * here - near)
                total = value if total is None else total + value
                earlier = here
            rhs1[m, x] = total
            running = f * total if running is None else f * (total + running)
            put(ERR1, m, x, running)

    phase(down_one, ERR1, functools.partial(send_last, P_ERR1), awaited=P_FIRST)
    wait_faces(ERR1)
    wait_last(P_ERR1)

    def down_two(x):
        g, diagonal, f = faces_at(x), 1.0 + 2.0 * coupling[x], factor[2, x]
        earlier = before[P_ERR1, x]
        total = None
        for t in range(2):
            here, near = beside(ERR1, t, x, g)
            value = rhs1[t, x] + earlier - (diagonal * here - 2.0 * near)
            total = value if total is None else total + value
            earlier = here
        rhs2[x] = total
        put(ERR2, 0, x, f * total)

    phase(down_two, ERR2, functools.partial(send_last, P_ERR2))
    wait_faces(ERR2)
    if n_tm > 2:
        wait_last(P_ERR2)

    def down_three(x):
        g, diagonal = faces_at(x), 1.0 + 4.0 * coupling[x]
        here, near = beside(ERR2, 0, x, g)
        earlier = here + before[P_ERR2, x] if n_tm > 2 else here
        value = rhs2[x] + jnp.where(even, earlier, 0.0) - (diagonal * here - 4.0 * near)
        mine[x] = value
        if n_tm == 2:
            put(PART, 0, x, factor[3, x] * value)

    def swap(part):
        return pltpu.make_async_remote_copy(
            src_ref=mine.at[halves[part]], dst_ref=theirs.at[halves[part]],
            send_sem=qsend.at[part], recv_sem=qrecv.at[part],
            device_id={"tm": partner}, device_id_type=MESH)

    if n_tm == 2:
        phase(down_three, PART, lambda part: swap(part).start(), True)
        wait_faces(PART)

        def part_two(x):
            here, near = beside(PART, 0, x, faces_at(x))
            put(PART2, 0, x, keep_weight * here + factor[3, x] * (mine[x] + 8.0 * near))

        phase(part_two, PART2, None, True)
    else:
        over_rows(down_three)
        swap(0).start()
        swap(1).start()
    swap(0).wait_recv()
    swap(1).wait_recv()

    def chain_copy(i, field):
        src = field.at[0, pl.ds(1, nx)] if i == 0 else second
        return pltpu.make_async_remote_copy(
            src_ref=src, dst_ref=chain.at[i], send_sem=csend.at[i],
            recv_sem=crecv.at[i], device_id={"tm": tm + 2}, device_id_type=MESH)

    def chain_wait(i):
        if n_tm > 2:
            @pl.when(tm > 1)
            def _():
                chain_copy(i, fields[ERR3]).wait_recv()

            @pl.when(tm < 2)
            def _():
                def clear(x):
                    chain[i, x] = jnp.zeros((ny, nz), jnp.float32)

                over_rows(clear, 1)

    def chain_send(i):
        if n_tm > 2:
            @pl.when(tm < n_tm - 2)
            def _():
                chain_copy(i, fields[ERR3]).start()

    chain_wait(0)

    def coarse_one(x):
        total = mine[x] + theirs[x]
        rhs3[x] = total
        if n_tm > 2:
            total = total + chain[0, x]
        value = factor[3, x] * total
        if n_tm > 2:
            put(ERR3, 0, x, value)
        else:
            fields[ERR3][0, x + 1] = value

    if n_tm > 2:
        phase(coarse_one, ERR3)
        chain_send(0)
        wait_faces(ERR3)
    else:
        over_rows(coarse_one)
        wait_faces(PART, True)
        for edge in (0, nx + 1):
            fields[ERR3][0, edge] = fields[PART][0, edge] + fields[PAIR][0, edge]
        for edge in range(2):
            yrecv[ERR3][edge, 0] = yrecv[PART][edge, 0] + yrecv[PAIR][edge, 0]
    if n_tm == 2:
        wait_last(P_ERR2)
    chain_wait(1)

    def coarse_two(x):
        here, near = beside(ERR3, 0, x, faces_at(x))
        total = rhs3[x] + 8.0 * near
        if n_tm > 2:
            total = total + chain[1, x]
        value = keep_weight * here + factor[3, x] * total
        if n_tm > 2:
            second[x] = value
            earlier = jnp.where(even, chain[1, x], value)
        else:
            earlier = jnp.where(even, 0.0, value)
        mine_next[x] = before[P_ERR2, x] + earlier
        value = fields[ERR2][0, x + 1] + value
        if n_tm > 2:
            put(FIX2, 0, x, value)
        else:
            fields[FIX2][0, x + 1] = value

    mine_next = res.at[0]
    if n_tm > 2:
        phase(coarse_two, FIX2)
        chain_send(1)
        wait_faces(FIX2)
    else:
        over_rows(coarse_two)
        wait_faces(PART2)
        wait_faces(PART2, True)
        for edge in (0, nx + 1):
            fields[FIX2][0, edge] = fields[ERR2][0, edge] + (
                fields[PART2][0, edge] + fields[PAIR2][0, edge])
        for edge in range(2):
            yrecv[FIX2][edge, 0] = yrecv[ERR2][edge, 0] + (
                yrecv[PART2][edge, 0] + yrecv[PAIR2][edge, 0])

    def up_two(x):
        here, near = beside(FIX2, 0, x, faces_at(x))
        value = keep_weight * here + factor[2, x] * (rhs2[x] + 4.0 * near + mine_next[x])
        for m in range(2):
            put(FIX1, m, x, fields[ERR1][m, x + 1] + value)

    phase(up_two, FIX1, functools.partial(send_last, P_FIX1))
    wait_faces(FIX1)

    def up_one(x):
        g, f = faces_at(x), factor[1, x]
        running = before[P_FIX1, x]
        for m in range(2):
            here, near = beside(FIX1, m, x, g)
            running = keep_weight * here + f * (rhs1[m, x] + 2.0 * near + running)
            for t in (2 * m, 2 * m + 1):
                put(SUM0, t, x, fields[FIRST][t, x + 1] + running)

    phase(up_one, SUM0, functools.partial(send_last, P_SUM0), awaited=P_FIX1)
    wait_faces(SUM0)
    wait_last(P_SUM0)

    def up_zero(x):
        g, f = faces_at(x), factor[0, x]
        running = before[P_SUM0, x]
        for t in range(steps):
            here, near = beside(SUM0, t, x, g)
            running = keep_weight * here + f * (hs[t, x] + near + running)
            put(SOL, t, x, running)
            sol_hbm[t, x] = running

    phase(up_zero, SOL, functools.partial(send_last, P_SOL))
    wait_faces(SOL)
    wait_last(P_SOL)

    def last_defect(x):
        g, diagonal = faces_at(x), 1.0 + coupling[x]
        earlier = before[P_SOL, x]
        for t in range(steps):
            here, near = beside(SOL, t, x, g)
            res_hbm[t, x] = hs[t, x] + earlier - (diagonal * here - near)
            earlier = here

    over_rows(last_defect)

    for i in range(FIELDS):
        if i in ((PAIR, PAIR2, ERR3, FIX2) if n_tm == 2 else (PART, PAIR, PART2, PAIR2)):
            continue
        for side in (XLO, XHI, YLO, YHI):
            @pl.when(has[side])
            def _(i=i, side=side):
                face_copy(i, side).wait_send()
                if i in (PART, PART2):
                    face_copy(i, side, True).wait_send()

    @pl.when(tm < n_tm - 1)
    def _():
        for i in range(7):
            for part in range(2):
                last_copy(i, part).wait_send()

    swap(0).wait_send()
    swap(1).wait_send()
    if n_tm > 2:
        @pl.when(tm < n_tm - 2)
        def _():
            for i in range(2):
                chain_copy(i, fields[ERR3]).wait_send()


DEPTH = 6
EDGE = 8
REACH = 4
EXCHANGES = {
    "kappa": ("k", (0, 1), ()),
    "kappa_far": ("k", (1, 6), ((0, 5, 0, 5),)),
    "init": ("in", (0, 1), ()),
    "source": ("hs", (0, 1), ()),
    "first": ("first", (0, 1), ()),
    "first_far": ("first", (1, 2), ((0, 1, 0, 1),)),
    "pair": ("pair", (0, 2), ((0, 1, 0, 1),)),
    "err": ("err", (0, 5), ((0, 4, 0, 4),)),
    "last": ("last", (0, 5), ((0, 4, 0, 4),)),
    "prev_one": ("prev", (0, 5), ((0, 4, 0, 4),)),
    "prev_zero": ("prev", (0, 5), ((0, 4, 0, 4),)),
    "rhs3": ("rhs3", (0, 5), ((0, 4, 0, 4),)),
}
NAMES = tuple(EXCHANGES)
X_FACES = ((-1, 0), (1, 0))
REST = ((0, -1), (0, 1), (-1, -1), (-1, 1), (1, -1), (1, 1))
ALL = X_FACES + REST
T_INIT, T_LAST, T_ONE, T_ZERO, T_MINE, T_GUESS = range(6)


def wide_kernel(n_sx, n_sy, hs_hbm, k_hbm, in_hbm, sol_out, res_out,
                kap, ini, src, first, pair, err, last, prev, sums, fr, rhs3, one, err3, wave,
                err2, fix, vee, total, sol, face, coupling, factor,
                before, mine, theirs, guess, ahead,
                send_sem, recv_sem, tsend, trecv, local):
    nx, ny, nz = k_hbm.shape
    steps = in_hbm.shape[0]
    wide = ny + 2 * EDGE
    tm, sx, sy = lax.axis_index("tm"), lax.axis_index("sx"), lax.axis_index("sy")
    at_one = jnp.where(tm > 0, 1.0, 0.0)
    at_zero = 1.0 - at_one
    mid = pl.ds(EDGE, ny)
    win = pl.ds(EDGE - REACH, ny + 2 * REACH)
    inner = pl.ds(DEPTH, nx)
    homes = {"k": kap, "in": ini, "hs": src, "first": first, "pair": pair, "err": err,
             "last": last, "prev": prev, "rhs3": rhs3}

    loads = [
        pltpu.make_async_copy(k_hbm, kap.at[0, inner, mid], local.at[0]),
        pltpu.make_async_copy(in_hbm, ini.at[:, inner, mid], local.at[1]),
        pltpu.make_async_copy(hs_hbm, src.at[:, inner, mid], local.at[2]),
    ]
    for load in loads:
        load.start()

    def there(way, sign=1):
        ok = None
        for step, at, size in ((sign * way[0], sx, n_sx), (sign * way[1], sy, n_sy)):
            if step:
                here = at > 0 if step < 0 else at < size - 1
                ok = here if ok is None else jnp.logical_and(ok, here)
        return ok

    def target(way):
        device = {}
        if way[0]:
            device["sx"] = sx + way[0]
        if way[1]:
            device["sy"] = sy + way[1]
        return device

    barrier = pltpu.get_barrier_semaphore()
    count = jnp.int32(1)
    for way in ALL:
        count = count + jnp.where(there(way), 1, 0)

        @pl.when(there(way))
        def _(way=way):
            pl.semaphore_signal(barrier, inc=1, device_id=target(way), device_id_type=MESH)

    pl.semaphore_signal(barrier, inc=1, device_id={"tm": 1 - tm}, device_id_type=MESH)

    def rows(body, depth, by=None):
        def step(x, carry):
            body(x)
            return carry

        if by is None:
            by = (nx + 2 * depth) // (2 if depth else 1)
        lax.fori_loop(DEPTH - depth, DEPTH + nx + depth, step, 0, unroll=by)

    filled = ((kap, 6), (ini, 1), (src, 1), (first, 2), (pair, 2), (err, 5), (last, 5), (prev, 5), (rhs3, 5))
    plane = jnp.zeros((wide, nz), jnp.float32)
    strip = jnp.zeros((EDGE, nz), jnp.float32)

    def fill(edge_rows):
        for array, depth in filled:
            for t in range(array.shape[0]):
                for i in range(depth):
                    array[t, DEPTH - 1 - i if edge_rows < 0 else DEPTH + nx + i] = plane

    def fill_side(start):
        for array, depth in filled:
            def body(x):
                for t in range(array.shape[0]):
                    array[t, x, pl.ds(start, EDGE), :] = strip

            rows(body, depth, 2)

    @pl.when(sx == 0)
    def _():
        fill(-1)

    @pl.when(sx == n_sx - 1)
    def _():
        fill(1)

    @pl.when(sy == 0)
    def _():
        fill_side(0)

    @pl.when(sy == n_sy - 1)
    def _():
        fill_side(EDGE + ny)

    @pl.when(tm == 0)
    def _():
        def body(x):
            last[0, x] = plane
            prev[0, x] = plane
            prev[1, x] = plane

        rows(body, 5, 2)

        def empty(x):
            before[x - DEPTH] = jnp.zeros((ny, nz), jnp.float32)
            ahead[x - DEPTH] = jnp.zeros((ny, nz), jnp.float32)

        rows(empty, 0, 2)

    pl.semaphore_wait(barrier, count)

    def span(step, size, low, high):
        if step == 0:
            return 0, size, 0
        if step < 0:
            return low, high - low, size + low
        return size - high, high - low, -high

    def pieces(name, ways):
        kind, (low, high), corners = EXCHANGES[name]
        slot = 0
        for way in ALL:
            boxes = corners if way[0] and way[1] else ((low, high, low, high),)
            for box in boxes:
                if way in ways:
                    yield way, box, slot
                slot += 1

    def copy_of(name, way, box, slot):
        kind = EXCHANGES[name][0]
        land = homes[kind]
        fx, wx, tx = span(way[0], nx, box[0], box[1])
        fy, wy, ty = span(way[1], ny, box[2], box[3])
        steps_at = {"prev_zero": pl.ds(0, 1), "prev_one": pl.ds(1, 1)}.get(name, slice(None))
        if kind == "k":
            source = land.at[0, pl.ds(DEPTH + fx, wx), pl.ds(EDGE + fy, wy)]
            dest = land.at[0, pl.ds(DEPTH + tx, wx), pl.ds(EDGE + ty, wy)]
        else:
            source = land.at[steps_at, pl.ds(DEPTH + fx, wx), pl.ds(EDGE + fy, wy)]
            dest = land.at[steps_at, pl.ds(DEPTH + tx, wx), pl.ds(EDGE + ty, wy)]
        number = NAMES.index(name)
        return pltpu.make_async_remote_copy(
            src_ref=source, dst_ref=dest, send_sem=send_sem.at[number, slot],
            recv_sem=recv_sem.at[number, slot], device_id=target(way), device_id_type=MESH)

    def send(name, ways=ALL):
        for way, box, slot in pieces(name, ways):
            @pl.when(there(way))
            def _(way=way, box=box, slot=slot):
                copy_of(name, way, box, slot).start()

    def wait(name):
        for way, box, slot in pieces(name, REST + X_FACES):
            @pl.when(there(way, -1))
            def _(way=way, box=box, slot=slot):
                copy_of(name, way, box, slot).wait_recv()

    def wait_sent(name):
        for way, box, slot in pieces(name, ALL):
            @pl.when(there(way))
            def _(way=way, box=box, slot=slot):
                copy_of(name, way, box, slot).wait_send()

    half = nx // 2
    ends = ((0, half), (half, nx - half))
    thirds = ((0, DEPTH - 1), (nx - DEPTH + 1, DEPTH - 1), (DEPTH - 1, nx - 2 * DEPTH + 2))

    def across(which, part):
        low, size = (thirds if which == T_MINE else ends)[part]
        near, far = pl.ds(low, size), pl.ds(DEPTH + low, size)
        source, dest = {
            T_INIT: lambda: (ini.at[steps - 1, far, mid], before.at[near]),
            T_LAST: lambda: (first.at[steps - 1, far, mid], last.at[0, far, mid]),
            T_ONE: lambda: (err.at[1, far, mid], prev.at[1, far, mid]),
            T_ZERO: lambda: (err.at[0, far, mid], prev.at[0, far, mid]),
            T_MINE: lambda: (mine.at[near], theirs.at[near]),
            T_GUESS: lambda: (guess.at[near], ahead.at[near]),
        }[which]()
        return pltpu.make_async_remote_copy(
            src_ref=source, dst_ref=dest, send_sem=tsend.at[which, part],
            recv_sem=trecv.at[which, part], device_id={"tm": 1 - tm}, device_id_type=MESH)

    def pass_on(which, parts=(0, 1)):
        @pl.when(tm == 0)
        def _():
            for part in parts:
                across(which, part).start()

    def arrive(which, parts=(0, 1)):
        @pl.when(tm > 0)
        def _():
            for part in parts:
                across(which, part).wait_recv()

    loads[0].wait()
    send("kappa")
    loads[1].wait()
    send("init")
    pass_on(T_INIT)
    loads[2].wait()
    send("source")
    send("kappa_far")

    column = lax.broadcasted_iota(jnp.int32, (wide, nz), 1)
    height = lax.broadcasted_iota(jnp.int32, (wide, nz), 0)
    low_side = jnp.where(sy == 0, EDGE, 0)
    high_side = jnp.where(sy == n_sy - 1, EDGE + ny, wide)
    within = jnp.logical_and(height >= low_side, height < high_side)
    low_row = jnp.where(sx == 0, DEPTH, 0)
    high_row = jnp.where(sx == n_sx - 1, DEPTH + nx, nx + 2 * DEPTH)

    def around(ref, t, x):
        here = ref[t, x]
        return here, (
            ref[t, x + 1], ref[t, x - 1],
            pltpu.roll(here, wide - 1, 0), pltpu.roll(here, 1, 0),
            pltpu.roll(here, nz - 1, 1), pltpu.roll(here, 1, 1),
        )

    def around_part(ref, t, x, size):
        low = EDGE - (size - ny) // 2
        part = pl.ds(low, size)
        here = ref[t, x, part, :]
        return here, (
            ref[t, x + 1, part, :], ref[t, x - 1, part, :],
            ref[t, x, pl.ds(low + 1, size), :], ref[t, x, pl.ds(low - 1, size), :],
            pltpu.roll(here, nz - 1, 1), pltpu.roll(here, 1, 1),
        )

    def beside(ref, t, x, g):
        here, sides = around_part(ref, t, x, g[0].shape[0])
        terms = [g[j] * sides[j] for j in range(6)]
        return here, (terms[0] + terms[1]) + (terms[2] + terms[3]) + (terms[4] + terms[5])

    def faces(x):
        return [face[j, x, win, :] for j in range(6)]

    def faces_mid(x):
        return [face[j, x, mid, :] for j in range(6)]

    def couple(here, sides, col):
        sides = list(sides)
        top, bottom = col == nz - 1, col == 0
        sides[4] = jnp.where(top, 0.0, sides[4])
        sides[5] = jnp.where(bottom, 0.0, sides[5])
        g = [0.5 * (here + side) for side in sides]
        whole = (g[0] + g[1]) + (g[2] + g[3]) + (g[4] + g[5])
        g[4] = jnp.where(top, 0.0, g[4])
        g[5] = jnp.where(bottom, 0.0, g[5])
        return g, whole

    def coefficients_mid(x):
        g, whole = couple(*around_part(kap, 0, x, ny), column[:ny])
        coupling[x, mid, :] = whole
        for j in range(6):
            face[j, x, mid, :] = g[j]
        for level in range(2):
            factor[level, x, mid, :] = relax_weight / (1.0 + (2.0 ** level) * whole)

    def coefficients(x):
        g, whole = couple(*around(kap, 0, x), column)
        coupling[x] = whole
        inside = jnp.logical_and(within, jnp.logical_and(x >= low_row, x < high_row))
        for j in range(6):
            face[j, x] = g[j]
        for level in range(4):
            factor[level, x] = jnp.where(inside, relax_weight / (1.0 + (2.0 ** level) * whole), 0.0)

    def phase(body, edge, name):
        for i in range(edge):
            body(DEPTH + i)
            body(DEPTH + nx - 1 - i)
        send(name, X_FACES)

        def step(x, carry):
            body(x)
            return carry

        lax.fori_loop(DEPTH + edge, DEPTH + nx - edge, step, 0, unroll=nx // 2 - edge)
        send(name, REST)

    wait("kappa")
    rows(coefficients_mid, 0)
    wait("init")
    arrive(T_INIT)

    def sweep_first(x):
        g, f = faces_mid(x), factor[0, x, mid, :]
        running = before[x - DEPTH]
        for t in range(steps):
            here, near = beside(ini, t, x, g)
            running = keep_weight * here + f * (src[t, x, mid, :] + near + running)
            first[t, x, mid, :] = running

    phase(sweep_first, 1, "first")
    pass_on(T_LAST)
    wait("kappa_far")
    rows(coefficients, 5)
    send("first_far")
    wait("first")

    def down_one(x):
        g, f, c = faces_mid(x), factor[0, x, mid, :], coupling[x, mid, :]
        f_one = factor[1, x, mid, :]
        diagonal = 1.0 + c
        earlier = None
        ahead_value = None
        running = None
        pair_zero = None
        for m in range(2):
            both = None
            for t in (2 * m, 2 * m + 1):
                here, near = beside(first, t, x, g)
                supply = src[t, x, mid, :] + near
                value = supply - diagonal * here
                if earlier is not None:
                    value = value + earlier
                both = value if both is None else both + value
                ahead_value = keep_weight * here + f * (supply if ahead_value is None else supply + ahead_value)
                earlier = here
            running = f_one * both if running is None else f_one * (both + running)
            err[m, x, mid, :] = running
            pair_zero = running if m == 0 else pair_zero
        both = pair_zero + running
        pair[1, x, mid, :] = both
        pair[0, x, mid, :] = both + at_zero * ((f_one + f_one * f_one) * earlier)
        pair[2, x, mid, :] = at_zero * running
        guess[x - DEPTH] = ahead_value

    phase(down_one, 2, "pair")
    pass_on(T_ONE)
    pass_on(T_ZERO)
    send("err")
    arrive(T_LAST)

    @pl.when(tm > 0)
    def _():
        send("last")

    wait("pair")

    def down_two(x):
        here, near = beside(pair, 0, x, faces(x))
        value = 0.25 * (1.0 + 2.0 * coupling[x, win, :]) * here + 2.0 * near + pair[2, x, win, :]
        fr[0, x, win, :] = factor[2, x, win, :] * value

    rows(down_two, 1)

    def down_three(x):
        g, c = faces_mid(x), coupling[x, mid, :]
        here, near = beside(fr, 0, x, g)
        value = 0.25 * (1.0 + 4.0 * c) * here + 4.0 * near
        here, near = beside(pair, 1, x, g)
        base = factor[2, x, mid, :] * (0.25 * (1.0 + 2.0 * c) * here + 2.0 * near)
        mine[x - DEPTH] = value + at_zero * base

    def part_rows(body, part):
        low, size = thirds[part]

        def step(x, carry):
            body(x)
            return carry

        lax.fori_loop(DEPTH + low, DEPTH + low + size, step, 0, unroll=size)

    for part in range(3):
        part_rows(down_three, part)
        across(T_MINE, part).start()
    pass_on(T_GUESS)
    arrive(T_ONE)

    @pl.when(tm > 0)
    def _():
        send("prev_one")

    arrive(T_ZERO)

    @pl.when(tm > 0)
    def _():
        send("prev_zero")

    def add_up(x):
        rhs3[0, x, mid, :] = mine[x - DEPTH] + theirs[x - DEPTH]

    for part in range(2):
        across(T_MINE, part).wait_recv()
        part_rows(add_up, part)
        send("rhs3", ((2 * part - 1, 0), (2 * part - 1, -1), (2 * part - 1, 1)))
    across(T_MINE, 2).wait_recv()
    part_rows(add_up, 2)
    send("rhs3", ((0, -1), (0, 1)))

    wait("err")
    wait("first_far")

    @pl.when(tm > 0)
    def _():
        wait("last")
        wait("prev_one")
        wait("prev_zero")

    def gather_far(x):
        f = factor[1, x]
        sums[0, x] = err[0, x] + err[1, x] + (f + f * f) * last[0, x]
        sums[1, x] = prev[0, x] + prev[1, x]

    rows(gather_far, 5)

    def level_two(x):
        g, f, weight = faces(x), factor[2, x, win, :], 0.25 * (1.0 + 2.0 * coupling[x, win, :])
        here, near = beside(sums, 0, x, g)
        err2[0, x, win, :] = f * (weight * here + 2.0 * near + prev[1, x, win, :])
        here, near = beside(sums, 1, x, g)
        err2[1, x, win, :] = f * (weight * here + 2.0 * near)

    rows(level_two, 4)

    def own_errors(x):
        f = factor[1, x, win, :]
        carried = f * last[0, x, win, :]
        return err[0, x, win, :] + carried, err[1, x, win, :] + f * carried

    def fix_two(x):
        g, f = faces(x), factor[2, x, win, :]
        own, near = beside(err2, 0, x, g)
        past, near_past = beside(err2, 1, x, g)
        value = (2.0 - relax_weight) * own + f * (4.0 * near + past)
        value_past = (2.0 - relax_weight) * past + 4.0 * (f * near_past)
        zero, first_one = own_errors(x)
        fix[0, x, win, :] = zero + value
        fix[1, x, win, :] = first_one + value
        fix[2, x, win, :] = prev[0, x, win, :] + value_past
        fix[3, x, win, :] = prev[1, x, win, :] + value_past

    rows(fix_two, 3)

    def fix_one(x):
        g, f = faces(x), factor[1, x, win, :]
        here, near = [], []
        for i in range(4):
            a, b = beside(fix, i, x, g)
            here.append(a)
            near.append(keep_weight * a + 2.0 * (f * b))
        zero, first_one = own_errors(x)
        value = near[0] + zero + f * here[3]
        vee[0, x, win, :] = value
        vee[1, x, win, :] = near[1] + first_one + f * (value - zero)
        value = near[2] + prev[0, x, win, :]
        vee[2, x, win, :] = value
        vee[3, x, win, :] = near[3] + prev[1, x, win, :] + f * (value - prev[0, x, win, :])

    rows(fix_one, 2)
    for name in NAMES:
        if name in ("last", "prev_one", "prev_zero"):
            @pl.when(tm > 0)
            def _(name=name):
                wait_sent(name)
        elif name != "rhs3":
            wait_sent(name)

    @pl.when(tm == 0)
    def _():
        for which in (T_INIT, T_LAST, T_ONE, T_ZERO):
            for part in range(2):
                across(which, part).wait_send()

    for part in range(3):
        across(T_MINE, part).wait_send()

    wait("source")
    wait("rhs3")

    def coarse_one(x):
        one[0, x] = factor[3, x] * rhs3[0, x]

    rows(coarse_one, 5)

    def coarse_two(x):
        here, near = beside(one, 0, x, faces(x))
        err3[0, x, win, :] = keep_weight * here + factor[3, x, win, :] * (rhs3[0, x, win, :] + 8.0 * near)

    rows(coarse_two, 4)

    def up_two(x):
        f = factor[2, x, win, :]
        here, near = beside(err3, 0, x, faces(x))
        value = keep_weight * here + 4.0 * (f * near)
        wave[0, x, win, :] = value + at_one * (f * here)
        wave[1, x, win, :] = value

    rows(up_two, 3)

    def up_one(x):
        g, f = faces(x), factor[1, x, win, :]
        here, near = beside(wave, 0, x, g)
        past, near_past = beside(wave, 1, x, g)
        own = keep_weight * here + 2.0 * (f * near)
        shadow = at_one * (keep_weight * past + 2.0 * (f * near_past))
        zero = own + at_one * (f * past)
        gain = (vee[0, x, win, :] + zero, vee[1, x, win, :] + own + f * zero)
        for t in range(steps):
            total[t, x, win, :] = first[t, x, win, :] + gain[t // 2]
        vee[2, x, win, :] = vee[2, x, win, :] + shadow
        vee[3, x, win, :] = vee[3, x, win, :] + shadow + f * shadow

    rows(up_one, 2)

    def up_zero(x):
        g, f = faces(x), factor[0, x, win, :]
        running = last[0, x, win, :] + vee[3, x, win, :]
        for t in range(steps):
            here, near = beside(total, t, x, g)
            running = keep_weight * here + f * (src[t, x, win, :] + near + running)
            sol[t, x, win, :] = running

    rows(up_zero, 1)
    arrive(T_GUESS)

    def finish(x):
        g, f = faces_mid(x), factor[0, x, mid, :]
        diagonal = 1.0 + coupling[x, mid, :]
        lifted = []
        for i in (2, 3):
            here, near = beside(vee, i, x, g)
            lifted.append(keep_weight * here + f * near)
        earlier = ahead[x - DEPTH] + (1.0 + f) * (f * f * lifted[0] + lifted[1])
        for t in range(steps):
            here, near = beside(sol, t, x, g)
            sol_out[t, x - DEPTH] = here
            res_out[t, x - DEPTH] = src[t, x, mid, :] + earlier - (diagonal * here - near)
            earlier = here

    rows(finish, 0)

    wait_sent("rhs3")

    @pl.when(tm == 0)
    def _():
        for part in range(2):
            across(T_GUESS, part).wait_send()


def wide_scratch(steps, nx, ny, nz):
    f32, dma = jnp.float32, pltpu.SemaphoreType.DMA
    depths = (1, steps, steps, steps, 3, 2, 1, 2, 2, 1, 1, 1, 1, 2, 2, 4, 4, steps, steps, 6)
    large = (nx + 2 * DEPTH, ny + 2 * EDGE, nz)
    scratch = [pltpu.VMEM((d,) + large, f32) for d in depths]
    scratch += [pltpu.VMEM(large, f32), pltpu.VMEM((4,) + large, f32)]
    scratch += [pltpu.VMEM((nx, ny, nz), f32)] * 5
    scratch += [dma((len(NAMES), 12)), dma((len(NAMES), 12)), dma((6, 3)), dma((6, 3)), dma((3,))]
    return scratch


def store(one, two, one_hbm, two_hbm, sem):
    copies = [
        pltpu.make_async_copy(held.at[t], hbm.at[t], sem.at[i, t])
        for i, (held, hbm) in enumerate(((one, one_hbm), (two, two_hbm)))
        for t in range(one.shape[0])
    ]
    for copy in copies:
        copy.start()
    for copy in copies:
        copy.wait()


def solution(mesh):
    n_tm, n_sx, n_sy = (mesh.shape[axis] for axis in ("tm", "sx", "sy"))
    f32 = jnp.float32

    def per_device(heat_source, conductivity, initial_iterate):
        steps, nx, ny, nz = heat_source.shape
        depth = (1, steps, steps, steps // 2, 1, 1, 1, steps // 2, steps, steps, 1, 1, 1, 1)
        scratch = [pltpu.VMEM((d, nx + 2, ny, nz), f32) for d in depth]
        scratch += [pltpu.VMEM((2, d, nx, nz), f32) for d in depth] * 2
        cells = (nx, ny, nz)
        dma = pltpu.SemaphoreType.DMA
        scratch += [
            pltpu.VMEM((steps,) + cells, f32),
            pltpu.VMEM((steps,) + cells, f32),
            pltpu.VMEM((7,) + cells, f32),
            pltpu.VMEM(cells, f32),
            pltpu.VMEM((steps // 2,) + cells, f32),
            pltpu.VMEM(cells, f32),
            pltpu.VMEM(cells, f32),
            pltpu.VMEM(cells, f32),
            pltpu.VMEM(cells, f32),
            pltpu.VMEM((2,) + cells, f32),
            pltpu.VMEM((6,) + cells, f32),
            pltpu.VMEM(cells, f32),
            pltpu.VMEM((4,) + cells, f32),
            dma((FIELDS, 4)), dma((FIELDS, 4)), dma((7, 2)), dma((7, 2)),
            dma((2,)), dma((2,)), dma((2,)), dma((2,)), dma((5,)),
        ]
        field = jax.ShapeDtypeStruct(heat_source.shape, f32)
        small = n_tm == 2 and steps == 4 and nx >= 2 * DEPTH and ny >= EDGE and ny % EDGE == 0
        if small:
            scratch = wide_scratch(steps, nx, ny, nz)
        one, two = pl.pallas_call(
            functools.partial(wide_kernel, n_sx, n_sy) if small else functools.partial(kernel, n_tm, n_sx, n_sy),
            out_shape=(pltpu.VMEM(heat_source.shape, f32),) * 2,
            in_specs=[pl.BlockSpec(memory_space=pltpu.HBM)] * 3,
            out_specs=(pl.BlockSpec(memory_space=pltpu.VMEM),) * 2,
            scratch_shapes=scratch,
            compiler_params=pltpu.CompilerParams(
                collective_id=0, has_side_effects=True, vmem_limit_bytes=40000000
            ),
            name="vcycle",
        )(*(pltpu.with_memory_space_constraint(x, pltpu.HBM) for x in (heat_source, conductivity, initial_iterate)))
        return pl.pallas_call(
            store,
            out_shape=(field, field),
            in_specs=[pl.BlockSpec(memory_space=pltpu.VMEM)] * 2,
            out_specs=(pl.BlockSpec(memory_space=pltpu.HBM),) * 2,
            scratch_shapes=[dma((2, steps))],
            name="store",
        )(*(pltpu.with_memory_space_constraint(x, pltpu.VMEM) for x in (one, two)))

    placed = (P("tm", "sx", "sy", None), P("sx", "sy", None), P("tm", "sx", "sy", None))
    return jax.shard_map(
        per_device,
        mesh=mesh,
        in_specs=placed,
        out_specs=(P("tm", "sx", "sy", None), P("tm", "sx", "sy", None)),
        check_vma=False,
    )
```
